512 devices in a mesh: orb: 64 (over z, y_hi, core), slab: 8 (over y_lo, x).
Axes of the slice: x: 4, y: 8 (y_hi: 4, y_lo: 2; y = y_hi * 2 + y_lo), z: 8, core: 2. Of those that a mesh axis runs over, the one named last changes fastest.
Arguments:
- orbitals: bfloat16 [64, 64, 4096], P('orb', 'slab'), may hold values from -6 to 6
- partners: int32 [64, 2], P('orb'), may hold values from 0 to 63, as said below
- offsets: int32 [64, 3], P('orb'), may hold values from 0 to 32
- kernel: float32 [128, 128, 128], P(None, 'slab'), may hold values from 0.5 to 8
Outputs:
- exchange: float32 [64, 64, 4096], P('orb', 'slab')
The draws below stay inside these ranges and needn't reach their ends.
Inputs may be any that keep to these rules, and one draw needn't show every extreme that they name: Orbital i's two partners differ from each other and equal (i + e) mod 64 with 1 <= e <= 4.
All inputs are finite; a program needn't handle non-finite values.
Results may differ from the reference program's by a relative error of at most 0.0042.
Values may be sent and summed in bfloat16 or wider, within the bound.
No kernel may reach another device: no remote copies, remote signals or barrier semaphores. Data moves between devices by JAX's collectives and lax.ppermute only.
A program may use at most 128 MiB of HBM per device.

```python
import math
import jax
import jax.numpy as jnp
from jax import lax

B = 64
G = 128
ORB_DEV = 1
REACH = 4
ORBITALS = 64


def draw_partners(key, part):
    reach_orbits = REACH * ORB_DEV
    first_key, second_key = jax.random.split(key)
    nearer = jax.random.randint(first_key, (ORBITALS,), 1, reach_orbits + 1)
    second_step = jax.random.randint(second_key, (ORBITALS,), 1, reach_orbits)
    farther = (nearer - 1 + second_step) % reach_orbits + 1
    orbit_ids = jnp.arange(ORBITALS, dtype=jnp.int32)
    return jnp.stack([(orbit_ids + nearer) % ORBITALS, (orbit_ids + farther) % ORBITALS], axis=1).astype(jnp.int32)


def touch_ends(drawn, own_key, smallest, largest):
    extent = drawn.shape
    place = [jax.random.randint(jax.random.fold_in(own_key, axis), (), 0, extent[axis]) for axis in range(len(extent))]
    drawn = drawn.at[tuple(place)].set(smallest)
    longest = extent.index(max(extent))
    place[longest] = (place[longest] + 1) % extent[longest]
    return drawn.at[tuple(place)].set(largest)


def block_levels(own_key, shape, pieces, low, top_value):
    def one(position, parts):
        heights = jax.random.uniform(jax.random.fold_in(jax.random.fold_in(own_key, 6), position), (parts,), jnp.float32, low / len(pieces), top_value / len(pieces))
        return jnp.repeat(jnp.exp(heights), shape[position] // parts).reshape((-1,) + (1,) * (len(shape) - position - 1))

    loudness = one(*pieces[0])
    for cut in pieces[1:]:
        loudness = loudness * one(*cut)
    return loudness


def bell_draw(stream_key, shape, width, bound, pieces=(), held_as=jnp.bfloat16):
    gain = block_levels(stream_key, shape, pieces, -0.22, 0.18) if pieces else 1.0
    values = jax.random.normal(stream_key, shape, jnp.float32) * width * gain
    return jnp.minimum(jnp.maximum(values, -bound), bound).astype(held_as)


def setup_inputs(seed: int = 0) -> dict:
    seeds = jax.random.split(jax.random.key(seed), 5)
    orbitals = bell_draw(seeds[0], (ORBITALS, B, B * B), 1.0, 6.0, ((0, 64), (1, 8)))
    partners = draw_partners(jax.random.fold_in(seeds[4], 71), 0)
    offsets = touch_ends(jax.random.randint(seeds[2], (ORBITALS, 3), 0, B // 2 + 1), jax.random.fold_in(seeds[2], 1), 0, (B // 2 + 1) - 1).astype(jnp.int32)
    kernel = jnp.clip(jnp.exp(math.log(8.0) - 2.7725887 * jax.random.uniform(seeds[3], (G, G, G), jnp.float32) ** block_levels(seeds[3], (G, G, G), ((1, 8),), -0.2, 0.2)), 0.5, 8.0)
    return {"orbitals": orbitals, "partners": partners, "offsets": offsets, "kernel": kernel}


def phase_table(length, offset, grid_len, signed):
    frequency = jnp.arange(grid_len, dtype=jnp.int32)
    places = offset + jnp.arange(length, dtype=jnp.int32)
    wrapped = (places[:, None] * frequency[None, :]) % grid_len
    angles = wrapped.astype(jnp.float32) * (2.0 * math.pi / grid_len)
    return jnp.cos(angles).astype(jnp.bfloat16), (signed * jnp.sin(angles)).astype(jnp.bfloat16)


def move_box(orbital_box, displacement, row_start, row_count):
    half_edge = orbital_box.shape[0] // 2
    padded = jnp.pad(orbital_box, half_edge)
    starts = (row_start + half_edge + displacement[0], half_edge + displacement[1], half_edge + displacement[2])
    return lax.dynamic_slice(padded, starts, (row_count, orbital_box.shape[1], orbital_box.shape[2]))


def mixed(form, left_side, right_side):
    return jnp.einsum(form, left_side.astype(jnp.float32), right_side.astype(jnp.float32))


def complex_pair(form, cos_table, sin_table, real_part, imag_part):
    real_out = mixed(form, cos_table, real_part) - mixed(form, sin_table, imag_part)
    imag_out = mixed(form, cos_table, imag_part) + mixed(form, sin_table, real_part)
    return real_out, imag_out


def box_tables(box_edge, half_edge, grid_len, displace_part):
    own_cos, own_sin = phase_table(box_edge, half_edge, grid_len, 1.0)
    far_cos, far_sin = phase_table(box_edge, half_edge + displace_part, grid_len, 1.0)
    return jnp.stack([own_cos, far_cos], 0), jnp.stack([own_sin, far_sin], 0)


def pair_terms(own_box, partner_box, displace, kernel):
    box_edge = own_box.shape[0]
    grid_len = 2 * box_edge
    half_edge = box_edge // 2
    partner_here = move_box(partner_box, -displace, 0, box_edge)
    own_there = move_box(own_box, displace, 0, box_edge)
    density = (own_box.astype(jnp.float32) * partner_here.astype(jnp.float32)).astype(jnp.bfloat16)
    fwd_cos, fwd_sin = phase_table(box_edge, half_edge, grid_len, -1.0)
    z_real = mixed('ayz,zk->ayk', density, fwd_cos).astype(jnp.bfloat16)
    z_imag = mixed('ayz,zk->ayk', density, fwd_sin).astype(jnp.bfloat16)
    y_real, y_imag = complex_pair('yk,ayq->akq', fwd_cos, fwd_sin, z_real, z_imag)
    y_real, y_imag = y_real.astype(jnp.bfloat16), y_imag.astype(jnp.bfloat16)
    x_real, x_imag = complex_pair('ak,aqz->kqz', fwd_cos, fwd_sin, y_real, y_imag)
    w_real = (kernel * x_real).astype(jnp.bfloat16)
    w_imag = (kernel * x_imag).astype(jnp.bfloat16)
    row_cos, row_sin = box_tables(box_edge, half_edge, grid_len, displace[0])
    v_real, v_imag = complex_pair('mak,kqz->maqz', row_cos, row_sin, w_real, w_imag)
    v_real, v_imag = v_real.astype(jnp.bfloat16), v_imag.astype(jnp.bfloat16)
    col_cos, col_sin = box_tables(box_edge, half_edge, grid_len, displace[1])
    u_real, u_imag = complex_pair('myk,makz->mayz', col_cos, col_sin, v_real, v_imag)
    u_real, u_imag = u_real.astype(jnp.bfloat16), u_imag.astype(jnp.bfloat16)
    dep_cos, dep_sin = box_tables(box_edge, half_edge, grid_len, displace[2])
    field = (mixed('mzk,mayk->mayz', dep_cos, u_real) - mixed('mzk,mayk->mayz', dep_sin, u_imag)) * (1.0 / grid_len ** 3)
    own_term = field[0] * partner_here.astype(jnp.float32)
    far_term = field[1] * own_there.astype(jnp.float32)
    return own_term, far_term


def reference(orbitals, partners, offsets, kernel):
    orbit_count = orbitals.shape[0]
    box_edge = orbitals.shape[1]
    boxes = orbitals.reshape(orbit_count, box_edge, box_edge, box_edge)
    partner_list = partners.reshape(-1)

    def visit(total_field, pair_index):
        own_index = pair_index // 2
        partner_index = partner_list[pair_index]
        displace = offsets[partner_index] - offsets[own_index]
        own_term, far_term = pair_terms(boxes[own_index], boxes[partner_index], displace, kernel)
        total_field = total_field.at[own_index].add(own_term).at[partner_index].add(far_term)
        return total_field, None

    empty_field = jnp.zeros((orbit_count, box_edge, box_edge, box_edge), jnp.float32)
    total_field, unused_out = lax.scan(visit, empty_field, jnp.arange(partner_list.shape[0], dtype=jnp.int32))
    return total_field.reshape(orbit_count, box_edge, box_edge * box_edge)
```

```python
import math

import jax
import jax.numpy as jnp
import numpy as np
from jax import lax
from jax.experimental import pallas as pl
from jax.experimental.pallas import tpu as pltpu
from jax.sharding import PartitionSpec as P

EDGE = 64
GRID = 128
HALF = 32
SLABS = 8
ROWS = EDGE // SLABS
WAVES = GRID // SLABS
PAIRS = 2
LANES = 128
FLAT = EDGE * EDGE // LANES
PAD = 24
SPAN = PAD + FLAT + PAD
F32 = jnp.float32
BF16 = jnp.bfloat16


def full_tables():
    index = np.arange(GRID)
    angle = (index[:, None] * index[None, :] % GRID) * (2.0 * np.pi / GRID)
    rounded = lambda a: a.astype(np.float32).astype(BF16)
    return rounded(np.cos(angle)), rounded(np.sin(angle))


COS, SIN = full_tables()
BOX = slice(HALF, HALF + EDGE)
SPLIT_CELLS = np.concatenate([np.arange(0, EDGE, 2), np.arange(1, EDGE, 2)]) + HALF


def forward_first():
    return np.concatenate([COS[:, SPLIT_CELLS], -SIN[:, SPLIT_CELLS]], axis=1)


def forward_depth():
    c, s = COS[BOX], SIN[BOX]
    return np.block([[c, -s], [s, c]])


def forward_rows():
    c, s = COS[:, BOX], SIN[:, BOX]
    return np.block([[c, s], [-s, c]])


def dot(a, b):
    return jnp.dot(a, b, preferred_element_type=F32)


def swapped(x):
    return pltpu.roll(x, EDGE, axis=1)


def low_half(shape):
    return lax.broadcasted_iota(jnp.int32, shape, 1) < EDGE


def moved(ref, row, d0, d1, d2):
    source = row - d0
    inside = jnp.logical_and(source >= 0, source < EDGE)
    source = jnp.clip(source, 0, EDGE - 1)
    flat = d1 * EDGE + d2
    turn = flat & (LANES - 1)
    jump = (flat - turn) // LANES
    here = pltpu.roll(ref[source, pl.ds(PAD - jump, FLAT), :], turn, axis=1)
    before = pltpu.roll(ref[source, pl.ds(PAD - jump - 1, FLAT), :], turn, axis=1)
    lane = lax.broadcasted_iota(jnp.int32, (FLAT, LANES), 1)
    depth = (lane & (EDGE - 1)) - d2
    keep = (depth >= 0) & (depth < EDGE) & inside
    return jnp.where(keep, jnp.where(lane >= turn, here, before), 0.0)


def unfold(box_of, target):
    flat_target = target.reshape(EDGE * SPAN, LANES)
    for t in range(SLABS):
        for k in range(FLAT):
            piece = box_of(t, k).astype(F32)
            flat_target[pl.ds(t * ROWS * SPAN + PAD + k, ROWS, stride=SPAN), :] = piece


def clear_edges(ref):
    zeros = jnp.zeros((EDGE, PAD, LANES), F32)
    ref[:, :PAD, :] = zeros
    ref[:, PAD + FLAT :, :] = zeros


def pair_kernel(
    scal,
    own_in,
    far_in,
    kern,
    cos_f,
    sin_f,
    first_t,
    depth_t,
    rows_t,
    send,
    here_out,
    there_out,
    own_s,
    far_s,
    zr,
    zi,
    back_s,
    row_tab,
    dep_tab,
):
    slab = scal[0]
    clear_edges(own_s)
    clear_edges(far_s)
    unfold(lambda t, k: own_in[t, :, k * LANES : (k + 1) * LANES], own_s)
    first = first_t[pl.ds(pl.multiple_of(slab * WAVES, WAVES), WAVES), :]
    first = jnp.concatenate([first[:, :EDGE], first[:, EDGE:]], axis=0)
    depth_m = depth_t[...]
    rows_m = rows_t[...]
    low_d = low_half((FLAT, LANES))
    low_w = low_half((WAVES, LANES))
    kern_flat = kern.reshape(GRID * WAVES, LANES)
    back_flat = back_s.reshape(2 * EDGE * WAVES, LANES)

    def tables_for(slot, d0, d2):
        c = cos_f[pl.ds(HALF + d0, EDGE), :].astype(BF16)
        s = sin_f[pl.ds(HALF + d0, EDGE), :].astype(BF16)
        base = slot * 2 * EDGE
        row_tab[base : base + EDGE, :GRID] = c
        row_tab[base : base + EDGE, GRID:] = -s
        row_tab[base + EDGE : base + 2 * EDGE, :GRID] = s
        row_tab[base + EDGE : base + 2 * EDGE, GRID:] = c
        turn = (GRID - HALF - d2) & (LANES - 1)
        low = low_half((GRID, LANES))
        c = pltpu.roll(cos_f[...], turn, axis=1)
        s = pltpu.roll(sin_f[...], turn, axis=1)
        dep_tab[slot, :GRID, :] = jnp.where(low, c, swapped(s)).astype(BF16)
        dep_tab[slot, GRID:, :] = jnp.where(low, -s, swapped(c)).astype(BF16)

    tables_for(0, 0, 0)
    for n in range(PAIRS):
        d0, d1, d2 = scal[1 + 3 * n], scal[2 + 3 * n], scal[3 + 3 * n]
        unfold(lambda t, k: far_in[t, n, :, k * LANES : (k + 1) * LANES], far_s)
        tables_for(1, d0, d2)

        def forward(step, carry):
            waves = []
            for half in range(2):
                a = step * 4 + half * 2
                dens_a = own_s[a, PAD : PAD + FLAT, :] * moved(far_s, a, d0, d1, d2)
                dens_b = own_s[a + 1, PAD : PAD + FLAT, :] * moved(far_s, a + 1, d0, d1, d2)
                even = jnp.where(low_d, dens_a, swapped(dens_b)).astype(BF16)
                odd = jnp.where(low_d, swapped(dens_a), dens_b).astype(BF16)
                y = dot(first, jnp.concatenate([even, odd], axis=0))
                re, im = y[:WAVES], y[WAVES:]
                waves.append(jnp.where(low_w, re, swapped(im)))
                waves.append(jnp.where(low_w, swapped(re), im))
            z = dot(jnp.concatenate(waves, axis=0).astype(BF16), depth_m)
            for q in range(4):
                block = z[q * WAVES : (q + 1) * WAVES]
                zr[pl.ds(step * 4 + q, WAVES, stride=EDGE), :] = block[:, :LANES]
                zi[pl.ds(step * 4 + q, WAVES, stride=EDGE), :] = block[:, LANES:]
            return carry

        lax.fori_loop(0, EDGE // 4, forward, 0)

        def middle(step, carry):
            def plane(w):
                at = pl.ds(pl.multiple_of(w * EDGE, EDGE), EDGE)
                return jnp.concatenate([zr[at, :], zi[at, :]], axis=0).astype(BF16)

            w0, w1 = step * 2, step * 2 + 1
            x = dot(rows_m, jnp.concatenate([plane(w0), plane(w1)], axis=1))
            scale = jnp.concatenate(
                [kern_flat[pl.ds(w0, GRID, stride=WAVES), :], kern_flat[pl.ds(w1, GRID, stride=WAVES), :]], axis=1
            )
            w = jnp.concatenate([x[:GRID] * scale, x[GRID:] * scale], axis=0).astype(BF16)
            v = dot(row_tab[...], w).astype(BF16)
            for m in range(2):
                re = v[2 * m * EDGE : (2 * m + 1) * EDGE]
                im = v[(2 * m + 1) * EDGE : (2 * m + 2) * EDGE]
                left = jnp.concatenate(
                    [
                        jnp.concatenate([re[:, :LANES], im[:, :LANES]], axis=1),
                        jnp.concatenate([re[:, LANES:], im[:, LANES:]], axis=1),
                    ],
                    axis=0,
                )
                r = dot(left, dep_tab[m])
                back_flat[pl.ds(m * EDGE * WAVES + w0, EDGE, stride=WAVES), :] = r[:EDGE]
                back_flat[pl.ds(m * EDGE * WAVES + w1, EDGE, stride=WAVES), :] = r[EDGE:]
            return carry

        lax.fori_loop(0, WAVES // 2, middle, 0)
        for m in range(2):
            for t in range(SLABS):
                send[t, n, m] = back_s[m * EDGE + t * ROWS : m * EDGE + (t + 1) * ROWS].astype(BF16)
        for r in range(ROWS):
            here_out[n, r] = moved(far_s, slab * ROWS + r, d0, d1, d2).astype(BF16)
            there_out[n, r] = moved(own_s, slab * ROWS + r, -d0, -d1, -d2).astype(BF16)


def pair_call(scal, own_box, far_box, kernel, interpret=False):
    vmem = pl.BlockSpec(memory_space=pltpu.VMEM)
    return pl.pallas_call(
        pair_kernel,
        out_shape=(
            jax.ShapeDtypeStruct((SLABS, PAIRS, 2, ROWS, WAVES, LANES), BF16),
            jax.ShapeDtypeStruct((PAIRS, ROWS, FLAT, LANES), BF16),
            jax.ShapeDtypeStruct((PAIRS, ROWS, FLAT, LANES), BF16),
        ),
        in_specs=[pl.BlockSpec(memory_space=pltpu.SMEM)] + [vmem] * 8,
        out_specs=(vmem, vmem, vmem),
        scratch_shapes=[
            pltpu.VMEM((EDGE, SPAN, LANES), F32),
            pltpu.VMEM((EDGE, SPAN, LANES), F32),
            pltpu.VMEM((WAVES * EDGE, LANES), F32),
            pltpu.VMEM((WAVES * EDGE, LANES), F32),
            pltpu.VMEM((2 * EDGE, WAVES, LANES), F32),
            pltpu.VMEM((4 * EDGE, 2 * GRID), BF16),
            pltpu.VMEM((2, 2 * GRID, LANES), BF16),
        ],
        interpret=interpret,
        name="pair_waves",
    )(
        scal,
        own_box,
        far_box,
        kernel,
        jnp.asarray(COS.astype(np.float32)),
        jnp.asarray(SIN.astype(np.float32)),
        jnp.asarray(forward_first()),
        jnp.asarray(forward_depth()),
        jnp.asarray(forward_rows()),
    )


def term_kernel(scal, got, here, there, cos_f, sin_f, own_out, odd_out, even_out, far_s):
    low = low_half((FLAT, LANES))
    scale = 1.0 / GRID**3

    def table(shift):
        parts = [ref[pl.ds(HALF + shift + par, FLAT, stride=2), :] for ref in (cos_f, sin_f) for par in range(2)]
        return jnp.concatenate(parts, axis=0).astype(BF16)

    def fields(n, m, tab, row):
        def column(r):
            return jnp.concatenate([got[t, n, m, r] for t in range(SLABS)], axis=0)

        g = dot(tab, jnp.concatenate([column(row), column(row + 1)], axis=1))
        out = []
        for side in range(2):
            part = g[:, side * LANES : (side + 1) * LANES]
            c0, c1, s0, s1 = (part[q * FLAT : (q + 1) * FLAT] for q in range(4))
            out.append(jnp.where(low, c0 - swapped(s0), swapped(c1) - s1) * scale)
        return out

    own_tab = table(0)
    far_tabs = [table(scal[1 + n]) for n in range(PAIRS)]
    for row in range(0, ROWS, 2):
        total = [jnp.zeros((FLAT, LANES), F32)] * 2
        for n in range(PAIRS):
            pots = fields(n, 0, own_tab, row)
            total = [total[q] + pots[q] * here[n, row + q].astype(F32) for q in range(2)]
            pots = fields(n, 1, far_tabs[n], row)
            for q in range(2):
                far_s[n, row + q] = pots[q] * there[n, row + q].astype(F32)
        for q in range(2):
            own_out[row + q] = total[q]
    hops = [scal[3 + n] for n in range(PAIRS)]
    for e in range(1, 5):
        target = odd_out if e % 2 else even_out
        for row in range(ROWS):
            value = sum(jnp.where(hops[n] == e, far_s[n, row], 0.0) for n in range(PAIRS))
            target[(e - 1) // 2, row] = value.astype(BF16)


def term_call(scal, got, here, there, interpret=False):
    vmem = pl.BlockSpec(memory_space=pltpu.VMEM)
    return pl.pallas_call(
        term_kernel,
        out_shape=(
            jax.ShapeDtypeStruct((ROWS, FLAT, LANES), F32),
            jax.ShapeDtypeStruct((2, ROWS, FLAT, LANES), BF16),
            jax.ShapeDtypeStruct((2, ROWS, FLAT, LANES), BF16),
        ),
        in_specs=[pl.BlockSpec(memory_space=pltpu.SMEM)] + [vmem] * 5,
        out_specs=(vmem, vmem, vmem),
        scratch_shapes=[pltpu.VMEM((PAIRS, ROWS, FLAT, LANES), F32)],
        interpret=interpret,
        name="pair_terms",
    )(scal, got, here, there, jnp.asarray(COS.astype(np.float32)), jnp.asarray(SIN.astype(np.float32)))


def passed_along(block, distance):
    count = lax.axis_size("orb")
    return lax.ppermute(block, "orb", [((i - distance) % count, i) for i in range(count)])


def other_core(block):
    count = lax.axis_size("orb")
    return lax.ppermute(block, "orb", [(i ^ 1, i) for i in range(count)])


def to_everyone(shard):
    copies = jnp.broadcast_to(shard, (lax.axis_size("slab"), *shard.shape))
    return lax.all_to_all(copies, "slab", split_axis=0, concat_axis=0, tiled=True)


def per_device(orbitals, partners, offsets, kernel):
    orbit = lax.axis_index("orb")
    slab = lax.axis_index("slab")
    even_core = orbit % 2 == 0
    cells = EDGE * EDGE
    own = orbitals[0]
    corner = jnp.pad(offsets.astype(BF16), ((0, 0), (0, LANES - 3)))
    loaded = jnp.concatenate([own, jnp.broadcast_to(corner, (ROWS, LANES))], axis=1)
    four = passed_along(loaded, -4)
    two = passed_along(loaded, -2)
    own_box = to_everyone(own)
    given = jnp.stack([jnp.where(even_core, two, loaded), jnp.where(even_core, four, two)])
    odd = other_core(given)
    hops = (partners[0] - orbit) % lax.axis_size("orb")

    def chosen(hop):
        low = jnp.where(hop == 1, odd[0], two)
        high = jnp.where(hop == 3, odd[1], four)
        return jnp.where(hop <= 2, low, high)

    picked = jnp.stack([chosen(hops[n]) for n in range(PAIRS)])
    shifts = picked[:, 0, cells : cells + 3].astype(jnp.int32) - offsets
    far_box = to_everyone(picked[:, :, :cells])
    scal = jnp.concatenate([slab[None].astype(jnp.int32), shifts.reshape(-1)])
    send, here, there = pair_call(scal, own_box, far_box, kernel)
    got = lax.all_to_all(send, "slab", split_axis=0, concat_axis=0, tiled=True)
    scal = jnp.concatenate([jnp.zeros((1,), jnp.int32), shifts[:, 1], hops])
    mine, odd_out, even_out = term_call(scal, got, here, there)
    crossed = other_core(odd_out).astype(F32)
    by_two = even_out[0].astype(F32) + jnp.where(even_core, crossed[0], crossed[1])
    by_four = even_out[1].astype(F32) + jnp.where(even_core, crossed[1], 0.0)
    four_back = passed_along(by_four.astype(BF16), 4).astype(F32)
    two_back = passed_along(by_two.astype(BF16), 2).astype(F32)
    total = mine + jnp.where(even_core, 0.0, crossed[0]) + two_back + four_back
    return total.reshape(1, ROWS, cells)


def solution(mesh):
    return jax.shard_map(
        per_device,
        mesh=mesh,
        in_specs=(P("orb", "slab", None), P("orb", None), P("orb", None), P(None, "slab", None)),
        out_specs=P("orb", "slab", None),
        check_vma=False,
    )
```

```python
import math

import jax
import jax.numpy as jnp
import numpy as np
from jax import lax
from jax.experimental import pallas as pl
from jax.experimental.pallas import tpu as pltpu
from jax.sharding import PartitionSpec as P

EDGE = 64
GRID = 128
HALF = 32
SLABS = 8
ROWS = EDGE // SLABS
WAVES = GRID // SLABS
PAIRS = 2
LANES = 128
FLAT = EDGE * EDGE // LANES
PAD = 24
SPAN = PAD + FLAT + PAD + 1
SLOTS = 8
ZSPAN = EDGE + 1
BSPAN = 2 * SLOTS + 1
ROOM = HALF + EDGE + HALF
F32 = jnp.float32
BF16 = jnp.bfloat16


def full_tables():
    index = np.arange(GRID)
    angle = (index[:, None] * index[None, :] % GRID) * (2.0 * np.pi / GRID)
    rounded = lambda a: a.astype(np.float32).astype(BF16).astype(np.float32)
    return rounded(np.cos(angle)), rounded(np.sin(angle))


COS, SIN = full_tables()
SIGN = COS[:, EDGE]
BOX = slice(HALF, HALF + EDGE)
SPLIT_CELLS = np.concatenate([np.arange(0, EDGE, 2), np.arange(1, EDGE, 2)]) + HALF
OWN_WAVES = np.array([[16 * (q // 2) + 2 * s + q % 2 for q in range(SLOTS)] for s in range(SLABS)])


def forward_first():
    re = COS[:, SPLIT_CELLS]
    im = -SIN[:, SPLIT_CELLS]
    im[0] = SIGN[SPLIT_CELLS]
    return np.concatenate([re[OWN_WAVES], im[OWN_WAVES]], axis=1).astype(BF16)


def backward_last():
    c, s = COS.copy(), SIN.copy()
    s[:, 0] = -SIGN
    out = []
    for m in range(2):
        for table in (c, s):
            wide = np.zeros((GRID, SLABS, 2, SLOTS), np.float32)
            wide[:, :, m] = table[:, OWN_WAVES]
            out.append(wide.reshape(GRID, GRID))
    return np.concatenate(out)


def forward_depth():
    c, s = COS[BOX], SIN[BOX]
    return np.block([[c, -s], [s, c]]).astype(BF16)


def forward_rows():
    c, s = COS[:, BOX], SIN[:, BOX]
    return np.block([[c, s], [-s, c]]).astype(BF16)


def reversal():
    flip = np.zeros((GRID, GRID), np.float32)
    flip[np.arange(GRID), -np.arange(GRID) % GRID] = 1.0
    return flip.astype(BF16)


def dot(a, b):
    return jnp.dot(a, b, preferred_element_type=F32)


def swapped(x):
    return pltpu.roll(x, EDGE, axis=1)


def lanes_of(shape):
    return lax.broadcasted_iota(jnp.int32, shape, 1)


def low_half(shape):
    return lanes_of(shape) < EDGE


def in_depth(lane, d2):
    depth = (lane & (EDGE - 1)) - d2
    return (depth >= 0) & (depth < EDGE)


def offer_kernel(slab_ref, own, kern, send):
    slab = slab_ref[0]
    kern_flat = kern.reshape(GRID * WAVES, LANES)
    mine = [jnp.concatenate([own[:, (k + h) * LANES : (k + h + 1) * LANES] for h in range(2)], axis=0) for k in range(0, FLAT, 2)]
    mine = jnp.concatenate(mine, axis=0)
    for t in range(SLABS):
        for j in range(2):
            high = (WAVES - 2 * t) % WAVES if j == 0 else WAVES - 1 - 2 * t
            at = jnp.where(slab < SLABS // 2, 2 * t + j, high)
            send[t, j * GRID : (j + 1) * GRID, :] = kern_flat[pl.ds(at, GRID, stride=WAVES), :].astype(BF16)
        send[t, 2 * GRID :, :] = mine


def moved(ref, row, d0, d1, d2):
    source = row - d0
    inside = jnp.logical_and(source >= 0, source < EDGE)
    base = jnp.clip(source, 0, EDGE - 1) * SPAN + PAD
    flat = d1 * EDGE + d2
    turn = flat & (LANES - 1)
    jump = (flat - turn) // LANES
    here = pltpu.roll(ref[pl.ds(base - jump, FLAT), :], turn, axis=1)
    before = pltpu.roll(ref[pl.ds(base - jump - 1, FLAT), :], turn, axis=1)
    lane = lanes_of((FLAT, LANES))
    return jnp.where(in_depth(lane, d2) & inside, jnp.where(lane >= turn, here, before), 0.0)


def prepare_kernel(scal, got, flip_t, cos_f, sin_f, own_out, scale_out, there_out, row_out, dep_out, own_s):
    slab = scal[0]
    zeros = jnp.zeros((PAD + 1, LANES), F32)
    for c in range(EDGE):
        own_s[c * SPAN : c * SPAN + PAD, :] = zeros[:PAD]
        own_s[c * SPAN + PAD + FLAT : (c + 1) * SPAN, :] = zeros
    for t in range(SLABS):
        for k in range(FLAT):
            at = 2 * GRID + k * ROWS
            own_s[pl.ds(t * ROWS * SPAN + PAD + k, ROWS, stride=SPAN), :] = got[t, at : at + ROWS, :].astype(F32)
    for c in range(EDGE):
        own_out[c * FLAT : (c + 1) * FLAT, :] = own_s[c * SPAN + PAD : c * SPAN + PAD + FLAT, :].astype(BF16)
    flip = flip_t[...]

    def reversed_plane(plane):
        return dot(dot(flip, plane).astype(BF16), flip)

    first = slab == 0
    for t in range(SLABS // 2):
        for j in range(2):
            here = got[t, j * GRID : (j + 1) * GRID, :]
            if j:
                there = got[SLABS - 1 - t, GRID : 2 * GRID, :]
            else:
                there = got[jnp.where(first, (SLABS - t) % SLABS, SLABS - 1 - t), :GRID, :]
            both = here.astype(F32) + reversed_plane(there)
            if t + j:
                scale_out[2 * t + j] = both
            else:
                top = got[SLABS // 2, :GRID, :]
                top = top.astype(F32) + reversed_plane(top)
                scale_out[0] = jnp.where(first, 0.25 * (both + top), both)
                scale_out[SLOTS] = jnp.where(first, 0.25 * (both - top), 0.0)
    for n in range(PAIRS):
        d0, d1, d2 = scal[1 + 3 * n], scal[2 + 3 * n], scal[3 + 3 * n]
        for r in range(ROWS):
            there_out[n, r] = moved(own_s, slab * ROWS + r, -d0, -d1, -d2).astype(BF16)
    for n in range(PAIRS):
        for m in range(2):
            d0 = scal[1 + 3 * n] * m
            d2 = scal[3 + 3 * n] * m
            c = cos_f[pl.ds(HALF + d0, EDGE), :].astype(BF16)
            s = sin_f[pl.ds(HALF + d0, EDGE), :].astype(BF16)
            base = m * 2 * EDGE
            row_out[n, base : base + EDGE, :GRID] = c
            row_out[n, base : base + EDGE, GRID:] = -s
            row_out[n, base + EDGE : base + 2 * EDGE, :GRID] = s
            row_out[n, base + EDGE : base + 2 * EDGE, GRID:] = c
            turn = (GRID - HALF - d2) & (LANES - 1)
            low = low_half((GRID, LANES))
            c = pltpu.roll(cos_f[...], turn, axis=1)
            s = pltpu.roll(sin_f[...], turn, axis=1)
            dep_out[n, m, :GRID, :] = jnp.where(low, c, swapped(s)).astype(BF16)
            dep_out[n, m, GRID:, :] = jnp.where(low, -s, swapped(c)).astype(BF16)


def pair_kernel(scal, own_s, far_in, scale_t, row_t, dep_t, first_t, depth_t, rows_t, flip_t, send, here_out, far_s, zr, zi, back_s):
    slab = scal[0]
    first = first_t[slab]
    depth_m = depth_t[...]
    rows_m = rows_t[...]
    flip = flip_t[...]
    low_d = low_half((FLAT, LANES))
    low_w = low_half((SLOTS, LANES))
    lane_d = lanes_of((FLAT, LANES))
    lane_r = lanes_of((ROWS, LANES))
    blank = jnp.zeros((FLAT + 8, LANES), F32)
    for n in range(PAIRS):
        d0, d1, d2 = scal[1 + 3 * n], scal[2 + 3 * n], scal[3 + 3 * n]
        flat = d1 * EDGE + d2
        turn = flat & (LANES - 1)
        jump = (flat - turn) // LANES

        def clear(c, carry):
            far_s[pl.ds((HALF + c) * SPAN + PAD - 8, FLAT + 8), :] = blank
            return carry

        lax.fori_loop(0, EDGE, clear, 0, unroll=8)
        keep = in_depth(lane_r, d2)
        for t in range(SLABS):
            start = (HALF + t * ROWS + d0) * SPAN + PAD + jump
            for k in range(FLAT):
                piece = far_in[t, n, :, k * LANES : (k + 1) * LANES].astype(F32)
                piece = jnp.where(keep, pltpu.roll(piece, turn, axis=1), 0.0)
                far_s[pl.ds(start + k, ROWS, stride=SPAN), :] = piece
        after = lane_d >= turn

        def aligned(c):
            base = (HALF + c) * SPAN + PAD
            return jnp.where(after, far_s[pl.ds(base, FLAT), :], far_s[pl.ds(base - 1, FLAT), :])

        def own_row(c):
            return own_s[pl.ds(pl.multiple_of(c * FLAT, FLAT), FLAT), :].astype(F32)

        def forward(step, carry):
            waves = []
            for quad in range(2):
                sides = []
                for half in range(2):
                    a = step * 8 + quad * 4 + half * 2
                    dens_a = own_row(a) * aligned(a)
                    dens_b = own_row(a + 1) * aligned(a + 1)
                    even = jnp.where(low_d, dens_a, swapped(dens_b)).astype(BF16)
                    odd = jnp.where(low_d, swapped(dens_a), dens_b).astype(BF16)
                    sides.append(jnp.concatenate([even, odd], axis=0))
                y = dot(first, jnp.concatenate(sides, axis=1))
                for half in range(2):
                    re = y[:SLOTS, half * LANES : (half + 1) * LANES]
                    im = y[SLOTS:, half * LANES : (half + 1) * LANES]
                    waves.append(jnp.where(low_w, re, swapped(im)))
                    waves.append(jnp.where(low_w, swapped(re), im))
            z = dot(jnp.concatenate(waves, axis=0).astype(BF16), depth_m)
            for q in range(8):
                block = z[q * SLOTS : (q + 1) * SLOTS]
                zr[pl.ds(step * 8 + q, SLOTS, stride=ZSPAN), :] = block[:, :LANES]
                zi[pl.ds(step * 8 + q, SLOTS, stride=ZSPAN), :] = block[:, LANES:]
            return carry

        lax.fori_loop(0, EDGE // 8, forward, 0, unroll=2)
        tab = row_t[n]

        def plane(w):
            at = slice(w * ZSPAN, w * ZSPAN + EDGE)
            return jnp.concatenate([zr[at, :], zi[at, :]], axis=0).astype(BF16)

        for w0 in range(0, SLOTS, 2):
            x = dot(rows_m, jnp.concatenate([plane(w0), plane(w0 + 1)], axis=1))
            weight = jnp.concatenate([scale_t[w0], scale_t[w0 + 1]], axis=1)
            re, im = x[:GRID] * weight, x[GRID:] * weight
            if w0 == 0:
                edge = x[:, :LANES].astype(BF16)
                back_re = dot(dot(flip, edge[:GRID]).astype(BF16), flip)
                back_im = dot(dot(flip, edge[GRID:]).astype(BF16), flip)
                extra = scale_t[SLOTS]
                re = jnp.concatenate([re[:, :LANES] + extra * back_re, re[:, LANES:]], axis=1)
                im = jnp.concatenate([im[:, :LANES] - extra * back_im, im[:, LANES:]], axis=1)
            w = jnp.concatenate([re, im], axis=0).astype(BF16)
            v = dot(tab, w).astype(BF16)
            for m in range(2):
                re = v[2 * m * EDGE : (2 * m + 1) * EDGE]
                im = v[(2 * m + 1) * EDGE : (2 * m + 2) * EDGE]
                left = jnp.concatenate(
                    [
                        jnp.concatenate([re[:, :LANES], im[:, :LANES]], axis=1),
                        jnp.concatenate([re[:, LANES:], im[:, LANES:]], axis=1),
                    ],
                    axis=0,
                )
                r = dot(left, dep_t[n, m])
                for h in range(2):
                    back_s[pl.ds(m * SLOTS + w0 + h, EDGE, stride=BSPAN), :] = r[h * EDGE : (h + 1) * EDGE]
        for t in range(SLABS):
            for r in range(ROWS):
                at = (t * ROWS + r) * BSPAN
                send[t, n, r] = back_s[at : at + 2 * SLOTS, :].astype(BF16)
        for r in range(ROWS):
            here_out[n, r] = aligned(slab * ROWS + r).astype(BF16)


def term_kernel(scal, got, here, there, last_t, own_out, odd_out, even_out, far_s):
    low = low_half((FLAT, LANES))
    scale = 1.0 / GRID**3

    def table(m, shift):
        parts = [last_t[pl.ds((2 * m + f) * GRID + HALF + shift + par, FLAT, stride=2), :] for f in range(2) for par in range(2)]
        return jnp.concatenate(parts, axis=0)

    own_tab = table(0, 0)
    for n in range(PAIRS):
        tab = jnp.concatenate([own_tab, table(1, scal[1 + n])], axis=0).astype(BF16)
        for row in range(0, ROWS, 2):
            data = [jnp.concatenate([got[t, n, row + q] for t in range(SLABS)], axis=0) for q in range(2)]
            g = dot(tab, jnp.concatenate(data, axis=1))
            for q in range(2):
                pots = []
                for m in range(2):
                    part = g[m * GRID : (m + 1) * GRID, q * LANES : (q + 1) * LANES]
                    c0, c1, s0, s1 = (part[f * FLAT : (f + 1) * FLAT] for f in range(4))
                    pots.append(jnp.where(low, c0 - swapped(s0), swapped(c1) - s1) * scale)
                term = pots[0] * here[n, row + q].astype(F32)
                own_out[row + q] = term if n == 0 else own_out[row + q] + term
                far_s[n, row + q] = pots[1] * there[n, row + q].astype(F32)
    hops = [scal[3 + n] for n in range(PAIRS)]
    for e in range(1, 5):
        target = odd_out if e % 2 else even_out
        for row in range(ROWS):
            value = sum(jnp.where(hops[n] == e, far_s[n, row], 0.0) for n in range(PAIRS))
            target[(e - 1) // 2, row] = value.astype(BF16)


VMEM = pl.BlockSpec(memory_space=pltpu.VMEM)
SMEM = pl.BlockSpec(memory_space=pltpu.SMEM)


def kept(shape, dtype):
    return pltpu.VMEM(shape, dtype)


def near(x):
    return pltpu.with_memory_space_constraint(x, pltpu.VMEM)


def offer_call(slab, own, kernel, interpret=False):
    return pl.pallas_call(
        offer_kernel,
        out_shape=jax.ShapeDtypeStruct((SLABS, 4 * GRID, LANES), BF16),
        in_specs=[SMEM, VMEM, VMEM],
        out_specs=VMEM,
        interpret=interpret,
        name="offer",
        compiler_params=pltpu.CompilerParams(vmem_limit_bytes=10 << 20),
    )(slab, own, kernel)


def prepare_call(scal, got, interpret=False):
    return pl.pallas_call(
        prepare_kernel,
        out_shape=(
            kept((EDGE * FLAT, LANES), BF16),
            kept((SLOTS + 1, GRID, LANES), F32),
            jax.ShapeDtypeStruct((PAIRS, ROWS, FLAT, LANES), BF16),
            jax.ShapeDtypeStruct((PAIRS, 4 * EDGE, 2 * GRID), BF16),
            jax.ShapeDtypeStruct((PAIRS, 2, 2 * GRID, LANES), BF16),
        ),
        in_specs=[SMEM] + [VMEM] * 4,
        out_specs=(VMEM,) * 5,
        scratch_shapes=[pltpu.VMEM((EDGE * SPAN, LANES), F32)],
        interpret=interpret,
        name="prepare",
        compiler_params=pltpu.CompilerParams(vmem_limit_bytes=12 << 20),
    )(scal, near(got), jnp.asarray(reversal()), jnp.asarray(COS), jnp.asarray(SIN))


def pair_call(scal, own_s, far_box, scale, rows, depths, interpret=False):
    return pl.pallas_call(
        pair_kernel,
        out_shape=(
            jax.ShapeDtypeStruct((SLABS, PAIRS, ROWS, 2 * SLOTS, LANES), BF16),
            kept((PAIRS, ROWS, FLAT, LANES), BF16),
        ),
        in_specs=[SMEM] + [VMEM] * 9,
        out_specs=(VMEM, VMEM),
        scratch_shapes=[
            pltpu.VMEM((ROOM * SPAN, LANES), F32),
            pltpu.VMEM((SLOTS * ZSPAN, LANES), F32),
            pltpu.VMEM((SLOTS * ZSPAN, LANES), F32),
            pltpu.VMEM((EDGE * BSPAN, LANES), F32),
        ],
        interpret=interpret,
        name="pair_waves",
        compiler_params=pltpu.CompilerParams(vmem_limit_bytes=20 << 20),
    )(
        scal,
        near(own_s),
        near(far_box),
        near(scale),
        rows,
        depths,
        jnp.asarray(forward_first()),
        jnp.asarray(forward_depth()),
        jnp.asarray(forward_rows()),
        jnp.asarray(reversal()),
    )


def term_call(scal, got, here, there, interpret=False):
    return pl.pallas_call(
        term_kernel,
        out_shape=(
            kept((ROWS, FLAT, LANES), F32),
            kept((2, ROWS, FLAT, LANES), BF16),
            kept((2, ROWS, FLAT, LANES), BF16),
        ),
        in_specs=[SMEM] + [VMEM] * 4,
        out_specs=(VMEM,) * 3,
        scratch_shapes=[pltpu.VMEM((PAIRS, ROWS, FLAT, LANES), F32)],
        interpret=interpret,
        name="pair_terms",
        compiler_params=pltpu.CompilerParams(vmem_limit_bytes=12 << 20),
    )(scal, near(got), near(here), there, jnp.asarray(backward_last()))


def passed_along(block, distance):
    count = lax.axis_size("orb")
    return lax.ppermute(block, "orb", [((i - distance) % count, i) for i in range(count)])


def other_core(block):
    count = lax.axis_size("orb")
    return lax.ppermute(block, "orb", [(i ^ 1, i) for i in range(count)])


def to_everyone(shard):
    copies = jnp.broadcast_to(shard, (lax.axis_size("slab"), *shard.shape))
    return lax.all_to_all(copies, "slab", split_axis=0, concat_axis=0, tiled=True)


def shared(block):
    return lax.all_to_all(block, "slab", split_axis=0, concat_axis=0, tiled=True)


def per_device(orbitals, partners, offsets, kernel):
    orbit = lax.axis_index("orb")
    slab = lax.axis_index("slab").astype(jnp.int32)
    even_core = orbit % 2 == 0
    cells = EDGE * EDGE
    own = orbitals[0]
    corner = jnp.pad(offsets.astype(BF16), ((0, 0), (0, LANES - 3)))
    loaded = jnp.concatenate([own, jnp.broadcast_to(corner, (ROWS, LANES))], axis=1)
    four = passed_along(loaded, -4)
    two = passed_along(loaded, -2)
    offered = shared(offer_call(slab[None], own, kernel))
    given = jnp.stack([jnp.where(even_core, two, loaded), jnp.where(even_core, four, two)])
    odd = other_core(given)
    hops = (partners[0] - orbit) % lax.axis_size("orb")

    def chosen(hop):
        low = jnp.where(hop == 1, odd[0], two)
        high = jnp.where(hop == 3, odd[1], four)
        return jnp.where(hop <= 2, low, high)

    picked = jnp.stack([chosen(hops[n]) for n in range(PAIRS)])
    shifts = picked[:, 0, cells : cells + 3].astype(jnp.int32) - offsets
    far_box = to_everyone(picked[:, :, :cells])
    scal = jnp.concatenate([slab[None], shifts.reshape(-1)])
    own_s, scale, there, rows, depths = prepare_call(scal, offered)
    send, here = pair_call(scal, own_s, far_box, scale, rows, depths)
    got = shared(send)
    scal = jnp.concatenate([jnp.zeros((1,), jnp.int32), shifts[:, 1], hops])
    mine, odd_out, even_out = term_call(scal, got, here, there)
    crossed = other_core(odd_out).astype(F32)
    by_two = even_out[0].astype(F32) + jnp.where(even_core, crossed[0], crossed[1])
    by_four = even_out[1].astype(F32) + jnp.where(even_core, crossed[1], 0.0)
    four_back = passed_along(by_four.astype(BF16), 4).astype(F32)
    two_back = passed_along(by_two.astype(BF16), 2).astype(F32)
    total = mine + jnp.where(even_core, 0.0, crossed[0]) + two_back + four_back
    return total.reshape(1, ROWS, cells)


def solution(mesh):
    return jax.shard_map(
        per_device,
        mesh=mesh,
        in_specs=(P("orb", "slab", None), P("orb", None), P("orb", None), P(None, "slab", None)),
        out_specs=P("orb", "slab", None),
        check_vma=False,
    )
```

```python
import jax
import jax.numpy as jnp
import numpy as np
from jax import lax
from jax.experimental import pallas as pl
from jax.experimental.pallas import tpu as pltpu
from jax.sharding import PartitionSpec as P


EDGE = 64
GRID = 128
HALF = 32
SLABS = 8
ROWS = EDGE // SLABS
WAVES = GRID // SLABS
PAIRS = 2
LANES = 128
FLAT = EDGE * EDGE // LANES
PAD = 24
SPAN = PAD + FLAT + PAD + 1
SLOTS = 8
ZSPAN = EDGE + 1
BSPAN = 2 * SLOTS + 1
ROOM = HALF + EDGE + HALF
F32 = jnp.float32
BF16 = jnp.bfloat16


def full_tables():
    index = np.arange(GRID)
    angle = (index[:, None] * index[None, :] % GRID) * (2.0 * np.pi / GRID)
    rounded = lambda a: a.astype(np.float32).astype(BF16).astype(np.float32)
    return rounded(np.cos(angle)), rounded(np.sin(angle))


COS, SIN = full_tables()
SIGN = COS[:, EDGE]
BOX = slice(HALF, HALF + EDGE)
SPLIT_CELLS = np.concatenate([np.arange(0, EDGE, 2), np.arange(1, EDGE, 2)]) + HALF
OWN_WAVES = np.array([[WAVES * s + (s >= SLABS // 2) + q for q in range(SLOTS)] for s in range(SLABS)])


def forward_first():
    re = COS[:, SPLIT_CELLS]
    im = -SIN[:, SPLIT_CELLS]
    im[0] = SIGN[SPLIT_CELLS]
    return np.concatenate([re[OWN_WAVES], im[OWN_WAVES]], axis=1).astype(BF16)


def backward_last():
    c, s = COS.copy(), SIN.copy()
    s[:, 0] = -SIGN
    out = []
    for m in range(2):
        for table in (c, s):
            wide = np.zeros((GRID, SLABS, 2, SLOTS), np.float32)
            wide[:, :, m] = table[:, OWN_WAVES]
            out.append(wide.reshape(GRID, GRID))
    return np.concatenate(out)


def forward_depth():
    c, s = COS[BOX], SIN[BOX]
    return np.block([[c, -s], [s, c]]).astype(BF16)


def forward_rows():
    c, s = COS[:, BOX], SIN[:, BOX]
    return np.block([[c, s], [-s, c]]).astype(BF16)


def reversal():
    flip = np.zeros((GRID, GRID), np.float32)
    flip[np.arange(GRID), -np.arange(GRID) % GRID] = 1.0
    return flip.astype(BF16)


def dot(a, b):
    return jnp.dot(a, b, preferred_element_type=F32)


def swapped(x):
    return pltpu.roll(x, EDGE, axis=1)


def lanes_of(shape):
    return lax.broadcasted_iota(jnp.int32, shape, 1)


def low_half(shape):
    return lanes_of(shape) < EDGE


def in_depth(lane, d2):
    depth = (lane & (EDGE - 1)) - d2
    return (depth >= 0) & (depth < EDGE)


def load_kernel(corner, own, loaded, copies):
    cells = own[...]
    loaded[:, : EDGE * EDGE] = cells
    lane = lanes_of((ROWS, LANES))
    mark = jnp.zeros((ROWS, LANES), F32)
    for k in range(3):
        mark = jnp.where(lane == k, corner[0, k].astype(F32), mark)
    loaded[:, EDGE * EDGE :] = mark.astype(BF16)
    for t in range(SLABS):
        copies[t] = cells


def mirror_kernel(kern, upper, lowest):
    kern_flat = kern.reshape(GRID * WAVES, LANES)
    for q in range(SLOTS):
        upper[q] = kern_flat[pl.ds(SLOTS + q, GRID, stride=WAVES), :].astype(BF16)
    lowest[...] = kern_flat[pl.ds(0, GRID, stride=WAVES), :].astype(BF16)


def pick_kernel(hops, two, four, odd, copies, marks, block, sems):
    for n in range(PAIRS):
        hop = hops[n]
        for k in range(0, EDGE * EDGE + LANES, LANES):
            at = slice(k, k + LANES)
            low = jnp.where(hop == 1, odd[0, :, at].astype(F32), two[:, at].astype(F32))
            high = jnp.where(hop == 3, odd[1, :, at].astype(F32), four[:, at].astype(F32))
            value = jnp.where(hop <= 2, low, high).astype(BF16)
            if k == EDGE * EDGE:
                marks[n] = value
            else:
                block[n, :, at] = value
    sends = [pltpu.make_async_copy(block, copies.at[t], sems.at[t]) for t in range(SLABS)]
    for one in sends:
        one.start()
    for one in sends:
        one.wait()


def moved(ref, row, d0, d1, d2):
    source = row - d0
    inside = jnp.logical_and(source >= 0, source < EDGE)
    base = jnp.clip(source, 0, EDGE - 1) * SPAN + PAD
    flat = d1 * EDGE + d2
    turn = flat & (LANES - 1)
    jump = (flat - turn) // LANES
    here = pltpu.roll(ref[pl.ds(base - jump, FLAT), :], turn, axis=1)
    before = pltpu.roll(ref[pl.ds(base - jump - 1, FLAT), :], turn, axis=1)
    lane = lanes_of((FLAT, LANES))
    return jnp.where(in_depth(lane, d2) & inside, jnp.where(lane >= turn, here, before), 0.0)


def prepare_kernel(scal, got, kern, upper, lowest, flip_t, cos_f, sin_f, own_out, scale_out, there_out, row_out, dep_out, own_s):
    slab = scal[0]
    zeros = jnp.zeros((PAD + 1, LANES), F32)
    for c in range(EDGE):
        own_s[c * SPAN : c * SPAN + PAD, :] = zeros[:PAD]
        own_s[c * SPAN + PAD + FLAT : (c + 1) * SPAN, :] = zeros
    for t in range(SLABS):
        for k in range(FLAT):
            piece = got[t, :, k * LANES : (k + 1) * LANES].astype(F32)
            own_s[pl.ds(t * ROWS * SPAN + PAD + k, ROWS, stride=SPAN), :] = piece
    for c in range(EDGE):
        own_out[c * FLAT : (c + 1) * FLAT, :] = own_s[c * SPAN + PAD : c * SPAN + PAD + FLAT, :].astype(BF16)
    flip = flip_t[...]

    def reversed_plane(plane):
        return dot(dot(flip, plane).astype(BF16), flip)

    kern_flat = kern.reshape(GRID * WAVES, LANES)
    first = slab == 0
    lower = slab < SLABS // 2
    for q in range(SLOTS):
        here = kern_flat[pl.ds(jnp.where(lower, q, q + 1), GRID, stride=WAVES), :]
        if q:
            there = upper[jnp.where(lower, SLOTS - q, SLOTS - 1 - q)]
            scale_out[q] = here + reversed_plane(there)
        else:
            here = here.astype(BF16).astype(F32)
            low = lowest[...].astype(F32)
            there = jnp.where(lower, low, upper[SLOTS - 1].astype(F32))
            both = here + reversed_plane(jnp.where(first, here, there).astype(BF16))
            top = low + reversed_plane(lowest[...])
            scale_out[0] = jnp.where(first, 0.25 * (both + top), both)
            scale_out[SLOTS] = jnp.where(first, 0.25 * (both - top), 0.0)
    for n in range(PAIRS):
        d0, d1, d2 = scal[1 + 3 * n], scal[2 + 3 * n], scal[3 + 3 * n]
        for r in range(ROWS):
            there_out[n, r] = moved(own_s, slab * ROWS + r, -d0, -d1, -d2).astype(BF16)
    for n in range(PAIRS):
        for m in range(2):
            d0 = scal[1 + 3 * n] * m
            d2 = scal[3 + 3 * n] * m
            c = cos_f[pl.ds(HALF + d0, EDGE), :].astype(BF16)
            s = sin_f[pl.ds(HALF + d0, EDGE), :].astype(BF16)
            base = m * 2 * EDGE
            row_out[n, base : base + EDGE, :GRID] = c
            row_out[n, base : base + EDGE, GRID:] = -s
            row_out[n, base + EDGE : base + 2 * EDGE, :GRID] = s
            row_out[n, base + EDGE : base + 2 * EDGE, GRID:] = c
            turn = (GRID - HALF - d2) & (LANES - 1)
            low = low_half((GRID, LANES))
            c = pltpu.roll(cos_f[...], turn, axis=1)
            s = pltpu.roll(sin_f[...], turn, axis=1)
            dep_out[n, m, :GRID, :] = jnp.where(low, c, swapped(s)).astype(BF16)
            dep_out[n, m, GRID:, :] = jnp.where(low, -s, swapped(c)).astype(BF16)


def pair_kernel(
    scal,
    own_h,
    far_in,
    scale_t,
    row_h,
    dep_h,
    first_h,
    depth_h,
    rows_h,
    flip_h,
    send,
    here_out,
    far_s,
    zr,
    zi,
    back_s,
    own_s,
    row_t,
    dep_t,
    first_t,
    depth_t,
    rows_t,
    flip_t,
    sems,
):
    slab = scal[0]
    held = (own_h, row_h, dep_h, first_h, depth_h, rows_h, flip_h)
    local = (own_s, row_t, dep_t, first_t, depth_t, rows_t, flip_t)
    loads = [pltpu.make_async_copy(a, b, sems.at[i]) for i, (a, b) in enumerate(zip(held, local))]
    for load in loads:
        load.start()
    low_d = low_half((FLAT, LANES))
    low_w = low_half((SLOTS, LANES))
    lane_d = lanes_of((FLAT, LANES))
    lane_r = lanes_of((ROWS, LANES))
    blank = jnp.zeros((FLAT + 8, LANES), F32)
    for n in range(PAIRS):
        d0, d1, d2 = scal[1 + 3 * n], scal[2 + 3 * n], scal[3 + 3 * n]
        flat = d1 * EDGE + d2
        turn = flat & (LANES - 1)
        jump = (flat - turn) // LANES

        def clear(c, carry):
            far_s[pl.ds((HALF + c) * SPAN + PAD - 8, FLAT + 8), :] = blank
            return carry

        lax.fori_loop(0, EDGE, clear, 0, unroll=8)
        keep = in_depth(lane_r, d2)
        for t in range(SLABS):
            start = (HALF + t * ROWS + d0) * SPAN + PAD + jump
            for k in range(FLAT):
                piece = far_in[t, n, :, k * LANES : (k + 1) * LANES].astype(F32)
                piece = jnp.where(keep, pltpu.roll(piece, turn, axis=1), 0.0)
                far_s[pl.ds(start + k, ROWS, stride=SPAN), :] = piece
        after = lane_d >= turn
        if n == 0:
            for load in loads:
                load.wait()
            first = first_t[slab]
        depth_m = depth_t[...]
        rows_m = rows_t[...]
        flip = flip_t[...]

        def aligned(c):
            base = (HALF + c) * SPAN + PAD
            return jnp.where(after, far_s[pl.ds(base, FLAT), :], far_s[pl.ds(base - 1, FLAT), :])

        def own_row(c):
            return own_s[pl.ds(pl.multiple_of(c * FLAT, FLAT), FLAT), :].astype(F32)

        def forward(step, carry):
            waves = []
            for quad in range(2):
                sides = []
                for half in range(2):
                    a = step * 8 + quad * 4 + half * 2
                    dens_a = own_row(a) * aligned(a)
                    dens_b = own_row(a + 1) * aligned(a + 1)
                    even = jnp.where(low_d, dens_a, swapped(dens_b)).astype(BF16)
                    odd = jnp.where(low_d, swapped(dens_a), dens_b).astype(BF16)
                    sides.append(jnp.concatenate([even, odd], axis=0))
                y = dot(first, jnp.concatenate(sides, axis=1))
                for half in range(2):
                    re = y[:SLOTS, half * LANES : (half + 1) * LANES]
                    im = y[SLOTS:, half * LANES : (half + 1) * LANES]
                    waves.append(jnp.where(low_w, re, swapped(im)))
                    waves.append(jnp.where(low_w, swapped(re), im))
            z = dot(jnp.concatenate(waves, axis=0).astype(BF16), depth_m)
            for q in range(8):
                block = z[q * SLOTS : (q + 1) * SLOTS]
                zr[pl.ds(step * 8 + q, SLOTS, stride=ZSPAN), :] = block[:, :LANES]
                zi[pl.ds(step * 8 + q, SLOTS, stride=ZSPAN), :] = block[:, LANES:]
            return carry

        lax.fori_loop(0, EDGE // 8, forward, 0, unroll=2)
        tab = row_t[n]

        def plane(w):
            at = slice(w * ZSPAN, w * ZSPAN + EDGE)
            return jnp.concatenate([zr[at, :], zi[at, :]], axis=0).astype(BF16)

        for w0 in range(0, SLOTS, 2):
            x = dot(rows_m, jnp.concatenate([plane(w0), plane(w0 + 1)], axis=1))
            weight = jnp.concatenate([scale_t[w0], scale_t[w0 + 1]], axis=1)
            re, im = x[:GRID] * weight, x[GRID:] * weight
            if w0 == 0:
                edge = x[:, :LANES].astype(BF16)
                back_re = dot(dot(flip, edge[:GRID]).astype(BF16), flip)
                back_im = dot(dot(flip, edge[GRID:]).astype(BF16), flip)
                extra = scale_t[SLOTS]
                re = jnp.concatenate([re[:, :LANES] + extra * back_re, re[:, LANES:]], axis=1)
                im = jnp.concatenate([im[:, :LANES] - extra * back_im, im[:, LANES:]], axis=1)
            w = jnp.concatenate([re, im], axis=0).astype(BF16)
            v = dot(tab, w).astype(BF16)
            for m in range(2):
                re = v[2 * m * EDGE : (2 * m + 1) * EDGE]
                im = v[(2 * m + 1) * EDGE : (2 * m + 2) * EDGE]
                left = jnp.concatenate(
                    [
                        jnp.concatenate([re[:, :LANES], im[:, :LANES]], axis=1),
                        jnp.concatenate([re[:, LANES:], im[:, LANES:]], axis=1),
                    ],
                    axis=0,
                )
                r = dot(left, dep_t[n, m])
                for h in range(2):
                    back_s[pl.ds(m * SLOTS + w0 + h, EDGE, stride=BSPAN), :] = r[h * EDGE : (h + 1) * EDGE]
        for t in range(SLABS):
            for r in range(ROWS):
                at = (t * ROWS + r) * BSPAN
                send[t, n, r] = back_s[at : at + 2 * SLOTS, :].astype(BF16)
        for r in range(ROWS):
            here_out[n, r] = aligned(slab * ROWS + r).astype(BF16)


def term_kernel(scal, got, here, there, last_t, own_out, odd_out, even_out, far_s):
    low = low_half((FLAT, LANES))
    scale = 1.0 / GRID**3

    def table(m, shift):
        parts = [last_t[pl.ds((2 * m + f) * GRID + HALF + shift + par, FLAT, stride=2), :] for f in range(2) for par in range(2)]
        return jnp.concatenate(parts, axis=0)

    own_tab = table(0, 0)
    for n in range(PAIRS):
        tab = jnp.concatenate([own_tab, table(1, scal[1 + n])], axis=0).astype(BF16)
        for row in range(0, ROWS, 2):
            data = [jnp.concatenate([got[t, n, row + q] for t in range(SLABS)], axis=0) for q in range(2)]
            g = dot(tab, jnp.concatenate(data, axis=1))
            for q in range(2):
                pots = []
                for m in range(2):
                    part = g[m * GRID : (m + 1) * GRID, q * LANES : (q + 1) * LANES]
                    c0, c1, s0, s1 = (part[f * FLAT : (f + 1) * FLAT] for f in range(4))
                    pots.append(jnp.where(low, c0 - swapped(s0), swapped(c1) - s1) * scale)
                term = pots[0] * here[n, row + q].astype(F32)
                own_out[row + q] = term if n == 0 else own_out[row + q] + term
                far_s[n, row + q] = pots[1] * there[n, row + q].astype(F32)
    hops = [scal[3 + n] for n in range(PAIRS)]
    for e in range(1, 5):
        target = odd_out if e % 2 else even_out
        for row in range(ROWS):
            value = sum(jnp.where(hops[n] == e, far_s[n, row], 0.0) for n in range(PAIRS))
            target[(e - 1) // 2, row] = value.astype(BF16)


VMEM = pl.BlockSpec(memory_space=pltpu.VMEM)
SMEM = pl.BlockSpec(memory_space=pltpu.SMEM)
HBM = pl.BlockSpec(memory_space=pltpu.HBM)


def kept(shape, dtype):
    return pltpu.VMEM(shape, dtype)


def far(shape, dtype):
    return pltpu.HBM(shape, dtype)


def away(x):
    return pltpu.with_memory_space_constraint(x, pltpu.HBM)


def near(x):
    return pltpu.with_memory_space_constraint(x, pltpu.VMEM)


def load_call(offsets, own, interpret=False):
    return pl.pallas_call(
        load_kernel,
        out_shape=(
            kept((ROWS, EDGE * EDGE + LANES), BF16),
            kept((SLABS, ROWS, EDGE * EDGE), BF16),
        ),
        in_specs=[SMEM, VMEM],
        out_specs=(VMEM,) * 2,
        interpret=interpret,
        name="load",
        compiler_params=pltpu.CompilerParams(vmem_limit_bytes=8 << 20),
    )(offsets, own)


def mirror_call(kernel, interpret=False):
    return pl.pallas_call(
        mirror_kernel,
        out_shape=(
            kept((SLOTS, GRID, LANES), BF16),
            kept((GRID, LANES), BF16),
        ),
        in_specs=[VMEM],
        out_specs=(VMEM,) * 2,
        interpret=interpret,
        name="mirror",
        compiler_params=pltpu.CompilerParams(vmem_limit_bytes=8 << 20),
    )(kernel)


def pick_call(hops, two, four, odd, interpret=False):
    return pl.pallas_call(
        pick_kernel,
        out_shape=(
            far((SLABS, PAIRS, ROWS, EDGE * EDGE), BF16),
            kept((PAIRS, ROWS, LANES), BF16),
        ),
        in_specs=[SMEM] + [VMEM] * 3,
        out_specs=(HBM, VMEM),
        scratch_shapes=[pltpu.VMEM((PAIRS, ROWS, EDGE * EDGE), BF16), pltpu.SemaphoreType.DMA((SLABS,))],
        interpret=interpret,
        name="pick",
        compiler_params=pltpu.CompilerParams(vmem_limit_bytes=8 << 20),
    )(hops, near(two), near(four), near(odd))


def prepare_call(scal, got, kernel, upper, lowest, interpret=False):
    return pl.pallas_call(
        prepare_kernel,
        out_shape=(
            far((EDGE * FLAT, LANES), BF16),
            kept((SLOTS + 1, GRID, LANES), F32),
            far((PAIRS, ROWS, FLAT, LANES), BF16),
            far((PAIRS, 4 * EDGE, 2 * GRID), BF16),
            far((PAIRS, 2, 2 * GRID, LANES), BF16),
        ),
        in_specs=[SMEM] + [VMEM] * 7,
        out_specs=(VMEM,) * 5,
        scratch_shapes=[pltpu.VMEM((EDGE * SPAN, LANES), F32)],
        interpret=interpret,
        name="prepare",
        compiler_params=pltpu.CompilerParams(vmem_limit_bytes=12 << 20),
    )(scal, near(got), kernel, near(upper), near(lowest), jnp.asarray(reversal()), jnp.asarray(COS), jnp.asarray(SIN))


def pair_call(scal, own_s, far_box, scale, rows, depths, interpret=False):
    return pl.pallas_call(
        pair_kernel,
        out_shape=(
            jax.ShapeDtypeStruct((SLABS, PAIRS, ROWS, 2 * SLOTS, LANES), BF16),
            kept((PAIRS, ROWS, FLAT, LANES), BF16),
        ),
        in_specs=[SMEM, HBM, VMEM, VMEM] + [HBM] * 6,
        out_specs=(VMEM, VMEM),
        scratch_shapes=[
            pltpu.VMEM((ROOM * SPAN, LANES), F32),
            pltpu.VMEM((SLOTS * ZSPAN, LANES), F32),
            pltpu.VMEM((SLOTS * ZSPAN, LANES), F32),
            pltpu.VMEM((EDGE * BSPAN, LANES), F32),
            pltpu.VMEM((EDGE * FLAT, LANES), BF16),
            pltpu.VMEM((PAIRS, 4 * EDGE, 2 * GRID), BF16),
            pltpu.VMEM((PAIRS, 2, 2 * GRID, LANES), BF16),
            pltpu.VMEM((SLABS, 2 * SLOTS, EDGE), BF16),
            pltpu.VMEM((GRID, 2 * GRID), BF16),
            pltpu.VMEM((2 * GRID, GRID), BF16),
            pltpu.VMEM((GRID, GRID), BF16),
            pltpu.SemaphoreType.DMA((7,)),
        ],
        interpret=interpret,
        name="pair_waves",
        compiler_params=pltpu.CompilerParams(vmem_limit_bytes=20 << 20),
    )(
        scal,
        away(own_s),
        near(far_box),
        near(scale),
        away(rows),
        away(depths),
        away(jnp.asarray(forward_first())),
        away(jnp.asarray(forward_depth())),
        away(jnp.asarray(forward_rows())),
        away(jnp.asarray(reversal())),
    )


def term_call(scal, got, here, there, interpret=False):
    return pl.pallas_call(
        term_kernel,
        out_shape=(
            kept((ROWS, FLAT, LANES), F32),
            kept((2, ROWS, FLAT, LANES), BF16),
            kept((2, ROWS, FLAT, LANES), BF16),
        ),
        in_specs=[SMEM] + [VMEM] * 4,
        out_specs=(VMEM,) * 3,
        scratch_shapes=[pltpu.VMEM((PAIRS, ROWS, FLAT, LANES), F32)],
        interpret=interpret,
        name="pair_terms",
        compiler_params=pltpu.CompilerParams(vmem_limit_bytes=12 << 20),
    )(scal, near(got), near(here), there, jnp.asarray(backward_last()))


def passed_along(block, distance):
    count = lax.axis_size("orb")
    return lax.ppermute(block, "orb", [((i - distance) % count, i) for i in range(count)])


def other_core(block):
    count = lax.axis_size("orb")
    return lax.ppermute(block, "orb", [(i ^ 1, i) for i in range(count)])


def shared(block):
    return lax.all_to_all(block, "slab", split_axis=0, concat_axis=0, tiled=True)


def per_device(orbitals, partners, offsets, kernel):
    orbit = lax.axis_index("orb")
    slab = lax.axis_index("slab").astype(jnp.int32)
    even_core = orbit % 2 == 0
    loaded, copies = load_call(offsets, orbitals[0])
    four = passed_along(loaded, -4)
    two = passed_along(loaded, -2)
    own_box = shared(copies)
    upper, lowest = mirror_call(kernel)
    given = jnp.stack([jnp.where(even_core, two, loaded), jnp.where(even_core, four, two)])
    odd = other_core(given)
    hops = (partners[0] - orbit) % lax.axis_size("orb")
    copies, marks = pick_call(hops, two, four, odd)
    far_box = shared(copies)
    upper = lax.ppermute(upper, "slab", [(s, SLABS - 1 - s) for s in range(SLABS)])
    lowest = lax.ppermute(lowest, "slab", [(4, 0), (7, 1), (6, 2), (5, 3)])
    shifts = marks[:, 0, :3].astype(jnp.int32) - offsets
    scal = jnp.concatenate([slab[None], shifts.reshape(-1)])
    own_s, scale, there, rows, depths = prepare_call(scal, own_box, kernel, upper, lowest)
    send, here = pair_call(scal, own_s, far_box, scale, rows, depths)
    got = shared(send)
    scal = jnp.concatenate([jnp.zeros((1,), jnp.int32), shifts[:, 1], hops])
    mine, odd_out, even_out = term_call(scal, got, here, there)
    crossed = other_core(odd_out).astype(F32)
    by_two = even_out[0].astype(F32) + jnp.where(even_core, crossed[0], crossed[1])
    by_four = even_out[1].astype(F32) + jnp.where(even_core, crossed[1], 0.0)
    four_back = passed_along(by_four.astype(BF16), 4).astype(F32)
    two_back = passed_along(by_two.astype(BF16), 2).astype(F32)
    total = mine + jnp.where(even_core, 0.0, crossed[0]) + two_back + four_back
    return total.reshape(1, ROWS, EDGE * EDGE)


def solution(mesh):
    return jax.shard_map(
        per_device,
        mesh=mesh,
        in_specs=(P("orb", "slab", None), P("orb", None), P("orb", None), P(None, "slab", None)),
        out_specs=P("orb", "slab", None),
        check_vma=False,
    )
```

```python
import jax
import jax.numpy as jnp
import numpy as np
from jax import lax
from jax.experimental import pallas as pl
from jax.experimental.pallas import tpu as pltpu
from jax.sharding import PartitionSpec as P


EDGE = 64
GRID = 128
HALF = 32
SLABS = 8
ROWS = EDGE // SLABS
WAVES = GRID // SLABS
PAIRS = 2
LANES = 128
CELLS = EDGE * EDGE
FLAT = CELLS // LANES
PAD = 24
SPAN = PAD + FLAT + PAD + 1
SLOTS = 8
TWIN = 2 * SLOTS
ZSPAN = EDGE + 1
BSPAN = SLOTS + 1
RSPAN = FLAT + 1
F32 = jnp.float32
BF16 = jnp.bfloat16


def full_tables():
    index = np.arange(GRID)
    angle = (index[:, None] * index[None, :] % GRID) * (2.0 * np.pi / GRID)
    rounded = lambda a: a.astype(np.float32).astype(BF16).astype(np.float32)
    return rounded(np.cos(angle)), rounded(np.sin(angle))


COS, SIN = full_tables()
SIGN = COS[:, EDGE]
OWN_WAVES = np.array([[WAVES * s + (s >= SLABS // 2) + q for q in range(SLOTS)] for s in range(SLABS)])


def forward_first():
    waves = OWN_WAVES.reshape(-1)
    im = -SIN[:, waves]
    im[:, 0] = SIGN
    return np.concatenate([COS[:, waves], im], axis=1)


def backward_last():
    c, s = COS.copy(), SIN.copy()
    s[:, 0] = -SIGN
    out = []
    for par in range(2):
        for table in (c, s):
            wide = np.zeros((GRID, SLABS, 2, SLOTS), np.float32)
            wide[:, :, par] = table[:, OWN_WAVES]
            out.append(wide.reshape(GRID, GRID))
    return np.concatenate(out)


def reversal():
    flip = np.zeros((GRID, GRID), np.float32)
    flip[np.arange(GRID), -np.arange(GRID) % GRID] = 1.0
    return flip.astype(BF16)


def dot(a, b):
    return jnp.dot(a, b, preferred_element_type=F32)


def swapped(x):
    return pltpu.roll(x, EDGE, axis=1)


def lanes_of(shape):
    return lax.broadcasted_iota(jnp.int32, shape, 1)


def low_half(shape):
    return lanes_of(shape) < EDGE


def shifted(ref, base, d1, d2):
    flat = d1 * EDGE + d2
    turn = flat & (LANES - 1)
    jump = (flat - turn) // LANES
    here = pltpu.roll(ref[pl.ds(base - jump, FLAT), :], turn, axis=1)
    before = pltpu.roll(ref[pl.ds(base - jump - 1, FLAT), :], turn, axis=1)
    lane = lanes_of((FLAT, LANES))
    depth = (lane & (EDGE - 1)) - d2
    return jnp.where((depth >= 0) & (depth < EDGE), jnp.where(lane >= turn, here, before), 0.0)


def clear_edges(ref, rows):
    zeros = jnp.zeros((PAD + 1, LANES), F32)
    for c in range(rows):
        ref[c * SPAN : c * SPAN + PAD, :] = zeros[:PAD]
        ref[c * SPAN + PAD + FLAT : (c + 1) * SPAN, :] = zeros


def load_kernel(corner, own, loaded, copies):
    cells = own[...]
    loaded[:, :CELLS] = cells
    lane = lanes_of((ROWS, LANES))
    mark = jnp.zeros((ROWS, LANES), F32)
    for k in range(3):
        mark = jnp.where(lane == k, corner[0, k].astype(F32), mark)
    loaded[:, CELLS:] = mark.astype(BF16)
    for t in range(SLABS):
        copies[t] = cells


def mirror_kernel(kern, upper, lowest):
    kern_flat = kern.reshape(GRID * WAVES, LANES)
    for q in range(SLOTS):
        upper[q] = kern_flat[pl.ds(SLOTS + q, GRID, stride=WAVES), :].astype(BF16)
    lowest[...] = kern_flat[pl.ds(0, GRID, stride=WAVES), :].astype(BF16)


def start_kernel(info, partners, corner, two, four, odd, own_in, first_t, send, there_out, with_out, scal, own_s, part_s):
    slab, orbit = info[0], info[1]
    clear_edges(own_s, EDGE)
    for t in range(SLABS):
        for k in range(FLAT):
            piece = own_in[t, :, k * LANES : (k + 1) * LANES].astype(F32)
            own_s[pl.ds(t * ROWS * SPAN + PAD + k, ROWS, stride=SPAN), :] = piece
    scal[0] = slab
    low_d = low_half((FLAT, LANES))
    low_w = low_half((EDGE, LANES))
    lane = lanes_of((ROWS, LANES))
    weight = jnp.where(lane == 0, 1.0, jnp.where(lane == 1, 64.0, jnp.where(lane == 2, 4096.0, 0.0)))
    for n in range(PAIRS):
        hop = (partners[0, n] - orbit) & (EDGE - 1)
        for k in range(FLAT + 1):
            at = slice(k * LANES, (k + 1) * LANES)
            low = jnp.where(hop == 1, odd[0, :, at].astype(F32), two[:, at].astype(F32))
            high = jnp.where(hop == 3, odd[1, :, at].astype(F32), four[:, at].astype(F32))
            value = jnp.where(hop <= 2, low, high)
            if k < FLAT:
                part_s[pl.ds(k, ROWS, stride=RSPAN), :] = value
            else:
                code = jnp.sum(value[:1] * weight[:1]).astype(jnp.int32)
        d0 = (code & 63) - corner[0, 0]
        d1 = ((code >> 6) & 63) - corner[0, 1]
        d2 = (code >> 12) - corner[0, 2]
        scal[1 + 3 * n] = d0
        scal[2 + 3 * n] = d1
        scal[3 + 3 * n] = d2
        scal[7 + n] = hop
        halves = [first_t[pl.ds(HALF + d1 + par, FLAT, stride=2), :] for par in range(2)]
        first = jnp.concatenate(halves, axis=0).T.astype(BF16)
        sides = []
        for r in range(ROWS):
            source = slab * ROWS + r + d0
            inside = jnp.logical_and(source >= 0, source < EDGE)
            base = jnp.clip(source, 0, EDGE - 1) * SPAN + PAD
            there = jnp.where(inside, shifted(own_s, base, -d1, -d2), 0.0)
            part = part_s[r * RSPAN : r * RSPAN + FLAT, :]
            there_out[n, r] = there.astype(BF16)
            with_out[n, r] = part.astype(BF16)
            sides.append(there * part)
        for quad in range(ROWS // 4):
            columns = []
            for half in range(2):
                a, b = sides[quad * 4 + half * 2], sides[quad * 4 + half * 2 + 1]
                even = jnp.where(low_d, a, swapped(b)).astype(BF16)
                odd_part = jnp.where(low_d, swapped(a), b).astype(BF16)
                columns.append(jnp.concatenate([even, odd_part], axis=0))
            y = dot(first, jnp.concatenate(columns, axis=1))
            for half in range(2):
                re = y[:EDGE, half * LANES : (half + 1) * LANES]
                im = y[EDGE:, half * LANES : (half + 1) * LANES]
                wave_a = jnp.where(low_w, re, swapped(im))
                wave_b = jnp.where(low_w, swapped(re), im)
                for s in range(SLABS):
                    at = slice(s * SLOTS, (s + 1) * SLOTS)
                    both = jnp.concatenate([wave_a[at], wave_b[at]], axis=0)
                    send[s, n, quad * 2 + half] = both.astype(BF16)


def prepare_kernel(scal, kern, upper, lowest, flip_t, cos_f, sin_f, scale_out, rowf_out, depf_out, rowb_out, depb_out):
    slab = scal[0]
    flip = flip_t[...]

    def reversed_plane(plane):
        return dot(dot(flip, plane).astype(BF16), flip)

    kern_flat = kern.reshape(GRID * WAVES, LANES)
    first = slab == 0
    lower = slab < SLABS // 2
    for q in range(SLOTS):
        here = kern_flat[pl.ds(jnp.where(lower, q, q + 1), GRID, stride=WAVES), :]
        if q:
            there = upper[jnp.where(lower, SLOTS - q, SLOTS - 1 - q)]
            scale_out[q] = here + reversed_plane(there)
        else:
            here = here.astype(BF16).astype(F32)
            low = lowest[...].astype(F32)
            there = jnp.where(lower, low, upper[SLOTS - 1].astype(F32))
            both = here + reversed_plane(jnp.where(first, here, there).astype(BF16))
            top = low + reversed_plane(lowest[...])
            scale_out[0] = jnp.where(first, 0.25 * (both + top), both)
            scale_out[SLOTS] = jnp.where(first, 0.25 * (both - top), 0.0)
    half = low_half((GRID, LANES))

    def by_wave(shift):
        turn = (GRID - HALF - shift) & (LANES - 1)
        c = pltpu.roll(cos_f[...], turn, axis=1)
        s = pltpu.roll(sin_f[...], turn, axis=1)
        return jnp.where(half, c, swapped(s)).astype(BF16), jnp.where(half, -s, swapped(c)).astype(BF16)

    for n in range(PAIRS):
        d0, d2 = scal[1 + 3 * n], scal[3 + 3 * n]
        rowf_out[n, :GRID, :], rowf_out[n, GRID:, :] = by_wave(d0)
        depb_out[n, :GRID, :], depb_out[n, GRID:, :] = by_wave(d2)
        c, s = (ref[pl.ds(HALF + d0, EDGE), :].astype(BF16) for ref in (cos_f, sin_f))
        rowb_out[n] = jnp.concatenate(
            [jnp.concatenate([c, -s], axis=1), jnp.concatenate([s, c], axis=1)], axis=0
        )
        c, s = (ref[pl.ds(HALF + d2, EDGE), :].astype(BF16) for ref in (cos_f, sin_f))
        depf_out[n] = jnp.concatenate(
            [jnp.concatenate([c, -s], axis=1), jnp.concatenate([s, c], axis=1)], axis=0
        )


def wave_kernel(got, scale_t, rowf_h, depf_h, rowb_h, depb_h, flip_h, send, zr, zi, back_s, rowf_t, depf_t, rowb_t, depb_t, flip_t, sems):
    held = (depf_h, rowf_h, rowb_h, depb_h, flip_h)
    local = (depf_t, rowf_t, rowb_t, depb_t, flip_t)
    loads = [pltpu.make_async_copy(a, b, sems.at[i]) for i, (a, b) in enumerate(zip(held, local))]
    for load in loads:
        load.start()
    for load in loads:
        load.wait()
    flip = flip_t[...]
    for n in range(PAIRS):
        at_z = n * SLOTS * ZSPAN
        at_b = n * EDGE * BSPAN
        depth_m = depf_t[n]
        rows_m = rowf_t[n]
        for t in range(SLABS):
            block = jnp.concatenate([got[t, n, p] for p in range(ROWS // 2)], axis=0)
            z = dot(block, depth_m)
            for r in range(ROWS):
                part = z[r * SLOTS : (r + 1) * SLOTS]
                zr[pl.ds(at_z + t * ROWS + r, SLOTS, stride=ZSPAN), :] = part[:, :LANES]
                zi[pl.ds(at_z + t * ROWS + r, SLOTS, stride=ZSPAN), :] = part[:, LANES:]

        def plane(w):
            at = slice(at_z + w * ZSPAN, at_z + w * ZSPAN + EDGE)
            return jnp.concatenate([zr[at, :], zi[at, :]], axis=0).astype(BF16)

        for w0 in range(0, SLOTS, 2):
            x = dot(rows_m, jnp.concatenate([plane(w0), plane(w0 + 1)], axis=1))
            weight = jnp.concatenate([scale_t[w0], scale_t[w0 + 1]], axis=1)
            re, im = x[:GRID] * weight, x[GRID:] * weight
            if w0 == 0:
                edge = x[:, :LANES].astype(BF16)
                back_re = dot(dot(flip, edge[:GRID]).astype(BF16), flip)
                back_im = dot(dot(flip, edge[GRID:]).astype(BF16), flip)
                extra = scale_t[SLOTS]
                re = jnp.concatenate([re[:, :LANES] + extra * back_re, re[:, LANES:]], axis=1)
                im = jnp.concatenate([im[:, :LANES] - extra * back_im, im[:, LANES:]], axis=1)
            v = dot(rowb_t[n], jnp.concatenate([re, im], axis=0).astype(BF16)).astype(BF16)
            re, im = v[:EDGE], v[EDGE:]
            left = jnp.concatenate(
                [
                    jnp.concatenate([re[:, :LANES], im[:, :LANES]], axis=1),
                    jnp.concatenate([re[:, LANES:], im[:, LANES:]], axis=1),
                ],
                axis=0,
            )
            r = dot(left, depb_t[n])
            for h in range(2):
                back_s[pl.ds(at_b + w0 + h, EDGE, stride=BSPAN), :] = r[h * EDGE : (h + 1) * EDGE]
        for t in range(SLABS):
            for p in range(ROWS // 2):
                at = at_b + (t * ROWS + 2 * p) * BSPAN
                both = jnp.concatenate([back_s[at : at + SLOTS, :], back_s[at + BSPAN : at + BSPAN + SLOTS, :]], axis=0)
                send[t, n, p] = both.astype(BF16)


def term_kernel(scal, got, there, withs, last_t, move_out, odd_out, even_out, far_s, own_s, sum_s):
    slab = scal[0]
    low = low_half((FLAT, LANES))
    scale = 1.0 / GRID**3
    clear_edges(own_s, PAIRS * ROWS)
    blank = jnp.zeros((FLAT, LANES), F32)
    for c in range(EDGE):
        sum_s[HALF + c] = blank
    for n in range(PAIRS):
        d0, d1, d2 = scal[1 + 3 * n], scal[2 + 3 * n], scal[3 + 3 * n]
        parts = [
            last_t[pl.ds((2 * row + f) * GRID + HALF + d1 + par, FLAT, stride=2), :]
            for row in range(2)
            for f in range(2)
            for par in range(2)
        ]
        tab = jnp.concatenate(parts, axis=0).astype(BF16)
        for quad in range(ROWS // 4):
            data = [jnp.concatenate([got[t, n, quad * 2 + h] for t in range(SLABS)], axis=0) for h in range(2)]
            g = dot(tab, jnp.concatenate(data, axis=1))
            for h in range(2):
                for par in range(2):
                    r = quad * 4 + h * 2 + par
                    part = g[par * GRID : (par + 1) * GRID, h * LANES : (h + 1) * LANES]
                    c0, c1, s0, s1 = (part[f * FLAT : (f + 1) * FLAT] for f in range(4))
                    pot = jnp.where(low, c0 - swapped(s0), swapped(c1) - s1) * scale
                    far_s[n, r] = pot * there[n, r].astype(F32)
                    base = (n * ROWS + r) * SPAN + PAD
                    own_s[base : base + FLAT, :] = pot * withs[n, r].astype(F32)
        for r in range(ROWS):
            base = (n * ROWS + r) * SPAN + PAD
            at = HALF + slab * ROWS + r + d0
            sum_s[at] = sum_s[at] + shifted(own_s, base, d1, d2)
    for t in range(SLABS):
        for r in range(ROWS):
            move_out[t, r] = sum_s[HALF + t * ROWS + r].astype(BF16)
    hops = [scal[7 + n] for n in range(PAIRS)]
    for e in range(1, 5):
        target = odd_out if e % 2 else even_out
        for row in range(ROWS):
            value = sum(jnp.where(hops[n] == e, far_s[n, row], 0.0) for n in range(PAIRS))
            target[(e - 1) // 2, row] = value.astype(BF16)


def final_kernel(odd_core, moved, crossed, two, four, out, total_s):
    keep = odd_core[0] == 1
    for r in range(ROWS):
        total = two[r].astype(F32) + four[r].astype(F32) + jnp.where(keep, crossed[0, r].astype(F32), 0.0)
        for t in range(SLABS):
            total = total + moved[t, r].astype(F32)
        total_s[r * RSPAN : r * RSPAN + FLAT, :] = total
    for k in range(FLAT):
        out[:, k * LANES : (k + 1) * LANES] = total_s[pl.ds(k, ROWS, stride=RSPAN), :]


VMEM = pl.BlockSpec(memory_space=pltpu.VMEM)
SMEM = pl.BlockSpec(memory_space=pltpu.SMEM)
HBM = pl.BlockSpec(memory_space=pltpu.HBM)


def kept(shape, dtype):
    return pltpu.VMEM(shape, dtype)


def far(shape, dtype):
    return pltpu.HBM(shape, dtype)


def away(x):
    return pltpu.with_memory_space_constraint(x, pltpu.HBM)


def near(x):
    return pltpu.with_memory_space_constraint(x, pltpu.VMEM)


def call(kernel, mib, in_specs, out_shape, out_specs, scratch, args):
    return pl.pallas_call(
        kernel,
        out_shape=out_shape,
        in_specs=in_specs,
        out_specs=out_specs,
        scratch_shapes=scratch,
        interpret=INTERPRET,
        compiler_params=pltpu.CompilerParams(vmem_limit_bytes=mib << 20),
    )(*args)


INTERPRET = False
ROWBOX = (PAIRS, ROWS, FLAT, LANES)
PACKET = (SLABS, PAIRS, ROWS // 2, TWIN, LANES)


def load_call(offsets, own):
    shapes = (kept((ROWS, CELLS + LANES), BF16), kept((SLABS, ROWS, CELLS), BF16))
    return call(load_kernel, 8, [SMEM, VMEM], shapes, (VMEM,) * 2, (), (offsets, own))


def mirror_call(kernel):
    shapes = (kept((SLOTS, GRID, LANES), BF16), kept((GRID, LANES), BF16))
    return call(mirror_kernel, 8, [VMEM], shapes, (VMEM,) * 2, (), (kernel,))


def start_call(info, partners, offsets, two, four, odd, own_box):
    shapes = (far(PACKET, BF16), far(ROWBOX, BF16), far(ROWBOX, BF16), jax.ShapeDtypeStruct((9,), jnp.int32))
    scratch = (pltpu.VMEM((EDGE * SPAN, LANES), F32), pltpu.VMEM((ROWS * RSPAN, LANES), F32))
    args = (info, partners, offsets, near(two), near(four), near(odd), near(own_box), jnp.asarray(forward_first()))
    return call(start_kernel, 12, [SMEM] * 3 + [VMEM] * 5, shapes, (VMEM,) * 3 + (SMEM,), scratch, args)


def prepare_call(scal, kernel, upper, lowest):
    shapes = (
        kept((SLOTS + 1, GRID, LANES), F32),
        far((PAIRS, 2 * GRID, LANES), BF16),
        far((PAIRS, GRID, 2 * LANES), BF16),
        far((PAIRS, GRID, 2 * LANES), BF16),
        far((PAIRS, 2 * GRID, LANES), BF16),
    )
    args = (scal, kernel, near(upper), near(lowest), jnp.asarray(reversal()), jnp.asarray(COS), jnp.asarray(SIN))
    return call(prepare_kernel, 12, [SMEM] + [VMEM] * 6, shapes, (VMEM,) * 5, (), args)


def wave_call(got, scale, tables):
    scratch = (
        pltpu.VMEM((PAIRS * SLOTS * ZSPAN, LANES), F32),
        pltpu.VMEM((PAIRS * SLOTS * ZSPAN, LANES), F32),
        pltpu.VMEM((PAIRS * EDGE * BSPAN, LANES), F32),
        pltpu.VMEM((PAIRS, 2 * GRID, LANES), BF16),
        pltpu.VMEM((PAIRS, GRID, 2 * LANES), BF16),
        pltpu.VMEM((PAIRS, GRID, 2 * LANES), BF16),
        pltpu.VMEM((PAIRS, 2 * GRID, LANES), BF16),
        pltpu.VMEM((GRID, GRID), BF16),
        pltpu.SemaphoreType.DMA((5,)),
    )
    args = (near(got), near(scale), *(away(t) for t in tables), away(jnp.asarray(reversal())))
    return call(wave_kernel, 16, [VMEM] * 2 + [HBM] * 5, far(PACKET, BF16), VMEM, scratch, args)


def term_call(scal, got, there, withs):
    half = (2, ROWS, FLAT, LANES)
    shapes = (far((SLABS, ROWS, FLAT, LANES), BF16), kept(half, BF16), kept(half, BF16))
    scratch = (
        pltpu.VMEM(ROWBOX, F32),
        pltpu.VMEM((PAIRS * ROWS * SPAN, LANES), F32),
        pltpu.VMEM((HALF + EDGE + HALF, FLAT, LANES), F32),
    )
    args = (scal, near(got), there, withs, jnp.asarray(backward_last()))
    return call(term_kernel, 16, [SMEM] + [VMEM] * 4, shapes, (VMEM,) * 3, scratch, args)


def final_call(odd_core, moved, crossed, two, four):
    scratch = (pltpu.VMEM((ROWS * RSPAN, LANES), F32),)
    shape = jax.ShapeDtypeStruct((ROWS, CELLS), F32)
    args = (odd_core, near(moved), near(crossed), near(two), near(four))
    return call(final_kernel, 8, [SMEM] + [VMEM] * 4, shape, VMEM, scratch, args)


def passed_along(block, distance):
    count = lax.axis_size("orb")
    return lax.ppermute(block, "orb", [((i - distance) % count, i) for i in range(count)])


def other_core(block):
    count = lax.axis_size("orb")
    return lax.ppermute(block, "orb", [(i ^ 1, i) for i in range(count)])


def shared(block):
    return lax.all_to_all(block, "slab", split_axis=0, concat_axis=0, tiled=True)


def per_device(orbitals, partners, offsets, kernel):
    orbit = lax.axis_index("orb").astype(jnp.int32)
    slab = lax.axis_index("slab").astype(jnp.int32)
    even_core = orbit % 2 == 0
    info = jnp.stack([slab, orbit])
    odd_core = (orbit % 2)[None]
    loaded, copies = load_call(offsets, orbitals[0])
    four = passed_along(loaded, -4)
    two = passed_along(loaded, -2)
    own_box = shared(copies)
    upper, lowest = mirror_call(kernel)
    given = jnp.stack([jnp.where(even_core, two, loaded), jnp.where(even_core, four, two)])
    odd = other_core(given)
    upper = lax.ppermute(upper, "slab", [(s, SLABS - 1 - s) for s in range(SLABS)])
    send, there, withs, scal = start_call(info, partners, offsets, two, four, odd, own_box)
    got = shared(send)
    lowest = lax.ppermute(lowest, "slab", [(4, 0), (7, 1), (6, 2), (5, 3)])
    scale, *tables = prepare_call(scal, kernel, upper, lowest)
    send = wave_call(got, scale, tables)
    got = shared(send)
    move, odd_out, even_out = term_call(scal, got, there, withs)
    crossed = other_core(odd_out)
    move = shared(move)
    by_two = even_out[0].astype(F32) + jnp.where(even_core, crossed[0], crossed[1]).astype(F32)
    by_four = even_out[1].astype(F32) + jnp.where(even_core, crossed[1], 0.0).astype(F32)
    four_back = passed_along(by_four.astype(BF16), 4)
    two_back = passed_along(by_two.astype(BF16), 2)
    return final_call(odd_core, move, crossed, two_back, four_back)[None]


def solution(mesh):
    return jax.shard_map(
        per_device,
        mesh=mesh,
        in_specs=(P("orb", "slab", None), P("orb", None), P("orb", None), P(None, "slab", None)),
        out_specs=P("orb", "slab", None),
        check_vma=False,
    )
```

```python
import jax
import jax.numpy as jnp
import numpy as np
from jax import lax
from jax.experimental import pallas as pl
from jax.experimental.pallas import tpu as pltpu
from jax.sharding import PartitionSpec as P


EDGE = 64
GRID = 128
HALF = 32
SLABS = 8
ROWS = EDGE // SLABS
WAVES = GRID // SLABS
PAIRS = 2
LANES = 128
CELLS = EDGE * EDGE
FLAT = CELLS // LANES
PAD = 24
SPAN = PAD + FLAT + PAD + 1
SLOTS = 8
TWIN = 2 * SLOTS
ZSPAN = EDGE + 1
BSPAN = SLOTS + 1
RSPAN = FLAT + 1
F32 = jnp.float32
BF16 = jnp.bfloat16


def full_tables():
    index = np.arange(GRID)
    angle = (index[:, None] * index[None, :] % GRID) * (2.0 * np.pi / GRID)
    rounded = lambda a: a.astype(np.float32).astype(BF16).astype(np.float32)
    return rounded(np.cos(angle)), rounded(np.sin(angle))


COS, SIN = full_tables()
SIGN = COS[:, EDGE]
OWN_WAVES = np.array([[WAVES * s + (s >= SLABS // 2) + q for q in range(SLOTS)] for s in range(SLABS)])


def forward_first():
    waves = OWN_WAVES.reshape(-1)
    im = -SIN[:, waves]
    im[:, 0] = SIGN
    return np.concatenate([COS[:, waves], im], axis=1)


def backward_last():
    c, s = COS.copy(), SIN.copy()
    s[:, 0] = -SIGN
    out = []
    for par in range(2):
        for table in (c, s):
            wide = np.zeros((GRID, SLABS, 2, SLOTS), np.float32)
            wide[:, :, par] = table[:, OWN_WAVES]
            out.append(wide.reshape(GRID, GRID))
    return np.concatenate(out)


def reversal():
    flip = np.zeros((GRID, GRID), np.float32)
    flip[np.arange(GRID), -np.arange(GRID) % GRID] = 1.0
    return flip.astype(BF16)


def dot(a, b):
    return jnp.dot(a, b, preferred_element_type=F32)


def swapped(x):
    return pltpu.roll(x, EDGE, axis=1)


def lanes_of(shape):
    return lax.broadcasted_iota(jnp.int32, shape, 1)


def low_half(shape):
    return lanes_of(shape) < EDGE


def shifted(ref, base, d1, d2):
    flat = d1 * EDGE + d2
    turn = flat & (LANES - 1)
    jump = (flat - turn) // LANES
    here = pltpu.roll(ref[pl.ds(base - jump, FLAT), :], turn, axis=1)
    before = pltpu.roll(ref[pl.ds(base - jump - 1, FLAT), :], turn, axis=1)
    lane = lanes_of((FLAT, LANES))
    depth = (lane & (EDGE - 1)) - d2
    return jnp.where((depth >= 0) & (depth < EDGE), jnp.where(lane >= turn, here, before), 0.0)


def reversed_plane(flip, plane):
    return dot(dot(flip, plane).astype(BF16), flip)


def clear_edges(ref, rows):
    zeros = jnp.zeros((PAD + 1, LANES), F32)
    for c in range(rows):
        ref[c * SPAN : c * SPAN + PAD, :] = zeros[:PAD]
        ref[c * SPAN + PAD + FLAT : (c + 1) * SPAN, :] = zeros


def load_kernel(corner, own, loaded, copies, sems):
    loads = [pltpu.make_async_copy(own, copies.at[t], sems.at[t]) for t in range(SLABS)]
    loads.append(pltpu.make_async_copy(own, loaded.at[:, pl.ds(0, CELLS)], sems.at[SLABS]))
    for one in loads:
        one.start()
    lane = lanes_of((ROWS, LANES))
    mark = jnp.zeros((ROWS, LANES), F32)
    for k in range(3):
        mark = jnp.where(lane == k, corner[0, k].astype(F32), mark)
    loaded[:, CELLS:] = mark.astype(BF16)
    for one in loads:
        one.wait()


def mirror_kernel(kern, upper, lowest):
    kern_flat = kern.reshape(GRID * WAVES, LANES)
    for q in range(SLOTS):
        upper[q] = kern_flat[pl.ds(SLOTS + q, GRID, stride=WAVES), :].astype(BF16)
    lowest[...] = kern_flat[pl.ds(0, GRID, stride=WAVES), :].astype(BF16)


def start_kernel(info, partners, corner, two, four, odd, own_in, first_t, send, there_out, with_out, scal, own_s, part_s):
    slab, orbit = info[0], info[1]
    clear_edges(own_s, EDGE)
    for t in range(SLABS):
        for k in range(FLAT):
            piece = own_in[t, :, k * LANES : (k + 1) * LANES].astype(F32)
            own_s[pl.ds(t * ROWS * SPAN + PAD + k, ROWS, stride=SPAN), :] = piece
    scal[0] = slab
    low_d = low_half((FLAT, LANES))
    low_w = low_half((EDGE, LANES))
    lane = lanes_of((ROWS, LANES))
    weight = jnp.where(lane == 0, 1.0, jnp.where(lane == 1, 64.0, jnp.where(lane == 2, 4096.0, 0.0)))
    for n in range(PAIRS):
        hop = (partners[0, n] - orbit) & (EDGE - 1)
        for k in range(FLAT + 1):
            at = slice(k * LANES, (k + 1) * LANES)
            low = jnp.where(hop == 1, odd[0, :, at].astype(F32), two[:, at].astype(F32))
            high = jnp.where(hop == 3, odd[1, :, at].astype(F32), four[:, at].astype(F32))
            value = jnp.where(hop <= 2, low, high)
            if k < FLAT:
                part_s[pl.ds(k, ROWS, stride=RSPAN), :] = value
            else:
                code = jnp.sum(value[:1] * weight[:1]).astype(jnp.int32)
        d0 = (code & 63) - corner[0, 0]
        d1 = ((code >> 6) & 63) - corner[0, 1]
        d2 = (code >> 12) - corner[0, 2]
        scal[1 + 3 * n] = d0
        scal[2 + 3 * n] = d1
        scal[3 + 3 * n] = d2
        scal[7 + n] = hop
        halves = [first_t[pl.ds(HALF + d1 + par, FLAT, stride=2), :] for par in range(2)]
        first = jnp.concatenate(halves, axis=0).T.astype(BF16)
        sides = []
        for r in range(ROWS):
            source = slab * ROWS + r + d0
            inside = jnp.logical_and(source >= 0, source < EDGE)
            base = jnp.clip(source, 0, EDGE - 1) * SPAN + PAD
            there = jnp.where(inside, shifted(own_s, base, -d1, -d2), 0.0)
            part = part_s[r * RSPAN : r * RSPAN + FLAT, :]
            there_out[n, r] = there.astype(BF16)
            with_out[n, r] = part.astype(BF16)
            sides.append(there * part)
        for quad in range(ROWS // 4):
            columns = []
            for half in range(2):
                a, b = sides[quad * 4 + half * 2], sides[quad * 4 + half * 2 + 1]
                even = jnp.where(low_d, a, swapped(b)).astype(BF16)
                odd_part = jnp.where(low_d, swapped(a), b).astype(BF16)
                columns.append(jnp.concatenate([even, odd_part], axis=0))
            y = dot(first, jnp.concatenate(columns, axis=1))
            for half in range(2):
                re = y[:EDGE, half * LANES : (half + 1) * LANES]
                im = y[EDGE:, half * LANES : (half + 1) * LANES]
                wave_a = jnp.where(low_w, re, swapped(im))
                wave_b = jnp.where(low_w, swapped(re), im)
                for s in range(SLABS):
                    at = slice(s * SLOTS, (s + 1) * SLOTS)
                    both = jnp.concatenate([wave_a[at], wave_b[at]], axis=0)
                    send[s, n, quad * 2 + half] = both.astype(BF16)


def prepare_kernel(scal, kern, upper, flip_t, cos_f, sin_f, scale_out, rowf_out, depf_out, rowb_out, depb_out):
    slab = scal[0]
    flip = flip_t[...]
    kern_flat = kern.reshape(GRID * WAVES, LANES)
    lower = slab < SLABS // 2
    for q in range(SLOTS):
        here = kern_flat[pl.ds(jnp.where(lower, q, q + 1), GRID, stride=WAVES), :]
        if q:
            there = upper[jnp.where(lower, SLOTS - q, SLOTS - 1 - q)]
            scale_out[q] = here + reversed_plane(flip, there)
        else:
            here = here.astype(BF16).astype(F32)
            scale_out[0] = here + jnp.where(lower, 0.0, reversed_plane(flip, upper[SLOTS - 1]))
            scale_out[SLOTS] = here + reversed_plane(flip, here.astype(BF16))
    half = low_half((GRID, LANES))

    def by_wave(shift):
        turn = (GRID - HALF - shift) & (LANES - 1)
        c = pltpu.roll(cos_f[...], turn, axis=1)
        s = pltpu.roll(sin_f[...], turn, axis=1)
        return jnp.where(half, c, swapped(s)).astype(BF16), jnp.where(half, -s, swapped(c)).astype(BF16)

    for n in range(PAIRS):
        d0, d2 = scal[1 + 3 * n], scal[3 + 3 * n]
        rowf_out[n, :GRID, :], rowf_out[n, GRID:, :] = by_wave(d0)
        depb_out[n, :GRID, :], depb_out[n, GRID:, :] = by_wave(d2)
        c, s = (ref[pl.ds(HALF + d0, EDGE), :].astype(BF16) for ref in (cos_f, sin_f))
        rowb_out[n] = jnp.concatenate(
            [jnp.concatenate([c, -s], axis=1), jnp.concatenate([s, c], axis=1)], axis=0
        )
        c, s = (ref[pl.ds(HALF + d2, EDGE), :].astype(BF16) for ref in (cos_f, sin_f))
        depf_out[n] = jnp.concatenate(
            [jnp.concatenate([c, -s], axis=1), jnp.concatenate([s, c], axis=1)], axis=0
        )


def wave_kernel(scal, got, scale_t, lowest, rowf_t, depf_t, rowb_t, depb_t, flip_t, send, zr, zi, back_s):
    slab = scal[0]
    first = slab == 0
    lower = slab < SLABS // 2
    flip = flip_t[...]
    low = lowest[...]
    low_back = reversed_plane(flip, low)
    both = scale_t[SLOTS]
    top = low.astype(F32) + low_back
    bottom = scale_t[0] + jnp.where(lower, low_back, 0.0)
    main = jnp.where(first, 0.25 * (both + top), bottom)
    extra = jnp.where(first, 0.25 * (both - top), 0.0)
    for n in range(PAIRS):
        at_z = n * SLOTS * ZSPAN
        at_b = n * EDGE * BSPAN
        depth_m = depf_t[n]
        rows_m = rowf_t[n]
        for t in range(SLABS):
            block = jnp.concatenate([got[t, n, p] for p in range(ROWS // 2)], axis=0)
            z = dot(block, depth_m)
            for r in range(ROWS):
                part = z[r * SLOTS : (r + 1) * SLOTS]
                zr[pl.ds(at_z + t * ROWS + r, SLOTS, stride=ZSPAN), :] = part[:, :LANES]
                zi[pl.ds(at_z + t * ROWS + r, SLOTS, stride=ZSPAN), :] = part[:, LANES:]

        def plane(w):
            at = slice(at_z + w * ZSPAN, at_z + w * ZSPAN + EDGE)
            return jnp.concatenate([zr[at, :], zi[at, :]], axis=0).astype(BF16)

        for w0 in range(0, SLOTS, 2):
            x = dot(rows_m, jnp.concatenate([plane(w0), plane(w0 + 1)], axis=1))
            weight = jnp.concatenate([scale_t[w0] if w0 else main, scale_t[w0 + 1]], axis=1)
            re, im = x[:GRID] * weight, x[GRID:] * weight
            if w0 == 0:
                edge = x[:, :LANES].astype(BF16)
                back_re = dot(dot(flip, edge[:GRID]).astype(BF16), flip)
                back_im = dot(dot(flip, edge[GRID:]).astype(BF16), flip)
                re = jnp.concatenate([re[:, :LANES] + extra * back_re, re[:, LANES:]], axis=1)
                im = jnp.concatenate([im[:, :LANES] - extra * back_im, im[:, LANES:]], axis=1)
            v = dot(rowb_t[n], jnp.concatenate([re, im], axis=0).astype(BF16)).astype(BF16)
            re, im = v[:EDGE], v[EDGE:]
            left = jnp.concatenate(
                [
                    jnp.concatenate([re[:, :LANES], im[:, :LANES]], axis=1),
                    jnp.concatenate([re[:, LANES:], im[:, LANES:]], axis=1),
                ],
                axis=0,
            )
            r = dot(left, depb_t[n])
            for h in range(2):
                back_s[pl.ds(at_b + w0 + h, EDGE, stride=BSPAN), :] = r[h * EDGE : (h + 1) * EDGE]
        for t in range(SLABS):
            for p in range(ROWS // 2):
                at = at_b + (t * ROWS + 2 * p) * BSPAN
                both = jnp.concatenate([back_s[at : at + SLOTS, :], back_s[at + BSPAN : at + BSPAN + SLOTS, :]], axis=0)
                send[t, n, p] = both.astype(BF16)


def ready_kernel(scal, last_t, tab_out):
    for n in range(PAIRS):
        d1 = scal[2 + 3 * n]
        parts = [
            last_t[pl.ds((2 * row + f) * GRID + HALF + d1 + par, FLAT, stride=2), :]
            for row in range(2)
            for f in range(2)
            for par in range(2)
        ]
        tab_out[n] = jnp.concatenate(parts, axis=0).astype(BF16)


def term_kernel(scal, got, there, withs, tabs, move_out, odd_out, even_out, far_s, own_s, sum_s):
    slab = scal[0]
    low = low_half((FLAT, LANES))
    scale = 1.0 / GRID**3
    clear_edges(own_s, PAIRS * ROWS)
    blank = jnp.zeros((FLAT, LANES), F32)
    for c in range(EDGE):
        sum_s[HALF + c] = blank
    for n in range(PAIRS):
        d0, d1, d2 = scal[1 + 3 * n], scal[2 + 3 * n], scal[3 + 3 * n]
        tab = tabs[n]
        for quad in range(ROWS // 4):
            data = [jnp.concatenate([got[t, n, quad * 2 + h] for t in range(SLABS)], axis=0) for h in range(2)]
            g = dot(tab, jnp.concatenate(data, axis=1))
            for h in range(2):
                for par in range(2):
                    r = quad * 4 + h * 2 + par
                    part = g[par * GRID : (par + 1) * GRID, h * LANES : (h + 1) * LANES]
                    c0, c1, s0, s1 = (part[f * FLAT : (f + 1) * FLAT] for f in range(4))
                    pot = jnp.where(low, c0 - swapped(s0), swapped(c1) - s1) * scale
                    far_s[n, r] = pot * there[n, r].astype(F32)
                    base = (n * ROWS + r) * SPAN + PAD
                    own_s[base : base + FLAT, :] = pot * withs[n, r].astype(F32)
        for r in range(ROWS):
            base = (n * ROWS + r) * SPAN + PAD
            at = HALF + slab * ROWS + r + d0
            sum_s[at] = sum_s[at] + shifted(own_s, base, d1, d2)
    for t in range(SLABS):
        for r in range(ROWS):
            move_out[t, r] = sum_s[HALF + t * ROWS + r].astype(BF16)
    hops = [scal[7 + n] for n in range(PAIRS)]
    for e in range(1, 5):
        target = odd_out if e % 2 else even_out
        for row in range(ROWS):
            value = sum(jnp.where(hops[n] == e, far_s[n, row], 0.0) for n in range(PAIRS))
            target[(e - 1) // 2, row] = value.astype(BF16)


def final_kernel(odd_core, moved, crossed, two, four, out, total_s):
    keep = odd_core[0] == 1
    for r in range(ROWS):
        total = two[r].astype(F32) + four[r].astype(F32) + jnp.where(keep, crossed[0, r].astype(F32), 0.0)
        for t in range(SLABS):
            total = total + moved[t, r].astype(F32)
        total_s[r * RSPAN : r * RSPAN + FLAT, :] = total
    for k in range(FLAT):
        out[:, k * LANES : (k + 1) * LANES] = total_s[pl.ds(k, ROWS, stride=RSPAN), :]


VMEM = pl.BlockSpec(memory_space=pltpu.VMEM)
SMEM = pl.BlockSpec(memory_space=pltpu.SMEM)
HBM = pl.BlockSpec(memory_space=pltpu.HBM)


def kept(shape, dtype):
    return pltpu.VMEM(shape, dtype)


def far(shape, dtype):
    return pltpu.HBM(shape, dtype)


def away(x):
    return pltpu.with_memory_space_constraint(x, pltpu.HBM)


def near(x):
    return pltpu.with_memory_space_constraint(x, pltpu.VMEM)


def call(kernel, mib, in_specs, out_shape, out_specs, scratch, args):
    return pl.pallas_call(
        kernel,
        out_shape=out_shape,
        in_specs=in_specs,
        out_specs=out_specs,
        scratch_shapes=scratch,
        interpret=INTERPRET,
        compiler_params=pltpu.CompilerParams(vmem_limit_bytes=mib << 20),
    )(*args)


INTERPRET = False
ROWBOX = (PAIRS, ROWS, FLAT, LANES)
PACKET = (SLABS, PAIRS, ROWS // 2, TWIN, LANES)


def load_call(offsets, own):
    shapes = (kept((ROWS, CELLS + LANES), BF16), kept((SLABS, ROWS, CELLS), BF16))
    scratch = (pltpu.SemaphoreType.DMA((SLABS + 1,)),)
    return call(load_kernel, 8, [SMEM, HBM], shapes, (VMEM,) * 2, scratch, (away(offsets), away(own)))


def mirror_call(kernel):
    shapes = (kept((SLOTS, GRID, LANES), BF16), kept((GRID, LANES), BF16))
    return call(mirror_kernel, 8, [VMEM], shapes, (VMEM,) * 2, (), (kernel,))


def start_call(info, partners, offsets, two, four, odd, own_box):
    shapes = (far(PACKET, BF16), far(ROWBOX, BF16), far(ROWBOX, BF16), jax.ShapeDtypeStruct((9,), jnp.int32))
    scratch = (pltpu.VMEM((EDGE * SPAN, LANES), F32), pltpu.VMEM((ROWS * RSPAN, LANES), F32))
    args = (info, partners, offsets, near(two), near(four), near(odd), near(own_box), jnp.asarray(forward_first()))
    return call(start_kernel, 12, [SMEM] * 3 + [VMEM] * 5, shapes, (VMEM,) * 3 + (SMEM,), scratch, args)


def prepare_call(scal, kernel, upper):
    shapes = (
        kept((SLOTS + 1, GRID, LANES), F32),
        kept((PAIRS, 2 * GRID, LANES), BF16),
        kept((PAIRS, GRID, 2 * LANES), BF16),
        kept((PAIRS, GRID, 2 * LANES), BF16),
        kept((PAIRS, 2 * GRID, LANES), BF16),
    )
    args = (scal, kernel, near(upper), jnp.asarray(reversal()), jnp.asarray(COS), jnp.asarray(SIN))
    return call(prepare_kernel, 12, [SMEM] + [VMEM] * 5, shapes, (VMEM,) * 5, (), args)


def wave_call(scal, got, scale, lowest, tables):
    scratch = (
        pltpu.VMEM((PAIRS * SLOTS * ZSPAN, LANES), F32),
        pltpu.VMEM((PAIRS * SLOTS * ZSPAN, LANES), F32),
        pltpu.VMEM((PAIRS * EDGE * BSPAN, LANES), F32),
    )
    args = (scal, near(got), near(scale), near(lowest), *(near(t) for t in tables), jnp.asarray(reversal()))
    return call(wave_kernel, 12, [SMEM] + [VMEM] * 8, far(PACKET, BF16), VMEM, scratch, args)


def ready_call(scal):
    args = (scal, jnp.asarray(backward_last()))
    return call(ready_kernel, 8, [SMEM, VMEM], kept((PAIRS, 2 * GRID, GRID), BF16), VMEM, (), args)


def term_call(scal, got, there, withs, tabs):
    half = (2, ROWS, FLAT, LANES)
    shapes = (far((SLABS, ROWS, FLAT, LANES), BF16), kept(half, BF16), kept(half, BF16))
    scratch = (
        pltpu.VMEM(ROWBOX, F32),
        pltpu.VMEM((PAIRS * ROWS * SPAN, LANES), F32),
        pltpu.VMEM((HALF + EDGE + HALF, FLAT, LANES), F32),
    )
    args = (scal, near(got), there, withs, near(tabs))
    return call(term_kernel, 16, [SMEM] + [VMEM] * 4, shapes, (VMEM,) * 3, scratch, args)


def final_call(odd_core, moved, crossed, two, four):
    scratch = (pltpu.VMEM((ROWS * RSPAN, LANES), F32),)
    shape = jax.ShapeDtypeStruct((ROWS, CELLS), F32)
    args = (odd_core, near(moved), near(crossed), near(two), near(four))
    return call(final_kernel, 8, [SMEM] + [VMEM] * 4, shape, VMEM, scratch, args)


def passed_along(block, distance):
    count = lax.axis_size("orb")
    return lax.ppermute(block, "orb", [((i - distance) % count, i) for i in range(count)])


def other_core(block):
    count = lax.axis_size("orb")
    return lax.ppermute(block, "orb", [(i ^ 1, i) for i in range(count)])


def shared(block):
    return lax.all_to_all(block, "slab", split_axis=0, concat_axis=0, tiled=True)


def per_device(orbitals, partners, offsets, kernel):
    orbit = lax.axis_index("orb").astype(jnp.int32)
    slab = lax.axis_index("slab").astype(jnp.int32)
    even_core = orbit % 2 == 0
    info = jnp.stack([slab, orbit])
    odd_core = (orbit % 2)[None]
    loaded, copies = load_call(offsets, orbitals[0])
    four = passed_along(loaded, -4)
    two = passed_along(loaded, -2)
    own_box = shared(copies)
    upper, lowest = mirror_call(kernel)
    given = jnp.stack([jnp.where(even_core, two, loaded), jnp.where(even_core, four, two)])
    odd = other_core(given)
    upper = lax.ppermute(upper, "slab", [(s, SLABS - 1 - s) for s in range(SLABS)])
    send, there, withs, scal = start_call(info, partners, offsets, two, four, odd, own_box)
    got = shared(send)
    lowest = lax.ppermute(lowest, "slab", [(4, 0), (7, 1), (6, 2), (5, 3)])
    scale, *tables = prepare_call(scal, kernel, upper)
    send = wave_call(scal, got, scale, lowest, tables)
    got = shared(send)
    tabs = ready_call(scal)
    move, odd_out, even_out = term_call(scal, got, there, withs, tabs)
    crossed = other_core(odd_out)
    move = shared(move)
    by_two = even_out[0].astype(F32) + jnp.where(even_core, crossed[0], crossed[1]).astype(F32)
    by_four = even_out[1].astype(F32) + jnp.where(even_core, crossed[1], 0.0).astype(F32)
    four_back = passed_along(by_four.astype(BF16), 4)
    two_back = passed_along(by_two.astype(BF16), 2)
    return final_call(odd_core, move, crossed, two_back, four_back)[None]


def solution(mesh):
    return jax.shard_map(
        per_device,
        mesh=mesh,
        in_specs=(P("orb", "slab", None), P("orb", None), P("orb", None), P(None, "slab", None)),
        out_specs=P("orb", "slab", None),
        check_vma=False,
    )
```

```python
import jax
import jax.numpy as jnp
import numpy as np
from jax import lax
from jax.experimental import pallas as pl
from jax.experimental.pallas import tpu as pltpu
from jax.sharding import PartitionSpec as P


EDGE = 64
GRID = 128
HALF = 32
SLABS = 8
ROWS = EDGE // SLABS
WAVES = GRID // SLABS
PAIRS = 2
LANES = 128
CELLS = EDGE * EDGE
FLAT = CELLS // LANES
PAD = 24
SPAN = PAD + FLAT + PAD + 1
SLOTS = 8
TWIN = 2 * SLOTS
ZSPAN = EDGE + 1
BSPAN = SLOTS + 1
RSPAN = FLAT + 1
F32 = jnp.float32
BF16 = jnp.bfloat16


def full_tables():
    index = np.arange(GRID)
    angle = (index[:, None] * index[None, :] % GRID) * (2.0 * np.pi / GRID)
    rounded = lambda a: a.astype(np.float32).astype(BF16).astype(np.float32)
    return rounded(np.cos(angle)), rounded(np.sin(angle))


COS, SIN = full_tables()
SIGN = COS[:, EDGE]
OWN_WAVES = np.array([[WAVES * s + (s >= SLABS // 2) + q for q in range(SLOTS)] for s in range(SLABS)])


def forward_first():
    waves = OWN_WAVES.reshape(-1)
    im = -SIN[:, waves]
    im[:, 0] = SIGN
    return np.concatenate([COS[:, waves], im], axis=1)


def backward_last():
    c, s = COS.copy(), SIN.copy()
    s[:, 0] = -SIGN
    out = []
    for par in range(2):
        for table in (c, s):
            wide = np.zeros((GRID, SLABS, 2, SLOTS), np.float32)
            wide[:, :, par] = table[:, OWN_WAVES]
            out.append(wide.reshape(GRID, GRID))
    return np.concatenate(out)


def reversal():
    flip = np.zeros((GRID, GRID), np.float32)
    flip[np.arange(GRID), -np.arange(GRID) % GRID] = 1.0
    return flip.astype(BF16)


def dot(a, b):
    return jnp.dot(a, b, preferred_element_type=F32)


def swapped(x):
    return pltpu.roll(x, EDGE, axis=1)


def lanes_of(shape):
    return lax.broadcasted_iota(jnp.int32, shape, 1)


def low_half(shape):
    return lanes_of(shape) < EDGE


def shifted(ref, base, d1, d2):
    flat = d1 * EDGE + d2
    turn = flat & (LANES - 1)
    jump = (flat - turn) // LANES
    here = pltpu.roll(ref[pl.ds(base - jump, FLAT), :], turn, axis=1)
    before = pltpu.roll(ref[pl.ds(base - jump - 1, FLAT), :], turn, axis=1)
    lane = lanes_of((FLAT, LANES))
    depth = (lane & (EDGE - 1)) - d2
    return jnp.where((depth >= 0) & (depth < EDGE), jnp.where(lane >= turn, here, before), 0.0)


def reversed_plane(flip, plane):
    return dot(dot(flip, plane).astype(BF16), flip)


def clear_edges(ref, rows):
    zeros = jnp.zeros((PAD + 1, LANES), F32)
    for c in range(rows):
        ref[c * SPAN : c * SPAN + PAD, :] = zeros[:PAD]
        ref[c * SPAN + PAD + FLAT : (c + 1) * SPAN, :] = zeros


def load_kernel(corner_h, own, loaded, copies, corner, sems):
    mark_load = pltpu.make_async_copy(corner_h, corner, sems.at[SLABS + 1])
    mark_load.start()
    loads = [pltpu.make_async_copy(own, copies.at[t], sems.at[t]) for t in range(SLABS)]
    loads.append(pltpu.make_async_copy(own, loaded.at[:, pl.ds(0, CELLS)], sems.at[SLABS]))
    for one in loads:
        one.start()
    mark_load.wait()
    lane = lanes_of((ROWS, LANES))
    mark = jnp.zeros((ROWS, LANES), F32)
    for k in range(3):
        mark = jnp.where(lane == k, corner[0, k].astype(F32), mark)
    loaded[:, CELLS:] = mark.astype(BF16)
    for one in loads:
        one.wait()


def mirror_kernel(kern, upper, lowest):
    kern_flat = kern.reshape(GRID * WAVES, LANES)
    for q in range(SLOTS):
        upper[q] = kern_flat[pl.ds(SLOTS + q, GRID, stride=WAVES), :].astype(BF16)
    lowest[...] = kern_flat[pl.ds(0, GRID, stride=WAVES), :].astype(BF16)


def start_kernel(info, partners, corner, two, four, odd, own_in, first_t, send, there_out, with_out, scal, own_s, part_s):
    slab, orbit = info[0], info[1]
    clear_edges(own_s, 2 * ROWS)
    scal[0] = slab
    low_d = low_half((FLAT, LANES))
    low_w = low_half((EDGE, LANES))
    lane = lanes_of((ROWS, LANES))
    weight = jnp.where(lane == 0, 1.0, jnp.where(lane == 1, 64.0, jnp.where(lane == 2, 4096.0, 0.0)))
    for n in range(PAIRS):
        hop = (partners[0, n] - orbit) & (EDGE - 1)
        for k in range(FLAT + 1):
            at = slice(k * LANES, (k + 1) * LANES)
            low = jnp.where(hop == 1, odd[0, :, at].astype(F32), two[:, at].astype(F32))
            high = jnp.where(hop == 3, odd[1, :, at].astype(F32), four[:, at].astype(F32))
            value = jnp.where(hop <= 2, low, high)
            if k < FLAT:
                part_s[pl.ds(k, ROWS, stride=RSPAN), :] = value
            else:
                code = jnp.sum(value[:1] * weight[:1]).astype(jnp.int32)
        d0 = (code & 63) - corner[0, 0]
        d1 = ((code >> 6) & 63) - corner[0, 1]
        d2 = (code >> 12) - corner[0, 2]
        scal[1 + 3 * n] = d0
        scal[2 + 3 * n] = d1
        scal[3 + 3 * n] = d2
        scal[7 + n] = hop
        halves = [first_t[pl.ds(HALF + d1 + par, FLAT, stride=2), :] for par in range(2)]
        first = jnp.concatenate(halves, axis=0).T.astype(BF16)
        sides = []
        window = slab + (d0 >> 3)
        for w in range(2):
            t = jnp.clip(window + w, 0, SLABS - 1)
            for k in range(FLAT):
                piece = own_in[t, :, k * LANES : (k + 1) * LANES].astype(F32)
                own_s[pl.ds(w * ROWS * SPAN + PAD + k, ROWS, stride=SPAN), :] = piece
        for r in range(ROWS):
            source = slab * ROWS + r + d0
            inside = jnp.logical_and(source >= 0, source < EDGE)
            base = (r + (d0 & (ROWS - 1))) * SPAN + PAD
            there = jnp.where(inside, shifted(own_s, base, -d1, -d2), 0.0)
            part = part_s[r * RSPAN : r * RSPAN + FLAT, :]
            there_out[n, r] = there.astype(BF16)
            with_out[n, r] = part.astype(BF16)
            sides.append(there * part)
        for quad in range(ROWS // 4):
            columns = []
            for half in range(2):
                a, b = sides[quad * 4 + half * 2], sides[quad * 4 + half * 2 + 1]
                even = jnp.where(low_d, a, swapped(b)).astype(BF16)
                odd_part = jnp.where(low_d, swapped(a), b).astype(BF16)
                columns.append(jnp.concatenate([even, odd_part], axis=0))
            y = dot(first, jnp.concatenate(columns, axis=1))
            for half in range(2):
                re = y[:EDGE, half * LANES : (half + 1) * LANES]
                im = y[EDGE:, half * LANES : (half + 1) * LANES]
                wave_a = jnp.where(low_w, re, swapped(im))
                wave_b = jnp.where(low_w, swapped(re), im)
                for s in range(SLABS):
                    at = slice(s * SLOTS, (s + 1) * SLOTS)
                    both = jnp.concatenate([wave_a[at], wave_b[at]], axis=0)
                    send[s, n, quad * 2 + half] = both.astype(BF16)


def prepare_kernel(scal, kern, upper, flip_t, cos_f, sin_f, scale_out, rowf_out, depf_out, rowb_out, depb_out):
    slab = scal[0]
    flip = flip_t[...]
    kern_flat = kern.reshape(GRID * WAVES, LANES)
    lower = slab < SLABS // 2
    for q in range(SLOTS):
        here = kern_flat[pl.ds(jnp.where(lower, q, q + 1), GRID, stride=WAVES), :]
        if q:
            there = upper[jnp.where(lower, SLOTS - q, SLOTS - 1 - q)]
            scale_out[q] = here + reversed_plane(flip, there)
        else:
            here = here.astype(BF16).astype(F32)
            scale_out[0] = here + jnp.where(lower, 0.0, reversed_plane(flip, upper[SLOTS - 1]))
            scale_out[SLOTS] = here + reversed_plane(flip, here.astype(BF16))
    half = low_half((GRID, LANES))

    def by_wave(shift):
        turn = (GRID - HALF - shift) & (LANES - 1)
        c = pltpu.roll(cos_f[...], turn, axis=1)
        s = pltpu.roll(sin_f[...], turn, axis=1)
        return jnp.where(half, c, swapped(s)).astype(BF16), jnp.where(half, -s, swapped(c)).astype(BF16)

    for n in range(PAIRS):
        d0, d2 = scal[1 + 3 * n], scal[3 + 3 * n]
        rowf_out[n, :GRID, :], rowf_out[n, GRID:, :] = by_wave(d0)
        depb_out[n, :GRID, :], depb_out[n, GRID:, :] = by_wave(d2)
        c, s = (ref[pl.ds(HALF + d0, EDGE), :].astype(BF16) for ref in (cos_f, sin_f))
        rowb_out[n] = jnp.concatenate(
            [jnp.concatenate([c, -s], axis=1), jnp.concatenate([s, c], axis=1)], axis=0
        )
        c, s = (ref[pl.ds(HALF + d2, EDGE), :].astype(BF16) for ref in (cos_f, sin_f))
        depf_out[n] = jnp.concatenate(
            [jnp.concatenate([c, -s], axis=1), jnp.concatenate([s, c], axis=1)], axis=0
        )


def wave_kernel(scal, got, scale_t, lowest, rowf_t, depf_t, rowb_t, depb_t, flip_t, send, zr, zi, back_s):
    slab = scal[0]
    first = slab == 0
    lower = slab < SLABS // 2
    flip = flip_t[...]
    low = lowest[...]
    low_back = reversed_plane(flip, low)
    both = scale_t[SLOTS]
    top = low.astype(F32) + low_back
    bottom = scale_t[0] + jnp.where(lower, low_back, 0.0)
    main = jnp.where(first, 0.25 * (both + top), bottom)
    extra = jnp.where(first, 0.25 * (both - top), 0.0)
    for n in range(PAIRS):
        at_z = n * SLOTS * ZSPAN
        at_b = n * EDGE * BSPAN
        depth_m = depf_t[n]
        rows_m = rowf_t[n]
        for t in range(SLABS):
            block = jnp.concatenate([got[t, n, p] for p in range(ROWS // 2)], axis=0)
            z = dot(block, depth_m)
            for r in range(ROWS):
                part = z[r * SLOTS : (r + 1) * SLOTS]
                zr[pl.ds(at_z + t * ROWS + r, SLOTS, stride=ZSPAN), :] = part[:, :LANES]
                zi[pl.ds(at_z + t * ROWS + r, SLOTS, stride=ZSPAN), :] = part[:, LANES:]

        def plane(w):
            at = slice(at_z + w * ZSPAN, at_z + w * ZSPAN + EDGE)
            return jnp.concatenate([zr[at, :], zi[at, :]], axis=0).astype(BF16)

        for w0 in range(0, SLOTS, 2):
            x = dot(rows_m, jnp.concatenate([plane(w0), plane(w0 + 1)], axis=1))
            weight = jnp.concatenate([scale_t[w0] if w0 else main, scale_t[w0 + 1]], axis=1)
            re, im = x[:GRID] * weight, x[GRID:] * weight
            if w0 == 0:
                edge = x[:, :LANES].astype(BF16)
                back_re = dot(dot(flip, edge[:GRID]).astype(BF16), flip)
                back_im = dot(dot(flip, edge[GRID:]).astype(BF16), flip)
                re = jnp.concatenate([re[:, :LANES] + extra * back_re, re[:, LANES:]], axis=1)
                im = jnp.concatenate([im[:, :LANES] - extra * back_im, im[:, LANES:]], axis=1)
            v = dot(rowb_t[n], jnp.concatenate([re, im], axis=0).astype(BF16)).astype(BF16)
            re, im = v[:EDGE], v[EDGE:]
            left = jnp.concatenate(
                [
                    jnp.concatenate([re[:, :LANES], im[:, :LANES]], axis=1),
                    jnp.concatenate([re[:, LANES:], im[:, LANES:]], axis=1),
                ],
                axis=0,
            )
            r = dot(left, depb_t[n])
            for h in range(2):
                back_s[pl.ds(at_b + w0 + h, EDGE, stride=BSPAN), :] = r[h * EDGE : (h + 1) * EDGE]
        for t in range(SLABS):
            for p in range(ROWS // 2):
                at = at_b + (t * ROWS + 2 * p) * BSPAN
                both = jnp.concatenate([back_s[at : at + SLOTS, :], back_s[at + BSPAN : at + BSPAN + SLOTS, :]], axis=0)
                send[t, n, p] = both.astype(BF16)


def ready_kernel(scal, last_t, tab_out):
    for n in range(PAIRS):
        d1 = scal[2 + 3 * n]
        parts = [
            last_t[pl.ds((2 * row + f) * GRID + HALF + d1 + par, FLAT, stride=2), :]
            for row in range(2)
            for f in range(2)
            for par in range(2)
        ]
        tab_out[n] = jnp.concatenate(parts, axis=0).astype(BF16)


def term_kernel(scal, got, there, withs, tabs, move_out, odd_out, even_out, far_s, own_s, sum_s):
    slab = scal[0]
    low = low_half((FLAT, LANES))
    scale = 1.0 / GRID**3
    clear_edges(own_s, PAIRS * ROWS)
    blank = jnp.zeros((FLAT, LANES), F32)
    for c in range(EDGE):
        sum_s[HALF + c] = blank
    for n in range(PAIRS):
        d0, d1, d2 = scal[1 + 3 * n], scal[2 + 3 * n], scal[3 + 3 * n]
        tab = tabs[n]
        for quad in range(ROWS // 4):
            data = [jnp.concatenate([got[t, n, quad * 2 + h] for t in range(SLABS)], axis=0) for h in range(2)]
            g = dot(tab, jnp.concatenate(data, axis=1))
            for h in range(2):
                for par in range(2):
                    r = quad * 4 + h * 2 + par
                    part = g[par * GRID : (par + 1) * GRID, h * LANES : (h + 1) * LANES]
                    c0, c1, s0, s1 = (part[f * FLAT : (f + 1) * FLAT] for f in range(4))
                    pot = jnp.where(low, c0 - swapped(s0), swapped(c1) - s1) * scale
                    far_s[n, r] = pot * there[n, r].astype(F32)
                    base = (n * ROWS + r) * SPAN + PAD
                    own_s[base : base + FLAT, :] = pot * withs[n, r].astype(F32)
        for r in range(ROWS):
            base = (n * ROWS + r) * SPAN + PAD
            at = HALF + slab * ROWS + r + d0
            sum_s[at] = sum_s[at] + shifted(own_s, base, d1, d2)
    for t in range(SLABS):
        for r in range(ROWS):
            move_out[t, r] = sum_s[HALF + t * ROWS + r].astype(BF16)
    hops = [scal[7 + n] for n in range(PAIRS)]
    for e in range(1, 5):
        target = odd_out if e % 2 else even_out
        for row in range(ROWS):
            value = sum(jnp.where(hops[n] == e, far_s[n, row], 0.0) for n in range(PAIRS))
            target[(e - 1) // 2, row] = value.astype(BF16)


def final_kernel(odd_core, moved, crossed, back, out, total_s):
    keep = odd_core[0] == 1
    for r in range(ROWS):
        total = back[r].astype(F32) + jnp.where(keep, crossed[0, r].astype(F32), 0.0)
        for t in range(SLABS):
            total = total + moved[t, r].astype(F32)
        total_s[r * RSPAN : r * RSPAN + FLAT, :] = total
    for k in range(FLAT):
        out[:, k * LANES : (k + 1) * LANES] = total_s[pl.ds(k, ROWS, stride=RSPAN), :]


VMEM = pl.BlockSpec(memory_space=pltpu.VMEM)
SMEM = pl.BlockSpec(memory_space=pltpu.SMEM)
HBM = pl.BlockSpec(memory_space=pltpu.HBM)


def kept(shape, dtype):
    return pltpu.VMEM(shape, dtype)


def away(x):
    return pltpu.with_memory_space_constraint(x, pltpu.HBM)


def near(x):
    return pltpu.with_memory_space_constraint(x, pltpu.VMEM)


def call(kernel, mib, in_specs, out_shape, out_specs, scratch, args):
    return pl.pallas_call(
        kernel,
        out_shape=out_shape,
        in_specs=in_specs,
        out_specs=out_specs,
        scratch_shapes=scratch,
        interpret=INTERPRET,
        compiler_params=pltpu.CompilerParams(vmem_limit_bytes=mib << 20),
    )(*args)


INTERPRET = False
ROWBOX = (PAIRS, ROWS, FLAT, LANES)
PACKET = (SLABS, PAIRS, ROWS // 2, TWIN, LANES)


def load_call(offsets, own):
    shapes = (kept((ROWS, CELLS + LANES), BF16), kept((SLABS, ROWS, CELLS), BF16))
    scratch = (pltpu.SMEM((1, 3), jnp.int32), pltpu.SemaphoreType.DMA((SLABS + 2,)))
    return call(load_kernel, 8, [HBM, HBM], shapes, (VMEM,) * 2, scratch, (away(offsets), away(own)))


def mirror_call(kernel):
    shapes = (kept((SLOTS, GRID, LANES), BF16), kept((GRID, LANES), BF16))
    return call(mirror_kernel, 8, [VMEM], shapes, (VMEM,) * 2, (), (kernel,))


def start_call(info, partners, offsets, two, four, odd, own_box):
    shapes = (kept(PACKET, BF16), kept(ROWBOX, BF16), kept(ROWBOX, BF16), jax.ShapeDtypeStruct((9,), jnp.int32))
    scratch = (pltpu.VMEM((2 * ROWS * SPAN, LANES), F32), pltpu.VMEM((ROWS * RSPAN, LANES), F32))
    args = (info, partners, offsets, near(two), near(four), near(odd), near(own_box), jnp.asarray(forward_first()))
    return call(start_kernel, 12, [SMEM] * 3 + [VMEM] * 5, shapes, (VMEM,) * 3 + (SMEM,), scratch, args)


def prepare_call(scal, kernel, upper):
    shapes = (
        kept((SLOTS + 1, GRID, LANES), F32),
        kept((PAIRS, 2 * GRID, LANES), BF16),
        kept((PAIRS, GRID, 2 * LANES), BF16),
        kept((PAIRS, GRID, 2 * LANES), BF16),
        kept((PAIRS, 2 * GRID, LANES), BF16),
    )
    args = (scal, kernel, near(upper), jnp.asarray(reversal()), jnp.asarray(COS), jnp.asarray(SIN))
    return call(prepare_kernel, 12, [SMEM] + [VMEM] * 5, shapes, (VMEM,) * 5, (), args)


def wave_call(scal, got, scale, lowest, tables):
    scratch = (
        pltpu.VMEM((PAIRS * SLOTS * ZSPAN, LANES), F32),
        pltpu.VMEM((PAIRS * SLOTS * ZSPAN, LANES), F32),
        pltpu.VMEM((PAIRS * EDGE * BSPAN, LANES), F32),
    )
    args = (scal, near(got), near(scale), near(lowest), *(near(t) for t in tables), jnp.asarray(reversal()))
    return call(wave_kernel, 12, [SMEM] + [VMEM] * 8, kept(PACKET, BF16), VMEM, scratch, args)


def ready_call(scal):
    args = (scal, jnp.asarray(backward_last()))
    return call(ready_kernel, 8, [SMEM, VMEM], kept((PAIRS, 2 * GRID, GRID), BF16), VMEM, (), args)


def term_call(scal, got, there, withs, tabs):
    half = (2, ROWS, FLAT, LANES)
    shapes = (kept((SLABS, ROWS, FLAT, LANES), BF16), kept(half, BF16), kept(half, BF16))
    scratch = (
        pltpu.VMEM(ROWBOX, F32),
        pltpu.VMEM((PAIRS * ROWS * SPAN, LANES), F32),
        pltpu.VMEM((HALF + EDGE + HALF, FLAT, LANES), F32),
    )
    args = (scal, near(got), near(there), near(withs), near(tabs))
    return call(term_kernel, 16, [SMEM] + [VMEM] * 4, shapes, (VMEM,) * 3, scratch, args)


def final_call(odd_core, moved, crossed, back):
    scratch = (pltpu.VMEM((ROWS * RSPAN, LANES), F32),)
    shape = jax.ShapeDtypeStruct((ROWS, CELLS), F32)
    args = (odd_core, near(moved), near(crossed), near(back))
    return call(final_kernel, 8, [SMEM] + [VMEM] * 3, shape, VMEM, scratch, args)


def passed_along(block, distance):
    count = lax.axis_size("orb")
    return lax.ppermute(block, "orb", [((i - distance) % count, i) for i in range(count)])


def other_core(block):
    count = lax.axis_size("orb")
    return lax.ppermute(block, "orb", [(i ^ 1, i) for i in range(count)])


def shared(block):
    return lax.all_to_all(block, "slab", split_axis=0, concat_axis=0, tiled=True)


def per_device(orbitals, partners, offsets, kernel):
    orbit = lax.axis_index("orb").astype(jnp.int32)
    slab = lax.axis_index("slab").astype(jnp.int32)
    even_core = orbit % 2 == 0
    info = jnp.stack([slab, orbit])
    odd_core = (orbit % 2)[None]
    loaded, copies = load_call(offsets, orbitals[0])
    two = passed_along(loaded, -2)
    own_box = shared(copies)
    four = passed_along(two, -2)
    upper, lowest = mirror_call(kernel)
    given = jnp.stack([jnp.where(even_core, two, loaded), jnp.where(even_core, four, two)])
    odd = other_core(given)
    upper = lax.ppermute(upper, "slab", [(s, SLABS - 1 - s) for s in range(SLABS)])
    send, there, withs, scal = start_call(info, partners, offsets, two, four, odd, own_box)
    got = shared(send)
    lowest = lax.ppermute(lowest, "slab", [(4, 0), (7, 1), (6, 2), (5, 3)])
    scale, *tables = prepare_call(scal, kernel, upper)
    send = wave_call(scal, got, scale, lowest, tables)
    got = shared(send)
    tabs = ready_call(scal)
    move, odd_out, even_out = term_call(scal, got, there, withs, tabs)
    crossed = other_core(odd_out)
    move = shared(move)
    by_two = even_out[0].astype(F32) + jnp.where(even_core, crossed[0], crossed[1]).astype(F32)
    by_four = even_out[1].astype(F32) + jnp.where(even_core, crossed[1], 0.0).astype(F32)
    half_way = passed_along(by_four.astype(BF16), 2)
    back = passed_along((by_two + half_way.astype(F32)).astype(BF16), 2)
    return final_call(odd_core, move, crossed, back)[None]


def solution(mesh):
    return jax.shard_map(
        per_device,
        mesh=mesh,
        in_specs=(P("orb", "slab", None), P("orb", None), P("orb", None), P(None, "slab", None)),
        out_specs=P("orb", "slab", None),
        check_vma=False,
    )
```

```python
import jax
import jax.numpy as jnp
import numpy as np
from jax import lax
from jax.experimental import pallas as pl
from jax.experimental.pallas import tpu as pltpu
from jax.sharding import PartitionSpec as P


EDGE = 64
GRID = 128
HALF = 32
SLABS = 8
ROWS = EDGE // SLABS
WAVES = GRID // SLABS
PAIRS = 2
LANES = 128
CELLS = EDGE * EDGE
FLAT = CELLS // LANES
PAD = 24
SPAN = PAD + FLAT + PAD + 1
SLOTS = 8
TWIN = 2 * SLOTS
ZSPAN = EDGE + 1
BSPAN = SLOTS + 1
RSPAN = FLAT + 1
F32 = jnp.float32
BF16 = jnp.bfloat16


def full_tables():
    index = np.arange(GRID)
    angle = (index[:, None] * index[None, :] % GRID) * (2.0 * np.pi / GRID)
    rounded = lambda a: a.astype(np.float32).astype(BF16).astype(np.float32)
    return rounded(np.cos(angle)), rounded(np.sin(angle))


COS, SIN = full_tables()
SIGN = COS[:, EDGE]
OWN_WAVES = np.array([[WAVES * s + (s >= SLABS // 2) + q for q in range(SLOTS)] for s in range(SLABS)])


def forward_first():
    waves = OWN_WAVES.reshape(-1)
    im = -SIN[:, waves]
    im[:, 0] = SIGN
    return np.concatenate([COS[:, waves], im], axis=1)


def backward_last():
    c, s = COS.copy(), SIN.copy()
    s[:, 0] = -SIGN
    out = []
    for par in range(2):
        for table in (c, s):
            wide = np.zeros((GRID, SLABS, 2, SLOTS), np.float32)
            wide[:, :, par] = table[:, OWN_WAVES]
            out.append(wide.reshape(GRID, GRID))
    return np.concatenate(out)


def reversal():
    flip = np.zeros((GRID, GRID), np.float32)
    flip[np.arange(GRID), -np.arange(GRID) % GRID] = 1.0
    return flip.astype(BF16)


def dot(a, b):
    return jnp.dot(a, b, preferred_element_type=F32)


def swapped(x):
    return pltpu.roll(x, EDGE, axis=1)


def lanes_of(shape):
    return lax.broadcasted_iota(jnp.int32, shape, 1)


def low_half(shape):
    return lanes_of(shape) < EDGE


def shifted(ref, base, d1, d2):
    flat = d1 * EDGE + d2
    turn = flat & (LANES - 1)
    jump = (flat - turn) // LANES
    here = pltpu.roll(ref[pl.ds(base - jump, FLAT), :], turn, axis=1)
    before = pltpu.roll(ref[pl.ds(base - jump - 1, FLAT), :], turn, axis=1)
    lane = lanes_of((FLAT, LANES))
    depth = (lane & (EDGE - 1)) - d2
    return jnp.where((depth >= 0) & (depth < EDGE), jnp.where(lane >= turn, here, before), 0.0)


def reversed_plane(flip, plane):
    return dot(dot(flip, plane).astype(BF16), flip)


def clear_edges(ref, rows):
    zeros = jnp.zeros((PAD + 1, LANES), F32)
    for c in range(rows):
        ref[c * SPAN : c * SPAN + PAD, :] = zeros[:PAD]
        ref[c * SPAN + PAD + FLAT : (c + 1) * SPAN, :] = zeros


def load_kernel(corner_h, own, loaded, corner, sems):
    mark_load = pltpu.make_async_copy(corner_h, corner, sems.at[0])
    own_load = pltpu.make_async_copy(own, loaded.at[:, pl.ds(0, CELLS)], sems.at[1])
    mark_load.start()
    own_load.start()
    mark_load.wait()
    lane = lanes_of((ROWS, LANES))
    mark = jnp.zeros((ROWS, LANES), F32)
    for k in range(3):
        mark = jnp.where(lane == k, corner[0, k].astype(F32), mark)
    loaded[:, CELLS:] = mark.astype(BF16)
    own_load.wait()


def spread_kernel(loaded, copies, sems):
    sends = [pltpu.make_async_copy(loaded.at[:, pl.ds(0, CELLS)], copies.at[t], sems.at[t]) for t in range(SLABS)]
    for one in sends:
        one.start()
    for one in sends:
        one.wait()


def mirror_kernel(kern, upper, lowest):
    kern_flat = kern.reshape(GRID * WAVES, LANES)
    for q in range(SLOTS):
        upper[q] = kern_flat[pl.ds(SLOTS + q, GRID, stride=WAVES), :].astype(BF16)
    lowest[...] = kern_flat[pl.ds(0, GRID, stride=WAVES), :].astype(BF16)


def start_kernel(info, partners, corner, two, four, odd, own_in, first_t, send, there_out, with_out, scal, own_s, part_s):
    slab, orbit = info[0], info[1]
    clear_edges(own_s, 2 * ROWS)
    scal[0] = slab
    low_d = low_half((FLAT, LANES))
    low_w = low_half((EDGE, LANES))
    lane = lanes_of((ROWS, LANES))
    weight = jnp.where(lane == 0, 1.0, jnp.where(lane == 1, 64.0, jnp.where(lane == 2, 4096.0, 0.0)))
    for n in range(PAIRS):
        hop = (partners[0, n] - orbit) & (EDGE - 1)
        for k in range(FLAT + 1):
            at = slice(k * LANES, (k + 1) * LANES)
            low = jnp.where(hop == 1, odd[0, :, at].astype(F32), two[:, at].astype(F32))
            high = jnp.where(hop == 3, odd[1, :, at].astype(F32), four[:, at].astype(F32))
            value = jnp.where(hop <= 2, low, high)
            if k < FLAT:
                part_s[pl.ds(k, ROWS, stride=RSPAN), :] = value
            else:
                code = jnp.sum(value[:1] * weight[:1]).astype(jnp.int32)
        d0 = (code & 63) - corner[0, 0]
        d1 = ((code >> 6) & 63) - corner[0, 1]
        d2 = (code >> 12) - corner[0, 2]
        scal[1 + 3 * n] = d0
        scal[2 + 3 * n] = d1
        scal[3 + 3 * n] = d2
        scal[7 + n] = hop
        halves = [first_t[pl.ds(HALF + d1 + par, FLAT, stride=2), :] for par in range(2)]
        first = jnp.concatenate(halves, axis=0).T.astype(BF16)
        window = slab + (d0 >> 3)
        for w in range(2):
            t = jnp.clip(window + w, 0, SLABS - 1)
            for k in range(FLAT):
                piece = own_in[t, :, k * LANES : (k + 1) * LANES].astype(F32)
                own_s[pl.ds(w * ROWS * SPAN + PAD + k, ROWS, stride=SPAN), :] = piece
        for quad in range(ROWS // 4):
            sides = []
            for r in range(quad * 4, quad * 4 + 4):
                source = slab * ROWS + r + d0
                inside = jnp.logical_and(source >= 0, source < EDGE)
                base = (r + (d0 & (ROWS - 1))) * SPAN + PAD
                there = jnp.where(inside, shifted(own_s, base, -d1, -d2), 0.0)
                part = part_s[r * RSPAN : r * RSPAN + FLAT, :]
                there_out[n, r] = there.astype(BF16)
                with_out[n, r] = part.astype(BF16)
                sides.append(there * part)
            columns = []
            for half in range(2):
                a, b = sides[half * 2], sides[half * 2 + 1]
                even = jnp.where(low_d, a, swapped(b)).astype(BF16)
                odd_part = jnp.where(low_d, swapped(a), b).astype(BF16)
                columns.append(jnp.concatenate([even, odd_part], axis=0))
            y = dot(first, jnp.concatenate(columns, axis=1))
            for half in range(2):
                re = y[:EDGE, half * LANES : (half + 1) * LANES]
                im = y[EDGE:, half * LANES : (half + 1) * LANES]
                wave_a = jnp.where(low_w, re, swapped(im))
                wave_b = jnp.where(low_w, swapped(re), im)
                for s in range(SLABS):
                    at = slice(s * SLOTS, (s + 1) * SLOTS)
                    both = jnp.concatenate([wave_a[at], wave_b[at]], axis=0)
                    send[s, n, quad * 2 + half] = both.astype(BF16)


def prepare_kernel(scal, kern, upper, flip_t, cos_f, sin_f, scale_out, rowf_out, depf_out, rowb_out, depb_out):
    slab = scal[0]
    flip = flip_t[...]
    kern_flat = kern.reshape(GRID * WAVES, LANES)
    lower = slab < SLABS // 2
    for q in range(SLOTS):
        here = kern_flat[pl.ds(jnp.where(lower, q, q + 1), GRID, stride=WAVES), :]
        if q:
            there = upper[jnp.where(lower, SLOTS - q, SLOTS - 1 - q)]
            scale_out[q] = here + reversed_plane(flip, there)
        else:
            here = here.astype(BF16).astype(F32)
            scale_out[0] = here + jnp.where(lower, 0.0, reversed_plane(flip, upper[SLOTS - 1]))
            scale_out[SLOTS] = here + reversed_plane(flip, here.astype(BF16))
    half = low_half((GRID, LANES))

    def by_wave(shift):
        turn = (GRID - HALF - shift) & (LANES - 1)
        c = pltpu.roll(cos_f[...], turn, axis=1)
        s = pltpu.roll(sin_f[...], turn, axis=1)
        return jnp.where(half, c, swapped(s)).astype(BF16), jnp.where(half, -s, swapped(c)).astype(BF16)

    for n in range(PAIRS):
        d0, d2 = scal[1 + 3 * n], scal[3 + 3 * n]
        rowf_out[n, :GRID, :], rowf_out[n, GRID:, :] = by_wave(d0)
        depb_out[n, :GRID, :], depb_out[n, GRID:, :] = by_wave(d2)
        c, s = (ref[pl.ds(HALF + d0, EDGE), :].astype(BF16) for ref in (cos_f, sin_f))
        rowb_out[n] = jnp.concatenate(
            [jnp.concatenate([c, -s], axis=1), jnp.concatenate([s, c], axis=1)], axis=0
        )
        c, s = (ref[pl.ds(HALF + d2, EDGE), :].astype(BF16) for ref in (cos_f, sin_f))
        depf_out[n] = jnp.concatenate(
            [jnp.concatenate([c, -s], axis=1), jnp.concatenate([s, c], axis=1)], axis=0
        )


def wave_kernel(scal, got, scale_t, lowest, rowf_t, depf_t, rowb_t, depb_t, flip_t, send, zr, zi, back_s):
    slab = scal[0]
    first = slab == 0
    lower = slab < SLABS // 2
    flip = flip_t[...]
    low = lowest[...]
    low_back = reversed_plane(flip, low)
    both = scale_t[SLOTS]
    top = low.astype(F32) + low_back
    bottom = scale_t[0] + jnp.where(lower, low_back, 0.0)
    main = jnp.where(first, 0.25 * (both + top), bottom)
    extra = jnp.where(first, 0.25 * (both - top), 0.0)
    for n in range(PAIRS):
        at_z = n * SLOTS * ZSPAN
        at_b = n * EDGE * BSPAN
        depth_m = depf_t[n]
        rows_m = rowf_t[n]
        block = jnp.concatenate([got[t, n, p] for t in range(SLABS) for p in range(ROWS // 2)], axis=0)
        z = dot(block, depth_m)
        for c in range(EDGE):
            part = z[c * SLOTS : (c + 1) * SLOTS]
            zr[pl.ds(at_z + c, SLOTS, stride=ZSPAN), :] = part[:, :LANES]
            zi[pl.ds(at_z + c, SLOTS, stride=ZSPAN), :] = part[:, LANES:]

        def plane(w):
            at = slice(at_z + w * ZSPAN, at_z + w * ZSPAN + EDGE)
            return jnp.concatenate([zr[at, :], zi[at, :]], axis=0).astype(BF16)

        lefts = []
        for w0 in range(0, SLOTS, 2):
            x = dot(rows_m, jnp.concatenate([plane(w0), plane(w0 + 1)], axis=1))
            weight = jnp.concatenate([scale_t[w0] if w0 else main, scale_t[w0 + 1]], axis=1)
            re, im = x[:GRID] * weight, x[GRID:] * weight
            if w0 == 0:
                edge = x[:, :LANES].astype(BF16)
                back_re = dot(dot(flip, edge[:GRID]).astype(BF16), flip)
                back_im = dot(dot(flip, edge[GRID:]).astype(BF16), flip)
                re = jnp.concatenate([re[:, :LANES] + extra * back_re, re[:, LANES:]], axis=1)
                im = jnp.concatenate([im[:, :LANES] - extra * back_im, im[:, LANES:]], axis=1)
            v = dot(rowb_t[n], jnp.concatenate([re, im], axis=0).astype(BF16)).astype(BF16)
            re, im = v[:EDGE], v[EDGE:]
            lefts.append(jnp.concatenate([re[:, :LANES], im[:, :LANES]], axis=1))
            lefts.append(jnp.concatenate([re[:, LANES:], im[:, LANES:]], axis=1))
        r = dot(jnp.concatenate(lefts, axis=0), depb_t[n])
        for w in range(SLOTS):
            back_s[pl.ds(at_b + w, EDGE, stride=BSPAN), :] = r[w * EDGE : (w + 1) * EDGE]
        for t in range(SLABS):
            for p in range(ROWS // 2):
                at = at_b + (t * ROWS + 2 * p) * BSPAN
                both = jnp.concatenate([back_s[at : at + SLOTS, :], back_s[at + BSPAN : at + BSPAN + SLOTS, :]], axis=0)
                send[t, n, p] = both.astype(BF16)


def ready_kernel(scal, last_t, tab_out):
    for n in range(PAIRS):
        d1 = scal[2 + 3 * n]
        parts = [
            last_t[pl.ds((2 * row + f) * GRID + HALF + d1 + par, FLAT, stride=2), :]
            for row in range(2)
            for f in range(2)
            for par in range(2)
        ]
        tab_out[n] = jnp.concatenate(parts, axis=0).astype(BF16)


def term_kernel(scal, got, there, withs, tabs, move_out, odd_out, even_out, far_s, own_s, sum_s):
    slab = scal[0]
    low = low_half((FLAT, LANES))
    scale = 1.0 / GRID**3
    clear_edges(own_s, PAIRS * ROWS)
    blank = jnp.zeros((FLAT, LANES), F32)
    for c in range(EDGE):
        sum_s[HALF + c] = blank
    for n in range(PAIRS):
        d0, d1, d2 = scal[1 + 3 * n], scal[2 + 3 * n], scal[3 + 3 * n]
        tab = tabs[n]
        for p in range(ROWS // 2):
            g = dot(tab, jnp.concatenate([got[t, n, p] for t in range(SLABS)], axis=0))
            for par in range(2):
                r = p * 2 + par
                c0, c1, s0, s1 = (g[par * GRID + f * FLAT : par * GRID + (f + 1) * FLAT] for f in range(4))
                pot = jnp.where(low, c0 - swapped(s0), swapped(c1) - s1) * scale
                far_s[n, r] = pot * there[n, r].astype(F32)
                base = (n * ROWS + r) * SPAN + PAD
                own_s[base : base + FLAT, :] = pot * withs[n, r].astype(F32)
        for r in range(ROWS):
            base = (n * ROWS + r) * SPAN + PAD
            at = HALF + slab * ROWS + r + d0
            sum_s[at] = sum_s[at] + shifted(own_s, base, d1, d2)
    for c in range(EDGE):
        move_out[c] = sum_s[HALF + c].astype(BF16)
    hops = [scal[7 + n] for n in range(PAIRS)]
    for e in range(1, 5):
        target = odd_out if e % 2 else even_out
        for row in range(ROWS):
            value = sum(jnp.where(hops[n] == e, far_s[n, row], 0.0) for n in range(PAIRS))
            target[(e - 1) // 2, row] = value.astype(BF16)


def final_kernel(odd_core, moved, crossed, two, four, out, total_s):
    keep = odd_core[0] == 1
    for r in range(ROWS):
        total = two[r].astype(F32) + four[r].astype(F32) + jnp.where(keep, crossed[0, r].astype(F32), 0.0)
        for t in range(SLABS):
            total = total + moved[t, r].astype(F32)
        total_s[r * RSPAN : r * RSPAN + FLAT, :] = total
    for k in range(FLAT):
        out[:, k * LANES : (k + 1) * LANES] = total_s[pl.ds(k, ROWS, stride=RSPAN), :]


VMEM = pl.BlockSpec(memory_space=pltpu.VMEM)
SMEM = pl.BlockSpec(memory_space=pltpu.SMEM)
HBM = pl.BlockSpec(memory_space=pltpu.HBM)


def kept(shape, dtype):
    return pltpu.VMEM(shape, dtype)


def far(shape, dtype):
    return pltpu.HBM(shape, dtype)


def away(x):
    return pltpu.with_memory_space_constraint(x, pltpu.HBM)


def near(x):
    return pltpu.with_memory_space_constraint(x, pltpu.VMEM)


def call(kernel, mib, in_specs, out_shape, out_specs, scratch, args):
    return pl.pallas_call(
        kernel,
        out_shape=out_shape,
        in_specs=in_specs,
        out_specs=out_specs,
        scratch_shapes=scratch,
        interpret=INTERPRET,
        compiler_params=pltpu.CompilerParams(vmem_limit_bytes=mib << 20),
    )(*args)


INTERPRET = False
ROWBOX = (PAIRS, ROWS, FLAT, LANES)
PACKET = (SLABS, PAIRS, ROWS // 2, TWIN, LANES)


def load_call(offsets, own):
    scratch = (pltpu.SMEM((1, 3), jnp.int32), pltpu.SemaphoreType.DMA((2,)))
    shape = kept((ROWS, CELLS + LANES), BF16)
    return call(load_kernel, 8, [HBM, HBM], shape, VMEM, scratch, (away(offsets), away(own)))


def spread_call(loaded):
    scratch = (pltpu.SemaphoreType.DMA((SLABS,)),)
    shape = far((SLABS, ROWS, CELLS), BF16)
    return call(spread_kernel, 8, [VMEM], shape, HBM, scratch, (near(loaded),))


def mirror_call(kernel):
    shapes = (kept((SLOTS, GRID, LANES), BF16), kept((GRID, LANES), BF16))
    return call(mirror_kernel, 8, [VMEM], shapes, (VMEM,) * 2, (), (kernel,))


def start_call(info, partners, offsets, two, four, odd, own_box):
    shapes = (kept(PACKET, BF16), kept(ROWBOX, BF16), kept(ROWBOX, BF16), jax.ShapeDtypeStruct((9,), jnp.int32))
    scratch = (pltpu.VMEM((2 * ROWS * SPAN, LANES), F32), pltpu.VMEM((ROWS * RSPAN, LANES), F32))
    args = (info, partners, offsets, near(two), near(four), near(odd), near(own_box), jnp.asarray(forward_first()))
    return call(start_kernel, 12, [SMEM] * 3 + [VMEM] * 5, shapes, (VMEM,) * 3 + (SMEM,), scratch, args)


def prepare_call(scal, kernel, upper):
    shapes = (
        kept((SLOTS + 1, GRID, LANES), F32),
        kept((PAIRS, 2 * GRID, LANES), BF16),
        kept((PAIRS, GRID, 2 * LANES), BF16),
        kept((PAIRS, GRID, 2 * LANES), BF16),
        kept((PAIRS, 2 * GRID, LANES), BF16),
    )
    args = (scal, kernel, near(upper), jnp.asarray(reversal()), jnp.asarray(COS), jnp.asarray(SIN))
    return call(prepare_kernel, 12, [SMEM] + [VMEM] * 5, shapes, (VMEM,) * 5, (), args)


def wave_call(scal, got, scale, lowest, tables):
    scratch = (
        pltpu.VMEM((PAIRS * SLOTS * ZSPAN, LANES), F32),
        pltpu.VMEM((PAIRS * SLOTS * ZSPAN, LANES), F32),
        pltpu.VMEM((PAIRS * EDGE * BSPAN, LANES), F32),
    )
    args = (scal, near(got), near(scale), near(lowest), *(near(t) for t in tables), jnp.asarray(reversal()))
    return call(wave_kernel, 12, [SMEM] + [VMEM] * 8, kept(PACKET, BF16), VMEM, scratch, args)


def ready_call(scal):
    args = (scal, jnp.asarray(backward_last()))
    return call(ready_kernel, 8, [SMEM, VMEM], kept((PAIRS, 2 * GRID, GRID), BF16), VMEM, (), args)


def term_call(scal, got, there, withs, tabs):
    half = (2, ROWS, FLAT, LANES)
    shapes = (kept((EDGE, FLAT, LANES), BF16), kept(half, BF16), kept(half, BF16))
    scratch = (
        pltpu.VMEM(ROWBOX, F32),
        pltpu.VMEM((PAIRS * ROWS * SPAN, LANES), F32),
        pltpu.VMEM((HALF + EDGE + HALF, FLAT, LANES), F32),
    )
    args = (scal, near(got), near(there), near(withs), near(tabs))
    return call(term_kernel, 16, [SMEM] + [VMEM] * 4, shapes, (VMEM,) * 3, scratch, args)


def final_call(odd_core, moved, crossed, two, four):
    scratch = (pltpu.VMEM((ROWS * RSPAN, LANES), F32),)
    shape = jax.ShapeDtypeStruct((ROWS, CELLS), F32)
    args = (odd_core, near(moved), near(crossed), near(two), near(four))
    return call(final_kernel, 8, [SMEM] + [VMEM] * 4, shape, VMEM, scratch, args)


def passed_along(block, distance):
    count = lax.axis_size("orb")
    return lax.ppermute(block, "orb", [((i - distance) % count, i) for i in range(count)])


def other_core(block):
    count = lax.axis_size("orb")
    return lax.ppermute(block, "orb", [(i ^ 1, i) for i in range(count)])


def shared(block):
    return lax.all_to_all(block, "slab", split_axis=0, concat_axis=0, tiled=True)


def per_device(orbitals, partners, offsets, kernel):
    orbit = lax.axis_index("orb").astype(jnp.int32)
    slab = lax.axis_index("slab").astype(jnp.int32)
    even_core = orbit % 2 == 0
    info = jnp.stack([slab, orbit])
    odd_core = (orbit % 2)[None]
    loaded = load_call(offsets, orbitals[0])
    four = passed_along(loaded, -4)
    two = passed_along(loaded, -2)
    copies = spread_call(loaded)
    own_box = shared(copies)
    upper, lowest = mirror_call(kernel)
    given = jnp.stack([jnp.where(even_core, two, loaded), jnp.where(even_core, four, two)])
    odd = other_core(given)
    upper = lax.ppermute(upper, "slab", [(s, SLABS - 1 - s) for s in range(SLABS)])
    send, there, withs, scal = start_call(info, partners, offsets, two, four, odd, own_box)
    got = shared(send)
    lowest = lax.ppermute(lowest, "slab", [(4, 0), (7, 1), (6, 2), (5, 3)])
    scale, *tables = prepare_call(scal, kernel, upper)
    send = wave_call(scal, got, scale, lowest, tables)
    got = shared(send)
    tabs = ready_call(scal)
    move, odd_out, even_out = term_call(scal, got, there, withs, tabs)
    crossed = other_core(odd_out)
    move = shared(move.reshape(SLABS, ROWS, FLAT, LANES))
    by_two = even_out[0].astype(F32) + jnp.where(even_core, crossed[0], crossed[1]).astype(F32)
    by_four = even_out[1].astype(F32) + jnp.where(even_core, crossed[1], 0.0).astype(F32)
    four_back = passed_along(by_four.astype(BF16), 4)
    two_back = passed_along(by_two.astype(BF16), 2)
    return final_call(odd_core, move, crossed, two_back, four_back)[None]


def solution(mesh):
    return jax.shard_map(
        per_device,
        mesh=mesh,
        in_specs=(P("orb", "slab", None), P("orb", None), P("orb", None), P(None, "slab", None)),
        out_specs=P("orb", "slab", None),
        check_vma=False,
    )
```

```python
import jax
import jax.numpy as jnp
import numpy as np
from jax import lax
from jax.experimental import pallas as pl
from jax.experimental.pallas import tpu as pltpu
from jax.sharding import PartitionSpec as P


EDGE = 64
GRID = 128
HALF = 32
SLABS = 8
ROWS = EDGE // SLABS
WAVES = GRID // SLABS
PAIRS = 2
LANES = 128
CELLS = EDGE * EDGE
FLAT = CELLS // LANES
PAD = 24
SPAN = PAD + FLAT + PAD + 1
SLOTS = 8
TWIN = 2 * SLOTS
ZSPAN = EDGE + 1
BSPAN = SLOTS + 1
RSPAN = FLAT + 1
F32 = jnp.float32
BF16 = jnp.bfloat16


def full_tables():
    index = np.arange(GRID)
    angle = (index[:, None] * index[None, :] % GRID) * (2.0 * np.pi / GRID)
    rounded = lambda a: a.astype(np.float32).astype(BF16).astype(np.float32)
    return rounded(np.cos(angle)), rounded(np.sin(angle))


COS, SIN = full_tables()
SIGN = COS[:, EDGE]
OWN_WAVES = np.array([[WAVES * s + (s >= SLABS // 2) + q for q in range(SLOTS)] for s in range(SLABS)])


def forward_first():
    waves = OWN_WAVES.reshape(-1)
    im = -SIN[:, waves]
    im[:, 0] = SIGN
    return np.concatenate([COS[:, waves], im], axis=1)


def backward_last():
    c, s = COS.copy(), SIN.copy()
    s[:, 0] = -SIGN
    out = []
    for par in range(2):
        for table in (c, s):
            wide = np.zeros((GRID, SLABS, 2, SLOTS), np.float32)
            wide[:, :, par] = table[:, OWN_WAVES]
            out.append(wide.reshape(GRID, GRID))
    return np.concatenate(out)


def reversal():
    flip = np.zeros((GRID, GRID), np.float32)
    flip[np.arange(GRID), -np.arange(GRID) % GRID] = 1.0
    return flip.astype(BF16)


def dot(a, b):
    return jnp.dot(a, b, preferred_element_type=F32)


def swapped(x):
    return pltpu.roll(x, EDGE, axis=1)


def lanes_of(shape):
    return lax.broadcasted_iota(jnp.int32, shape, 1)


def low_half(shape):
    return lanes_of(shape) < EDGE


def shifted(ref, base, d1, d2):
    flat = d1 * EDGE + d2
    turn = flat & (LANES - 1)
    jump = (flat - turn) // LANES
    here = pltpu.roll(ref[pl.ds(base - jump, FLAT), :], turn, axis=1)
    before = pltpu.roll(ref[pl.ds(base - jump - 1, FLAT), :], turn, axis=1)
    lane = lanes_of((FLAT, LANES))
    depth = (lane & (EDGE - 1)) - d2
    return jnp.where((depth >= 0) & (depth < EDGE), jnp.where(lane >= turn, here, before), 0.0)


def reversed_plane(flip, plane):
    return dot(dot(flip, plane).astype(BF16), flip)


def clear_edges(ref, rows):
    zeros = jnp.zeros((PAD + 1, LANES), F32)
    for c in range(rows):
        ref[c * SPAN : c * SPAN + PAD, :] = zeros[:PAD]
        ref[c * SPAN + PAD + FLAT : (c + 1) * SPAN, :] = zeros


def load_kernel(corner_h, own, loaded, corner, sems):
    mark_load = pltpu.make_async_copy(corner_h, corner, sems.at[0])
    own_load = pltpu.make_async_copy(own, loaded.at[:, pl.ds(0, CELLS)], sems.at[1])
    mark_load.start()
    own_load.start()
    mark_load.wait()
    lane = lanes_of((ROWS, LANES))
    mark = jnp.zeros((ROWS, LANES), F32)
    for k in range(3):
        mark = jnp.where(lane == k, corner[0, k].astype(F32), mark)
    loaded[:, CELLS:] = mark.astype(BF16)
    own_load.wait()


def spread_kernel(loaded, copies, sems):
    sends = [pltpu.make_async_copy(loaded.at[:, pl.ds(0, CELLS)], copies.at[t], sems.at[t]) for t in range(SLABS)]
    for one in sends:
        one.start()
    for one in sends:
        one.wait()


def mirror_kernel(kern, upper, lowest):
    kern_flat = kern.reshape(GRID * WAVES, LANES)
    for q in range(SLOTS):
        upper[q] = kern_flat[pl.ds(SLOTS + q, GRID, stride=WAVES), :].astype(BF16)
    lowest[...] = kern_flat[pl.ds(0, GRID, stride=WAVES), :].astype(BF16)


def start_kernel(info, partners, corner, two, four, odd, own_in, first_t, send, there_out, with_out, scal, own_s, part_s):
    slab, orbit = info[0], info[1]
    clear_edges(own_s, 2 * ROWS)
    scal[0] = slab
    low_d = low_half((FLAT, LANES))
    low_w = low_half((EDGE, LANES))
    lane = lanes_of((ROWS, LANES))
    weight = jnp.where(lane == 0, 1.0, jnp.where(lane == 1, 64.0, jnp.where(lane == 2, 4096.0, 0.0)))
    for n in range(PAIRS):
        hop = (partners[0, n] - orbit) & (EDGE - 1)
        for k in range(FLAT + 1):
            at = slice(k * LANES, (k + 1) * LANES)
            low = jnp.where(hop == 1, odd[0, :, at].astype(F32), two[:, at].astype(F32))
            high = jnp.where(hop == 3, odd[1, :, at].astype(F32), four[:, at].astype(F32))
            value = jnp.where(hop <= 2, low, high)
            if k < FLAT:
                part_s[pl.ds(k, ROWS, stride=RSPAN), :] = value
            else:
                code = jnp.sum(value[:1] * weight[:1]).astype(jnp.int32)
        d0 = (code & 63) - corner[0, 0]
        d1 = ((code >> 6) & 63) - corner[0, 1]
        d2 = (code >> 12) - corner[0, 2]
        scal[1 + 3 * n] = d0
        scal[2 + 3 * n] = d1
        scal[3 + 3 * n] = d2
        scal[7 + n] = hop
        halves = [first_t[pl.ds(HALF + d1 + par, FLAT, stride=2), :] for par in range(2)]
        first = jnp.concatenate(halves, axis=0).T.astype(BF16)
        window = slab + (d0 >> 3)
        for w in range(2):
            t = jnp.clip(window + w, 0, SLABS - 1)
            for k in range(FLAT):
                piece = own_in[t, :, k * LANES : (k + 1) * LANES].astype(F32)
                own_s[pl.ds(w * ROWS * SPAN + PAD + k, ROWS, stride=SPAN), :] = piece
        for quad in range(ROWS // 4):
            sides = []
            for r in range(quad * 4, quad * 4 + 4):
                source = slab * ROWS + r + d0
                inside = jnp.logical_and(source >= 0, source < EDGE)
                base = (r + (d0 & (ROWS - 1))) * SPAN + PAD
                there = jnp.where(inside, shifted(own_s, base, -d1, -d2), 0.0)
                part = part_s[r * RSPAN : r * RSPAN + FLAT, :]
                there_out[n, r] = there.astype(BF16)
                with_out[n, r] = part.astype(BF16)
                sides.append(there * part)
            columns = []
            for half in range(2):
                a, b = sides[half * 2], sides[half * 2 + 1]
                even = jnp.where(low_d, a, swapped(b)).astype(BF16)
                odd_part = jnp.where(low_d, swapped(a), b).astype(BF16)
                columns.append(jnp.concatenate([even, odd_part], axis=0))
            y = dot(first, jnp.concatenate(columns, axis=1))
            for half in range(2):
                re = y[:EDGE, half * LANES : (half + 1) * LANES]
                im = y[EDGE:, half * LANES : (half + 1) * LANES]
                wave_a = jnp.where(low_w, re, swapped(im))
                wave_b = jnp.where(low_w, swapped(re), im)
                for s in range(SLABS):
                    at = slice(s * SLOTS, (s + 1) * SLOTS)
                    both = jnp.concatenate([wave_a[at], wave_b[at]], axis=0)
                    send[s, n, quad * 2 + half] = both.astype(BF16)


def prepare_kernel(scal, kern, upper, flip_t, cos_f, sin_f, scale_out, rowf_out, depf_out, rowb_out, depb_out):
    slab = scal[0]
    flip = flip_t[...]
    kern_flat = kern.reshape(GRID * WAVES, LANES)
    lower = slab < SLABS // 2
    for q in range(SLOTS):
        here = kern_flat[pl.ds(jnp.where(lower, q, q + 1), GRID, stride=WAVES), :]
        if q:
            there = upper[jnp.where(lower, SLOTS - q, SLOTS - 1 - q)]
            scale_out[q] = here + reversed_plane(flip, there)
        else:
            here = here.astype(BF16).astype(F32)
            scale_out[0] = here + jnp.where(lower, 0.0, reversed_plane(flip, upper[SLOTS - 1]))
            scale_out[SLOTS] = here + reversed_plane(flip, here.astype(BF16))
    half = low_half((GRID, LANES))

    def by_wave(shift):
        turn = (GRID - HALF - shift) & (LANES - 1)
        c = pltpu.roll(cos_f[...], turn, axis=1)
        s = pltpu.roll(sin_f[...], turn, axis=1)
        return jnp.where(half, c, swapped(s)).astype(BF16), jnp.where(half, -s, swapped(c)).astype(BF16)

    for n in range(PAIRS):
        d0, d2 = scal[1 + 3 * n], scal[3 + 3 * n]
        rowf_out[n, :GRID, :], rowf_out[n, GRID:, :] = by_wave(d0)
        depb_out[n, :GRID, :], depb_out[n, GRID:, :] = by_wave(d2)
        c, s = (ref[pl.ds(HALF + d0, EDGE), :].astype(BF16) for ref in (cos_f, sin_f))
        rowb_out[n] = jnp.concatenate(
            [jnp.concatenate([c, -s], axis=1), jnp.concatenate([s, c], axis=1)], axis=0
        )
        c, s = (ref[pl.ds(HALF + d2, EDGE), :].astype(BF16) for ref in (cos_f, sin_f))
        depf_out[n] = jnp.concatenate(
            [jnp.concatenate([c, -s], axis=1), jnp.concatenate([s, c], axis=1)], axis=0
        )


def wave_kernel(scal, got, scale_t, lowest, rowf_t, depf_t, rowb_t, depb_t, flip_t, send, zr, zi, back_s):
    slab = scal[0]
    first = slab == 0
    lower = slab < SLABS // 2
    flip = flip_t[...]
    low = lowest[...]
    low_back = reversed_plane(flip, low)
    both = scale_t[SLOTS]
    top = low.astype(F32) + low_back
    bottom = scale_t[0] + jnp.where(lower, low_back, 0.0)
    main = jnp.where(first, 0.25 * (both + top), bottom)
    extra = jnp.where(first, 0.25 * (both - top), 0.0)
    for n in range(PAIRS):
        at_z = n * SLOTS * ZSPAN
        at_b = n * EDGE * BSPAN
        depth_m = depf_t[n]
        rows_m = rowf_t[n]
        block = jnp.concatenate([got[t, n, p] for t in range(SLABS) for p in range(ROWS // 2)], axis=0)
        z = dot(block, depth_m)
        for c in range(EDGE):
            part = z[c * SLOTS : (c + 1) * SLOTS]
            zr[pl.ds(at_z + c, SLOTS, stride=ZSPAN), :] = part[:, :LANES]
            zi[pl.ds(at_z + c, SLOTS, stride=ZSPAN), :] = part[:, LANES:]

        def plane(w):
            at = slice(at_z + w * ZSPAN, at_z + w * ZSPAN + EDGE)
            return jnp.concatenate([zr[at, :], zi[at, :]], axis=0).astype(BF16)

        lefts = []
        for w0 in range(0, SLOTS, 2):
            x = dot(rows_m, jnp.concatenate([plane(w0), plane(w0 + 1)], axis=1))
            weight = jnp.concatenate([scale_t[w0] if w0 else main, scale_t[w0 + 1]], axis=1)
            re, im = x[:GRID] * weight, x[GRID:] * weight
            if w0 == 0:
                edge = x[:, :LANES].astype(BF16)
                turned = dot(flip, jnp.concatenate([edge[:GRID], edge[GRID:]], axis=1)).astype(BF16)
                turned = dot(jnp.concatenate([turned[:, :LANES], turned[:, LANES:]], axis=0), flip)
                back_re, back_im = turned[:GRID], turned[GRID:]
                re = jnp.concatenate([re[:, :LANES] + extra * back_re, re[:, LANES:]], axis=1)
                im = jnp.concatenate([im[:, :LANES] - extra * back_im, im[:, LANES:]], axis=1)
            v = dot(rowb_t[n], jnp.concatenate([re, im], axis=0).astype(BF16)).astype(BF16)
            re, im = v[:EDGE], v[EDGE:]
            lefts.append(jnp.concatenate([re[:, :LANES], im[:, :LANES]], axis=1))
            lefts.append(jnp.concatenate([re[:, LANES:], im[:, LANES:]], axis=1))
        r = dot(jnp.concatenate(lefts, axis=0), depb_t[n])
        for w in range(SLOTS):
            back_s[pl.ds(at_b + w, EDGE, stride=BSPAN), :] = r[w * EDGE : (w + 1) * EDGE]
        for t in range(SLABS):
            for p in range(ROWS // 2):
                at = at_b + (t * ROWS + 2 * p) * BSPAN
                both = jnp.concatenate([back_s[at : at + SLOTS, :], back_s[at + BSPAN : at + BSPAN + SLOTS, :]], axis=0)
                send[t, n, p] = both.astype(BF16)


def ready_kernel(scal, last_t, tab_out):
    for n in range(PAIRS):
        d1 = scal[2 + 3 * n]
        parts = [
            last_t[pl.ds((2 * row + f) * GRID + HALF + d1 + par, FLAT, stride=2), :]
            for row in range(2)
            for f in range(2)
            for par in range(2)
        ]
        tab_out[n] = jnp.concatenate(parts, axis=0).astype(BF16)


def term_kernel(scal, got, there, withs, tabs, move_out, odd_out, even_out, far_s, own_s, sum_s):
    slab = scal[0]
    low = low_half((FLAT, LANES))
    scale = 1.0 / GRID**3
    clear_edges(own_s, PAIRS * ROWS)
    blank = jnp.zeros((FLAT, LANES), F32)
    for c in range(EDGE):
        sum_s[HALF + c] = blank
    for n in range(PAIRS):
        d0, d1, d2 = scal[1 + 3 * n], scal[2 + 3 * n], scal[3 + 3 * n]
        tab = tabs[n]
        for p in range(ROWS // 2):
            g = dot(tab, jnp.concatenate([got[t, n, p] for t in range(SLABS)], axis=0))
            for par in range(2):
                r = p * 2 + par
                c0, c1, s0, s1 = (g[par * GRID + f * FLAT : par * GRID + (f + 1) * FLAT] for f in range(4))
                pot = jnp.where(low, c0 - swapped(s0), swapped(c1) - s1) * scale
                far_s[n, r] = pot * there[n, r].astype(F32)
                base = (n * ROWS + r) * SPAN + PAD
                own_s[base : base + FLAT, :] = pot * withs[n, r].astype(F32)
        for r in range(ROWS):
            base = (n * ROWS + r) * SPAN + PAD
            at = HALF + slab * ROWS + r + d0
            sum_s[at] = sum_s[at] + shifted(own_s, base, d1, d2)
    for c in range(EDGE):
        move_out[c] = sum_s[HALF + c].astype(BF16)
    hops = [scal[7 + n] for n in range(PAIRS)]
    for e in range(1, 5):
        target = odd_out if e % 2 else even_out
        for row in range(ROWS):
            value = sum(jnp.where(hops[n] == e, far_s[n, row], 0.0) for n in range(PAIRS))
            target[(e - 1) // 2, row] = value.astype(BF16)


def final_kernel(odd_core, moved, crossed, two, four, out, total_s):
    keep = odd_core[0] == 1
    for r in range(ROWS):
        total = two[r].astype(F32) + four[r].astype(F32) + jnp.where(keep, crossed[0, r].astype(F32), 0.0)
        for t in range(SLABS):
            total = total + moved[t, r].astype(F32)
        total_s[r * RSPAN : r * RSPAN + FLAT, :] = total
    for k in range(FLAT):
        out[:, k * LANES : (k + 1) * LANES] = total_s[pl.ds(k, ROWS, stride=RSPAN), :]


VMEM = pl.BlockSpec(memory_space=pltpu.VMEM)
SMEM = pl.BlockSpec(memory_space=pltpu.SMEM)
HBM = pl.BlockSpec(memory_space=pltpu.HBM)


def kept(shape, dtype):
    return pltpu.VMEM(shape, dtype)


def far(shape, dtype):
    return pltpu.HBM(shape, dtype)


def away(x):
    return pltpu.with_memory_space_constraint(x, pltpu.HBM)


def near(x):
    return pltpu.with_memory_space_constraint(x, pltpu.VMEM)


def call(kernel, mib, in_specs, out_shape, out_specs, scratch, args):
    return pl.pallas_call(
        kernel,
        out_shape=out_shape,
        in_specs=in_specs,
        out_specs=out_specs,
        scratch_shapes=scratch,
        interpret=INTERPRET,
        compiler_params=pltpu.CompilerParams(vmem_limit_bytes=mib << 20),
    )(*args)


INTERPRET = False
ROWBOX = (PAIRS, ROWS, FLAT, LANES)
PACKET = (SLABS, PAIRS, ROWS // 2, TWIN, LANES)


def load_call(offsets, own):
    scratch = (pltpu.SMEM((1, 3), jnp.int32), pltpu.SemaphoreType.DMA((2,)))
    shape = kept((ROWS, CELLS + LANES), BF16)
    return call(load_kernel, 8, [HBM, HBM], shape, VMEM, scratch, (away(offsets), away(own)))


def spread_call(loaded):
    scratch = (pltpu.SemaphoreType.DMA((SLABS,)),)
    shape = far((SLABS, ROWS, CELLS), BF16)
    return call(spread_kernel, 8, [VMEM], shape, HBM, scratch, (near(loaded),))


def mirror_call(kernel):
    shapes = (kept((SLOTS, GRID, LANES), BF16), kept((GRID, LANES), BF16))
    return call(mirror_kernel, 8, [VMEM], shapes, (VMEM,) * 2, (), (kernel,))


def start_call(info, partners, offsets, two, four, odd, own_box):
    shapes = (kept(PACKET, BF16), kept(ROWBOX, BF16), kept(ROWBOX, BF16), jax.ShapeDtypeStruct((9,), jnp.int32))
    scratch = (pltpu.VMEM((2 * ROWS * SPAN, LANES), F32), pltpu.VMEM((ROWS * RSPAN, LANES), F32))
    args = (info, partners, offsets, near(two), near(four), near(odd), near(own_box), jnp.asarray(forward_first()))
    return call(start_kernel, 12, [SMEM] * 3 + [VMEM] * 5, shapes, (VMEM,) * 3 + (SMEM,), scratch, args)


def prepare_call(scal, kernel, upper):
    shapes = (
        kept((SLOTS + 1, GRID, LANES), F32),
        kept((PAIRS, 2 * GRID, LANES), BF16),
        kept((PAIRS, GRID, 2 * LANES), BF16),
        kept((PAIRS, GRID, 2 * LANES), BF16),
        kept((PAIRS, 2 * GRID, LANES), BF16),
    )
    args = (scal, kernel, near(upper), jnp.asarray(reversal()), jnp.asarray(COS), jnp.asarray(SIN))
    return call(prepare_kernel, 12, [SMEM] + [VMEM] * 5, shapes, (VMEM,) * 5, (), args)


def wave_call(scal, got, scale, lowest, tables):
    scratch = (
        pltpu.VMEM((PAIRS * SLOTS * ZSPAN, LANES), F32),
        pltpu.VMEM((PAIRS * SLOTS * ZSPAN, LANES), F32),
        pltpu.VMEM((PAIRS * EDGE * BSPAN, LANES), F32),
    )
    args = (scal, near(got), near(scale), near(lowest), *(near(t) for t in tables), jnp.asarray(reversal()))
    return call(wave_kernel, 12, [SMEM] + [VMEM] * 8, kept(PACKET, BF16), VMEM, scratch, args)


def ready_call(scal):
    args = (scal, jnp.asarray(backward_last()))
    return call(ready_kernel, 8, [SMEM, VMEM], kept((PAIRS, 2 * GRID, GRID), BF16), VMEM, (), args)


def term_call(scal, got, there, withs, tabs):
    half = (2, ROWS, FLAT, LANES)
    shapes = (kept((EDGE, FLAT, LANES), BF16), kept(half, BF16), kept(half, BF16))
    scratch = (
        pltpu.VMEM(ROWBOX, F32),
        pltpu.VMEM((PAIRS * ROWS * SPAN, LANES), F32),
        pltpu.VMEM((HALF + EDGE + HALF, FLAT, LANES), F32),
    )
    args = (scal, near(got), near(there), near(withs), near(tabs))
    return call(term_kernel, 16, [SMEM] + [VMEM] * 4, shapes, (VMEM,) * 3, scratch, args)


def final_call(odd_core, moved, crossed, two, four):
    scratch = (pltpu.VMEM((ROWS * RSPAN, LANES), F32),)
    shape = jax.ShapeDtypeStruct((ROWS, CELLS), F32)
    args = (odd_core, near(moved), near(crossed), near(two), near(four))
    return call(final_kernel, 8, [SMEM] + [VMEM] * 4, shape, VMEM, scratch, args)


def passed_along(block, distance):
    count = lax.axis_size("orb")
    return lax.ppermute(block, "orb", [((i - distance) % count, i) for i in range(count)])


def other_core(block):
    count = lax.axis_size("orb")
    return lax.ppermute(block, "orb", [(i ^ 1, i) for i in range(count)])


def shared(block):
    return lax.all_to_all(block, "slab", split_axis=0, concat_axis=0, tiled=True)


def per_device(orbitals, partners, offsets, kernel):
    orbit = lax.axis_index("orb").astype(jnp.int32)
    slab = lax.axis_index("slab").astype(jnp.int32)
    even_core = orbit % 2 == 0
    info = jnp.stack([slab, orbit])
    odd_core = (orbit % 2)[None]
    loaded = load_call(offsets, orbitals[0])
    four = passed_along(loaded, -4)
    two = passed_along(loaded, -2)
    copies = spread_call(loaded)
    own_box = shared(copies)
    upper, lowest = mirror_call(kernel)
    given = jnp.stack([jnp.where(even_core, two, loaded), jnp.where(even_core, four, two)])
    odd = other_core(given)
    upper = lax.ppermute(upper, "slab", [(s, SLABS - 1 - s) for s in range(SLABS)])
    send, there, withs, scal = start_call(info, partners, offsets, two, four, odd, own_box)
    got = shared(send)
    lowest = lax.ppermute(lowest, "slab", [(4, 0), (7, 1), (6, 2), (5, 3)])
    scale, *tables = prepare_call(scal, kernel, upper)
    send = wave_call(scal, got, scale, lowest, tables)
    got = shared(send)
    tabs = ready_call(scal)
    move, odd_out, even_out = term_call(scal, got, there, withs, tabs)
    crossed = other_core(odd_out)
    move = shared(move.reshape(SLABS, ROWS, FLAT, LANES))
    by_two = even_out[0].astype(F32) + jnp.where(even_core, crossed[0], crossed[1]).astype(F32)
    by_four = even_out[1].astype(F32) + jnp.where(even_core, crossed[1], 0.0).astype(F32)
    four_back = passed_along(by_four.astype(BF16), 4)
    two_back = passed_along(by_two.astype(BF16), 2)
    return final_call(odd_core, move, crossed, two_back, four_back)[None]


def solution(mesh):
    return jax.shard_map(
        per_device,
        mesh=mesh,
        in_specs=(P("orb", "slab", None), P("orb", None), P("orb", None), P(None, "slab", None)),
        out_specs=P("orb", "slab", None),
        check_vma=False,
    )
```

```python
import jax
import jax.numpy as jnp
import numpy as np
from jax import lax
from jax.experimental import pallas as pl
from jax.experimental.pallas import tpu as pltpu
from jax.sharding import PartitionSpec as P


EDGE = 64
GRID = 128
HALF = 32
SLABS = 8
ROWS = EDGE // SLABS
WAVES = GRID // SLABS
PAIRS = 2
LANES = 128
CELLS = EDGE * EDGE
FLAT = CELLS // LANES
PAD = 24
SPAN = PAD + FLAT + PAD + 1
SLOTS = 8
TWIN = 2 * SLOTS
ZSPAN = EDGE + 1
BSPAN = SLOTS + 1
RSPAN = FLAT + 1
F32 = jnp.float32
BF16 = jnp.bfloat16


def full_tables():
    index = np.arange(GRID)
    angle = (index[:, None] * index[None, :] % GRID) * (2.0 * np.pi / GRID)
    rounded = lambda a: a.astype(np.float32).astype(BF16).astype(np.float32)
    return rounded(np.cos(angle)), rounded(np.sin(angle))


COS, SIN = full_tables()
SIGN = COS[:, EDGE]
OWN_WAVES = np.array([[WAVES * s + (s >= SLABS // 2) + q for q in range(SLOTS)] for s in range(SLABS)])


def forward_first():
    waves = OWN_WAVES.reshape(-1)
    im = -SIN[:, waves]
    im[:, 0] = SIGN
    return np.concatenate([COS[:, waves], im], axis=1)


def backward_last():
    c, s = COS.copy(), SIN.copy()
    s[:, 0] = -SIGN
    out = []
    for par in range(2):
        for table in (c, s):
            wide = np.zeros((GRID, SLABS, 2, SLOTS), np.float32)
            wide[:, :, par] = table[:, OWN_WAVES]
            out.append(wide.reshape(GRID, GRID))
    return np.concatenate(out)


def reversal():
    flip = np.zeros((GRID, GRID), np.float32)
    flip[np.arange(GRID), -np.arange(GRID) % GRID] = 1.0
    return flip.astype(BF16)


def dot(a, b):
    return jnp.dot(a, b, preferred_element_type=F32)


def swapped(x):
    return pltpu.roll(x, EDGE, axis=1)


def lanes_of(shape):
    return lax.broadcasted_iota(jnp.int32, shape, 1)


def low_half(shape):
    return lanes_of(shape) < EDGE


def shifted(ref, base, d1, d2):
    flat = d1 * EDGE + d2
    turn = flat & (LANES - 1)
    jump = (flat - turn) // LANES
    here = pltpu.roll(ref[pl.ds(base - jump, FLAT), :], turn, axis=1)
    before = pltpu.roll(ref[pl.ds(base - jump - 1, FLAT), :], turn, axis=1)
    lane = lanes_of((FLAT, LANES))
    depth = (lane & (EDGE - 1)) - d2
    return jnp.where((depth >= 0) & (depth < EDGE), jnp.where(lane >= turn, here, before), 0.0)


def reversed_plane(flip, plane):
    return dot(dot(flip, plane).astype(BF16), flip)


def clear_edges(ref, rows):
    zeros = jnp.zeros((PAD + 1, LANES), F32)
    for c in range(rows):
        ref[c * SPAN : c * SPAN + PAD, :] = zeros[:PAD]
        ref[c * SPAN + PAD + FLAT : (c + 1) * SPAN, :] = zeros


def load_kernel(corner_h, own, loaded, corner, sems):
    mark_load = pltpu.make_async_copy(corner_h, corner, sems.at[0])
    own_load = pltpu.make_async_copy(own, loaded.at[:, pl.ds(0, CELLS)], sems.at[1])
    mark_load.start()
    own_load.start()
    mark_load.wait()
    lane = lanes_of((ROWS, LANES))
    mark = jnp.zeros((ROWS, LANES), F32)
    for k in range(3):
        mark = jnp.where(lane == k, corner[0, k].astype(F32), mark)
    loaded[:, CELLS:] = mark.astype(BF16)
    own_load.wait()


def spread_kernel(loaded, copies, sems):
    sends = [pltpu.make_async_copy(loaded.at[:, pl.ds(0, CELLS)], copies.at[t], sems.at[t]) for t in range(SLABS)]
    for one in sends:
        one.start()
    for one in sends:
        one.wait()


def mirror_kernel(kern, upper, lowest):
    kern_flat = kern.reshape(GRID * WAVES, LANES)
    for q in range(SLOTS):
        upper[q] = kern_flat[pl.ds(SLOTS + q, GRID, stride=WAVES), :].astype(BF16)
    lowest[...] = kern_flat[pl.ds(0, GRID, stride=WAVES), :].astype(BF16)


def start_kernel(info, partners, corner, two, four, odd, own_in, first_t, send, there_out, with_out, scal, own_s, part_s):
    slab, orbit = info[0], info[1]
    clear_edges(own_s, 2 * ROWS)
    scal[0] = slab
    low_d = low_half((FLAT, LANES))
    low_w = low_half((EDGE, LANES))
    lane = lanes_of((ROWS, LANES))
    weight = jnp.where(lane == 0, 1.0, jnp.where(lane == 1, 64.0, jnp.where(lane == 2, 4096.0, 0.0)))
    for n in range(PAIRS):
        hop = (partners[0, n] - orbit) & (EDGE - 1)
        for k in range(FLAT + 1):
            at = slice(k * LANES, (k + 1) * LANES)
            low = jnp.where(hop == 1, odd[0, :, at].astype(F32), two[:, at].astype(F32))
            high = jnp.where(hop == 3, odd[1, :, at].astype(F32), four[:, at].astype(F32))
            value = jnp.where(hop <= 2, low, high)
            if k < FLAT:
                part_s[pl.ds(k, ROWS, stride=RSPAN), :] = value
            else:
                code = jnp.sum(value[:1] * weight[:1]).astype(jnp.int32)
        d0 = (code & 63) - corner[0, 0]
        d1 = ((code >> 6) & 63) - corner[0, 1]
        d2 = (code >> 12) - corner[0, 2]
        scal[1 + 3 * n] = d0
        scal[2 + 3 * n] = d1
        scal[3 + 3 * n] = d2
        scal[7 + n] = hop
        halves = [first_t[pl.ds(HALF + d1 + par, FLAT, stride=2), :] for par in range(2)]
        first = jnp.concatenate(halves, axis=0).T.astype(BF16)
        window = slab + (d0 >> 3)
        for w in range(2):
            t = jnp.clip(window + w, 0, SLABS - 1)
            for k in range(FLAT):
                piece = own_in[t, :, k * LANES : (k + 1) * LANES].astype(F32)
                own_s[pl.ds(w * ROWS * SPAN + PAD + k, ROWS, stride=SPAN), :] = piece
        for quad in range(ROWS // 4):
            sides = []
            for r in range(quad * 4, quad * 4 + 4):
                source = slab * ROWS + r + d0
                inside = jnp.logical_and(source >= 0, source < EDGE)
                base = (r + (d0 & (ROWS - 1))) * SPAN + PAD
                there = jnp.where(inside, shifted(own_s, base, -d1, -d2), 0.0)
                part = part_s[r * RSPAN : r * RSPAN + FLAT, :]
                there_out[n, r] = there.astype(BF16)
                with_out[n, r] = part.astype(BF16)
                sides.append(there * part)
            columns = []
            for half in range(2):
                a, b = sides[half * 2], sides[half * 2 + 1]
                even = jnp.where(low_d, a, swapped(b)).astype(BF16)
                odd_part = jnp.where(low_d, swapped(a), b).astype(BF16)
                columns.append(jnp.concatenate([even, odd_part], axis=0))
            y = dot(first, jnp.concatenate(columns, axis=1))
            for half in range(2):
                re = y[:EDGE, half * LANES : (half + 1) * LANES]
                im = y[EDGE:, half * LANES : (half + 1) * LANES]
                wave_a = jnp.where(low_w, re, swapped(im))
                wave_b = jnp.where(low_w, swapped(re), im)
                for s in range(SLABS):
                    at = slice(s * SLOTS, (s + 1) * SLOTS)
                    both = jnp.concatenate([wave_a[at], wave_b[at]], axis=0)
                    send[s, n, quad * 2 + half] = both.astype(BF16)


def prepare_kernel(scal, kern, upper, flip_t, cos_f, sin_f, scale_out, rowf_out, depf_out, rowb_out, depb_out):
    slab = scal[0]
    flip = flip_t[...]
    kern_flat = kern.reshape(GRID * WAVES, LANES)
    lower = slab < SLABS // 2
    for q in range(SLOTS):
        here = kern_flat[pl.ds(jnp.where(lower, q, q + 1), GRID, stride=WAVES), :]
        if q:
            there = upper[jnp.where(lower, SLOTS - q, SLOTS - 1 - q)]
            scale_out[q] = here + reversed_plane(flip, there)
        else:
            here = here.astype(BF16).astype(F32)
            scale_out[0] = here + jnp.where(lower, 0.0, reversed_plane(flip, upper[SLOTS - 1]))
            scale_out[SLOTS] = here + reversed_plane(flip, here.astype(BF16))
    half = low_half((GRID, LANES))

    def by_wave(shift):
        turn = (GRID - HALF - shift) & (LANES - 1)
        c = pltpu.roll(cos_f[...], turn, axis=1)
        s = pltpu.roll(sin_f[...], turn, axis=1)
        return jnp.where(half, c, swapped(s)).astype(BF16), jnp.where(half, -s, swapped(c)).astype(BF16)

    for n in range(PAIRS):
        d0, d2 = scal[1 + 3 * n], scal[3 + 3 * n]
        rowf_out[n, :GRID, :], rowf_out[n, GRID:, :] = by_wave(d0)
        depb_out[n, :GRID, :], depb_out[n, GRID:, :] = by_wave(d2)
        c, s = (ref[pl.ds(HALF + d0, EDGE), :].astype(BF16) for ref in (cos_f, sin_f))
        rowb_out[n] = jnp.concatenate(
            [jnp.concatenate([c, -s], axis=1), jnp.concatenate([s, c], axis=1)], axis=0
        )
        c, s = (ref[pl.ds(HALF + d2, EDGE), :].astype(BF16) for ref in (cos_f, sin_f))
        depf_out[n] = jnp.concatenate(
            [jnp.concatenate([c, -s], axis=1), jnp.concatenate([s, c], axis=1)], axis=0
        )


def wave_kernel(scal, got, scale_t, lowest, rowf_t, depf_t, rowb_t, depb_t, flip_t, send, zr, zi, back_s):
    slab = scal[0]
    first = slab == 0
    lower = slab < SLABS // 2
    flip = flip_t[...]
    low = lowest[...]
    low_back = reversed_plane(flip, low)
    both = scale_t[SLOTS]
    top = low.astype(F32) + low_back
    bottom = scale_t[0] + jnp.where(lower, low_back, 0.0)
    main = jnp.where(first, 0.25 * (both + top), bottom)
    extra = jnp.where(first, 0.25 * (both - top), 0.0)
    for n in range(PAIRS):
        at_z = n * SLOTS * ZSPAN
        at_b = n * EDGE * BSPAN
        depth_m = depf_t[n]
        rows_m = rowf_t[n]
        block = jnp.concatenate([got[t, n, p] for t in range(SLABS) for p in range(ROWS // 2)], axis=0)
        z = dot(block, depth_m)
        for c in range(EDGE):
            part = z[c * SLOTS : (c + 1) * SLOTS]
            zr[pl.ds(at_z + c, SLOTS, stride=ZSPAN), :] = part[:, :LANES]
            zi[pl.ds(at_z + c, SLOTS, stride=ZSPAN), :] = part[:, LANES:]

        def plane(w):
            at = slice(at_z + w * ZSPAN, at_z + w * ZSPAN + EDGE)
            return jnp.concatenate([zr[at, :], zi[at, :]], axis=0).astype(BF16)

        lefts = []
        for w0 in range(0, SLOTS, 2):
            x = dot(rows_m, jnp.concatenate([plane(w0), plane(w0 + 1)], axis=1))
            weight = jnp.concatenate([scale_t[w0] if w0 else main, scale_t[w0 + 1]], axis=1)
            re, im = x[:GRID] * weight, x[GRID:] * weight
            if w0 == 0:
                edge = x[:, :LANES].astype(BF16)
                turned = dot(flip, jnp.concatenate([edge[:GRID], edge[GRID:]], axis=1)).astype(BF16)
                turned = dot(jnp.concatenate([turned[:, :LANES], turned[:, LANES:]], axis=0), flip)
                back_re, back_im = turned[:GRID], turned[GRID:]
                re = jnp.concatenate([re[:, :LANES] + extra * back_re, re[:, LANES:]], axis=1)
                im = jnp.concatenate([im[:, :LANES] - extra * back_im, im[:, LANES:]], axis=1)
            v = dot(rowb_t[n], jnp.concatenate([re, im], axis=0).astype(BF16)).astype(BF16)
            re, im = v[:EDGE], v[EDGE:]
            lefts.append(jnp.concatenate([re[:, :LANES], im[:, :LANES]], axis=1))
            lefts.append(jnp.concatenate([re[:, LANES:], im[:, LANES:]], axis=1))
        r = dot(jnp.concatenate(lefts, axis=0), depb_t[n])
        for w in range(SLOTS):
            back_s[pl.ds(at_b + w, EDGE, stride=BSPAN), :] = r[w * EDGE : (w + 1) * EDGE]
        for t in range(SLABS):
            for p in range(ROWS // 2):
                at = at_b + (t * ROWS + 2 * p) * BSPAN
                both = jnp.concatenate([back_s[at : at + SLOTS, :], back_s[at + BSPAN : at + BSPAN + SLOTS, :]], axis=0)
                send[t, n, p] = both.astype(BF16)


def ready_kernel(scal, last_t, tab_out):
    for n in range(PAIRS):
        d1 = scal[2 + 3 * n]
        parts = [
            last_t[pl.ds((2 * row + f) * GRID + HALF + d1 + par, FLAT, stride=2), :]
            for row in range(2)
            for f in range(2)
            for par in range(2)
        ]
        tab_out[n] = jnp.concatenate(parts, axis=0).astype(BF16)


def term_kernel(scal, got, there, withs, tabs, move_h, odd_out, even_out, far_s, own_s, row_s, move_s, sem):
    slab = scal[0]
    low = low_half((FLAT, LANES))
    scale = 1.0 / GRID**3
    clear_edges(own_s, PAIRS * ROWS)
    blank = jnp.zeros((FLAT, LANES), BF16)
    for c in range(EDGE):
        move_s[HALF + c] = blank
    for n in range(PAIRS):
        d0, d1, d2 = scal[1 + 3 * n], scal[2 + 3 * n], scal[3 + 3 * n]
        tab = tabs[n]
        for p in range(ROWS // 2):
            g = dot(tab, jnp.concatenate([got[t, n, p] for t in range(SLABS)], axis=0))
            for par in range(2):
                r = p * 2 + par
                c0, c1, s0, s1 = (g[par * GRID + f * FLAT : par * GRID + (f + 1) * FLAT] for f in range(4))
                pot = jnp.where(low, c0 - swapped(s0), swapped(c1) - s1) * scale
                far_s[n, r] = pot * there[n, r].astype(F32)
                base = (n * ROWS + r) * SPAN + PAD
                own_s[base : base + FLAT, :] = pot * withs[n, r].astype(F32)
        for r in range(ROWS):
            base = (n * ROWS + r) * SPAN + PAD
            at = HALF + slab * ROWS + r + d0
            value = shifted(own_s, base, d1, d2)
            if n == 0:
                row_s[r] = value
            else:
                other = r + d0 - scal[1]
                meets = jnp.logical_and(other >= 0, other < ROWS)
                value = value + jnp.where(meets, row_s[jnp.clip(other, 0, ROWS - 1)], 0.0)
            move_s[at] = value.astype(BF16)
    copy = pltpu.make_async_copy(move_s.at[pl.ds(HALF, EDGE)], move_h, sem)
    copy.start()
    hops = [scal[7 + n] for n in range(PAIRS)]
    for e in range(1, 5):
        target = odd_out if e % 2 else even_out
        for row in range(ROWS):
            value = sum(jnp.where(hops[n] == e, far_s[n, row], 0.0) for n in range(PAIRS))
            target[(e - 1) // 2, row] = value.astype(BF16)
    copy.wait()


def final_kernel(odd_core, moved, crossed, two, four, out, total_s):
    keep = odd_core[0] == 1
    for r in range(ROWS):
        total = two[r].astype(F32) + four[r].astype(F32) + jnp.where(keep, crossed[0, r].astype(F32), 0.0)
        for t in range(SLABS):
            total = total + moved[t, r].astype(F32)
        total_s[r * RSPAN : r * RSPAN + FLAT, :] = total
    for k in range(FLAT):
        out[:, k * LANES : (k + 1) * LANES] = total_s[pl.ds(k, ROWS, stride=RSPAN), :]


VMEM = pl.BlockSpec(memory_space=pltpu.VMEM)
SMEM = pl.BlockSpec(memory_space=pltpu.SMEM)
HBM = pl.BlockSpec(memory_space=pltpu.HBM)


def kept(shape, dtype):
    return pltpu.VMEM(shape, dtype)


def far(shape, dtype):
    return pltpu.HBM(shape, dtype)


def away(x):
    return pltpu.with_memory_space_constraint(x, pltpu.HBM)


def near(x):
    return pltpu.with_memory_space_constraint(x, pltpu.VMEM)


def call(kernel, mib, in_specs, out_shape, out_specs, scratch, args):
    return pl.pallas_call(
        kernel,
        out_shape=out_shape,
        in_specs=in_specs,
        out_specs=out_specs,
        scratch_shapes=scratch,
        interpret=INTERPRET,
        compiler_params=pltpu.CompilerParams(vmem_limit_bytes=mib << 20),
    )(*args)


INTERPRET = False
ROWBOX = (PAIRS, ROWS, FLAT, LANES)
PACKET = (SLABS, PAIRS, ROWS // 2, TWIN, LANES)


def load_call(offsets, own):
    scratch = (pltpu.SMEM((1, 3), jnp.int32), pltpu.SemaphoreType.DMA((2,)))
    shape = kept((ROWS, CELLS + LANES), BF16)
    return call(load_kernel, 8, [HBM, HBM], shape, VMEM, scratch, (away(offsets), away(own)))


def spread_call(loaded):
    scratch = (pltpu.SemaphoreType.DMA((SLABS,)),)
    shape = far((SLABS, ROWS, CELLS), BF16)
    return call(spread_kernel, 8, [VMEM], shape, HBM, scratch, (near(loaded),))


def mirror_call(kernel):
    shapes = (kept((SLOTS, GRID, LANES), BF16), kept((GRID, LANES), BF16))
    return call(mirror_kernel, 8, [VMEM], shapes, (VMEM,) * 2, (), (kernel,))


def start_call(info, partners, offsets, two, four, odd, own_box):
    shapes = (kept(PACKET, BF16), kept(ROWBOX, BF16), kept(ROWBOX, BF16), jax.ShapeDtypeStruct((9,), jnp.int32))
    scratch = (pltpu.VMEM((2 * ROWS * SPAN, LANES), F32), pltpu.VMEM((ROWS * RSPAN, LANES), F32))
    args = (info, partners, offsets, near(two), near(four), near(odd), near(own_box), jnp.asarray(forward_first()))
    return call(start_kernel, 12, [SMEM] * 3 + [VMEM] * 5, shapes, (VMEM,) * 3 + (SMEM,), scratch, args)


def prepare_call(scal, kernel, upper):
    shapes = (
        kept((SLOTS + 1, GRID, LANES), F32),
        kept((PAIRS, 2 * GRID, LANES), BF16),
        kept((PAIRS, GRID, 2 * LANES), BF16),
        kept((PAIRS, GRID, 2 * LANES), BF16),
        kept((PAIRS, 2 * GRID, LANES), BF16),
    )
    args = (scal, kernel, near(upper), jnp.asarray(reversal()), jnp.asarray(COS), jnp.asarray(SIN))
    return call(prepare_kernel, 12, [SMEM] + [VMEM] * 5, shapes, (VMEM,) * 5, (), args)


def wave_call(scal, got, scale, lowest, tables):
    scratch = (
        pltpu.VMEM((PAIRS * SLOTS * ZSPAN, LANES), F32),
        pltpu.VMEM((PAIRS * SLOTS * ZSPAN, LANES), F32),
        pltpu.VMEM((PAIRS * EDGE * BSPAN, LANES), F32),
    )
    args = (scal, near(got), near(scale), near(lowest), *(near(t) for t in tables), jnp.asarray(reversal()))
    return call(wave_kernel, 12, [SMEM] + [VMEM] * 8, kept(PACKET, BF16), VMEM, scratch, args)


def ready_call(scal):
    args = (scal, jnp.asarray(backward_last()))
    return call(ready_kernel, 8, [SMEM, VMEM], kept((PAIRS, 2 * GRID, GRID), BF16), VMEM, (), args)


def term_call(scal, got, there, withs, tabs):
    half = (2, ROWS, FLAT, LANES)
    shapes = (far((EDGE, FLAT, LANES), BF16), kept(half, BF16), kept(half, BF16))
    scratch = (
        pltpu.VMEM(ROWBOX, F32),
        pltpu.VMEM((PAIRS * ROWS * SPAN, LANES), F32),
        pltpu.VMEM((ROWS, FLAT, LANES), F32),
        pltpu.VMEM((HALF + EDGE + HALF, FLAT, LANES), BF16),
        pltpu.SemaphoreType.DMA,
    )
    args = (scal, near(got), near(there), near(withs), near(tabs))
    return call(term_kernel, 16, [SMEM] + [VMEM] * 4, shapes, (HBM, VMEM, VMEM), scratch, args)


def final_call(odd_core, moved, crossed, two, four):
    scratch = (pltpu.VMEM((ROWS * RSPAN, LANES), F32),)
    shape = jax.ShapeDtypeStruct((ROWS, CELLS), F32)
    args = (odd_core, near(moved), near(crossed), near(two), near(four))
    return call(final_kernel, 8, [SMEM] + [VMEM] * 4, shape, VMEM, scratch, args)


def passed_along(block, distance):
    count = lax.axis_size("orb")
    return lax.ppermute(block, "orb", [((i - distance) % count, i) for i in range(count)])


def other_core(block):
    count = lax.axis_size("orb")
    return lax.ppermute(block, "orb", [(i ^ 1, i) for i in range(count)])


def shared(block):
    return lax.all_to_all(block, "slab", split_axis=0, concat_axis=0, tiled=True)


def per_device(orbitals, partners, offsets, kernel):
    orbit = lax.axis_index("orb").astype(jnp.int32)
    slab = lax.axis_index("slab").astype(jnp.int32)
    even_core = orbit % 2 == 0
    info = jnp.stack([slab, orbit])
    odd_core = (orbit % 2)[None]
    loaded = load_call(offsets, orbitals[0])
    four = passed_along(loaded, -4)
    two = passed_along(loaded, -2)
    copies = spread_call(loaded)
    own_box = shared(copies)
    upper, lowest = mirror_call(kernel)
    given = jnp.stack([jnp.where(even_core, two, loaded), jnp.where(even_core, four, two)])
    odd = other_core(given)
    upper = lax.ppermute(upper, "slab", [(s, SLABS - 1 - s) for s in range(SLABS)])
    send, there, withs, scal = start_call(info, partners, offsets, two, four, odd, own_box)
    got = shared(send)
    lowest = lax.ppermute(lowest, "slab", [(4, 0), (7, 1), (6, 2), (5, 3)])
    scale, *tables = prepare_call(scal, kernel, upper)
    send = wave_call(scal, got, scale, lowest, tables)
    got = shared(send)
    tabs = ready_call(scal)
    move, odd_out, even_out = term_call(scal, got, there, withs, tabs)
    crossed = other_core(odd_out)
    move = shared(move.reshape(SLABS, ROWS, FLAT, LANES))
    by_two = even_out[0].astype(F32) + jnp.where(even_core, crossed[0], crossed[1]).astype(F32)
    by_four = even_out[1].astype(F32) + jnp.where(even_core, crossed[1], 0.0).astype(F32)
    four_back = passed_along(by_four.astype(BF16), 4)
    two_back = passed_along(by_two.astype(BF16), 2)
    return final_call(odd_core, move, crossed, two_back, four_back)[None]


def solution(mesh):
    return jax.shard_map(
        per_device,
        mesh=mesh,
        in_specs=(P("orb", "slab", None), P("orb", None), P("orb", None), P(None, "slab", None)),
        out_specs=P("orb", "slab", None),
        check_vma=False,
    )
```
